32 devices in a mesh: dp: 16 (over z, y, x), tensor: 2 (over core).
Axes of the slice: x: 2, y: 2, z: 4, core: 2. Of those that a mesh axis runs over, the one named last changes fastest.
Arguments:
- tokens: bfloat16 [64, 196, 512], P('dp'), may hold values from -6 to 6
- region_ids: int32 [64, 196], P('dp'), may hold values from 0 to 3
- norm1_gain: float32 [512], replicated, may hold values from 0.1 to 1.9
- norm1_bias: float32 [512], replicated, may hold values from -3 to 3
- w_qkv: bfloat16 [512, 3, 512], P(None, None, 'tensor'), may hold values from -0.25 to 0.25
- qv_bias: float32 [2, 512], P(None, 'tensor'), may hold values from -3 to 3
- rel_table: float32 [169, 16], P(None, 'tensor'), may hold values from -4 to 304
- w_proj: bfloat16 [512, 512], P(None, 'tensor'), may hold values from -0.75 to 0.75
- b_proj: float32 [512], replicated, may hold values from -3 to 3
- norm2_gain: float32 [512], replicated, may hold values from 0.1 to 1.9
- norm2_bias: float32 [512], replicated, may hold values from -3 to 3
- w_fc1: bfloat16 [512, 2048], P(None, 'tensor'), may hold values from -0.25 to 0.25
- b_fc1: float32 [2048], P('tensor'), may hold values from -3 to 3
- w_fc2: bfloat16 [512, 2048], P(None, 'tensor'), may hold values from -0.125 to 0.125
- b_fc2: float32 [512], replicated, may hold values from -3 to 3
- cotangent: bfloat16 [64, 196, 512], P('dp'), may hold values from -6 to 6
Outputs:
- out: bfloat16 [64, 196, 512], P('dp')
- grad_tokens: float32 [64, 196, 512], P('dp')
- grad_norm1_gain: float32 [512], replicated
- grad_norm1_bias: float32 [512], replicated
- grad_w_qkv: float32 [512, 3, 512], P('dp', None, 'tensor')
- grad_qv_bias: float32 [2, 512], P(None, 'tensor')
- grad_rel_table: float32 [169, 16], P(None, 'tensor')
- grad_w_proj: float32 [512, 512], P('dp', 'tensor')
- grad_b_proj: float32 [512], replicated
- grad_norm2_gain: float32 [512], replicated
- grad_norm2_bias: float32 [512], replicated
- grad_w_fc1: float32 [512, 2048], P('dp', 'tensor')
- grad_b_fc1: float32 [2048], P('tensor')
- grad_w_fc2: float32 [512, 2048], P('dp', 'tensor')
- grad_b_fc2: float32 [512], replicated
The draws below stay inside these ranges and needn't reach their ends.
Inputs may be any that keep to these rules, and one draw needn't show every extreme that they name: `region_ids`: tokens of a window attend only to tokens with the same label.
All inputs are finite; a program needn't handle non-finite values.
Results may differ from the reference program's by a relative error of at most 0.012.
Values may be sent and summed in bfloat16 or wider, within the bound.
No kernel may reach another device: no remote copies, remote signals or barrier semaphores. Data moves between devices by JAX's collectives and lax.ppermute only.
A program may use at most 128 MiB of HBM per device.

```python
import jax
import jax.numpy as jnp
from jax import lax

C = 512
HEADS = 16
FF = 2048
HEAD_DIM = 32
SIDE = 14
WIN = 7
SHIFT = 3
IMG_DEV = 4
IMAGES = 64
TABLE = 169


def draw_rel_table(key, part):
    key_main = jax.random.fold_in(key, 11)
    return jnp.clip(jax.random.normal(key_main, (TABLE, HEADS), jnp.float32), -4.0, 4.0)


def with_ends(drawn, key, smallest, largest):
    index_at = [jax.random.randint(jax.random.fold_in(key, axis), (), 0, length) for axis, length in enumerate(drawn.shape)]
    main_axis = drawn.shape.index(max(drawn.shape))
    next_to = index_at[:main_axis] + [(index_at[main_axis] + 1) % drawn.shape[main_axis]] + index_at[main_axis + 1:]
    return drawn.at[tuple(index_at)].set(smallest).at[tuple(next_to)].set(largest)


def with_spikes(array, rng, source, target, shards_of, factor):
    def block_of(axis_at):
        return (jnp.arange(array.shape[axis_at]) // (array.shape[axis_at] // shards_of)).reshape((-1,) + (1,) * (array.ndim - 1 - axis_at))

    near = jax.random.permutation(rng, shards_of)[block_of(target)]
    second = (block_of(target) + shards_of // 2) % shards_of
    return jnp.where((block_of(source) == near) | (block_of(source) == second), factor * array, array)


def shard_levels(key, dims, pieces, least, high):
    loudness = 1.0
    for position, blocks in pieces:
        draws = jax.random.uniform(jax.random.fold_in(jax.random.fold_in(key, 6), position), (blocks,), jnp.float32, least / len(pieces), high / len(pieces))
        loudness = loudness * jnp.repeat(jnp.exp(draws), dims[position] // blocks).reshape((-1,) + (1,) * (len(dims) - 1 - position))
    return loudness


def bell_draw(key, extent, scale, limit, pieces=(), kind=jnp.bfloat16):
    values = scale * jax.random.normal(key, extent, jnp.float32)
    if pieces:
        values = values * shard_levels(key, extent, pieces, -0.22, 0.18)
    return jnp.clip(values, -limit, limit).astype(kind)


def noise_with(rng, extent, scale, reach, split, heavy, kind=jnp.bfloat16):
    drawn = scale * jax.random.normal(rng, extent, jnp.float32)
    if split:
        drawn = drawn * shard_levels(rng, extent, split, -0.22, 0.18)
    return jnp.clip(with_spikes(drawn, jax.random.fold_in(rng, 3), *heavy), -reach, reach).astype(kind)


def setup_inputs(seed: int = 0) -> dict:
    key_of = jax.random.split(jax.random.key(seed), 17)
    tokens = noise_with(key_of[0], (IMAGES, SIDE * SIDE, C), 1.0, 6.0, ((0, 16),), (0, 2, 16, 2.0))
    region_ids = with_ends(jax.random.randint(key_of[1], (IMAGES, SIDE * SIDE), 0, 4), jax.random.fold_in(key_of[1], 1), 0, 3).astype(jnp.int32)
    norm1_gain = jnp.clip(1.0 + 0.18 * jax.random.normal(key_of[2], (C,), jnp.float32), 0.1, 1.9)
    norm1_bias = bell_draw(key_of[3], (C,), 0.5, 3.0, (), jnp.float32)
    w_qkv = bell_draw(key_of[4], (C, 3, C), C ** -0.5, 0.25, ((2, 2),))
    qv_bias = bell_draw(key_of[5], (2, C), 0.5, 3.0, ((1, 2),), jnp.float32)
    rel_table = draw_rel_table(jax.random.fold_in(key_of[16], 71), 0)
    w_proj = bell_draw(key_of[7], (C, C), (C // 8) ** -0.5, 0.75, ((1, 2),))
    b_proj = bell_draw(key_of[8], (C,), 0.5, 3.0, (), jnp.float32)
    norm2_gain = jnp.clip(1.0 + 0.18 * jax.random.normal(key_of[9], (C,), jnp.float32), 0.1, 1.9)
    norm2_bias = bell_draw(key_of[10], (C,), 0.5, 3.0, (), jnp.float32)
    w_fc1 = bell_draw(key_of[11], (C, FF), C ** -0.5, 0.25, ((1, 2),))
    b_fc1 = bell_draw(key_of[12], (FF,), 0.5, 3.0, ((0, 2),), jnp.float32)
    w_fc2 = bell_draw(key_of[13], (C, FF), FF ** -0.5, 0.125, ((1, 2),))
    b_fc2 = bell_draw(key_of[14], (C,), 0.5, 3.0, (), jnp.float32)
    cotangent = noise_with(key_of[15], (IMAGES, SIDE * SIDE, C), 1.0, 6.0, ((0, 16),), (0, 2, 16, 2.0))
    return dict(tokens=tokens, region_ids=region_ids, norm1_gain=norm1_gain, norm1_bias=norm1_bias, w_qkv=w_qkv, qv_bias=qv_bias, rel_table=rel_table, w_proj=w_proj, b_proj=b_proj, norm2_gain=norm2_gain, norm2_bias=norm2_bias, w_fc1=w_fc1, b_fc1=b_fc1, w_fc2=w_fc2, b_fc2=b_fc2, cotangent=cotangent)


NORM_EPS = 1e-05

def layer_norm(source, gain_vec, bias_vec):
    center = lax.optimization_barrier(jnp.mean(source, axis=-1, keepdims=True))
    centred = source - center
    inverse = lax.rsqrt(lax.optimization_barrier(jnp.mean(centred * centred, axis=-1, keepdims=True)) + NORM_EPS)
    normed = centred * inverse
    return (normed * gain_vec + bias_vec, normed, inverse)

def norm_back(upstream, normed, inverse, gain_vec):
    scaled = upstream * gain_vec
    return inverse * (scaled - lax.optimization_barrier(jnp.mean(scaled, axis=-1, keepdims=True)) - normed * lax.optimization_barrier(jnp.mean(scaled * normed, axis=-1, keepdims=True)))

def to_windows(source):
    images = source.shape[0]
    feature = source.shape[-1]
    blocks = SIDE // WIN
    spread = jnp.roll(source.reshape(images, SIDE, SIDE, feature), (-SHIFT, -SHIFT), axis=(1, 2))
    spread = spread.reshape(images, blocks, WIN, blocks, WIN, feature).transpose(0, 1, 3, 2, 4, 5)
    return spread.reshape(images * blocks * blocks, WIN * WIN, feature)

def from_windows(source, images):
    feature = source.shape[-1]
    blocks = SIDE // WIN
    spread = source.reshape(images, blocks, blocks, WIN, WIN, feature).transpose(0, 1, 3, 2, 4, 5)
    spread = jnp.roll(spread.reshape(images, SIDE, SIDE, feature), (SHIFT, SHIFT), axis=(1, 2))
    return spread.reshape(images, SIDE * SIDE, feature)

def gelu_slope(pre_act):
    return 0.5 * (1.0 + lax.erf(pre_act * 0.7071067811865476)) + pre_act * jnp.exp(-0.5 * pre_act * pre_act) * 0.3989422804014327

def relative_index():
    positions = jnp.arange(WIN * WIN, dtype=jnp.int32)
    row_at = positions // WIN
    col_at = positions % WIN
    return ((row_at[:, None] - row_at[None, :] + WIN - 1) * (2 * WIN - 1) + col_at[:, None] - col_at[None, :] + WIN - 1).astype(jnp.int32)

def split_heads(source):
    return source.reshape(source.shape[0], source.shape[1], -1, HEAD_DIM)

def block_pass(params, tokens_blk, cot_blk, ids_blk):
    norm1_gain, norm1_bias, w_qkv, qv_bias, rel_table, w_proj, b_proj, norm2_gain, norm2_bias, w_fc1, b_fc1, w_fc2, b_fc2 = params
    images = tokens_blk.shape[0]
    tok_rows = images * SIDE * SIDE
    factor = HEAD_DIM ** (-0.5)
    inputs = tokens_blk.reshape(tok_rows, C).astype(jnp.float32)
    norm_one, normed_one, inv_one = layer_norm(inputs, norm1_gain, norm1_bias)
    win_in = to_windows(norm_one.astype(jnp.bfloat16).reshape(images, SIDE * SIDE, C))
    win_ids = to_windows(ids_blk[..., None])[..., 0]
    allowed = (win_ids[:, :, None] == win_ids[:, None, :])[:, None]
    rel_bias = rel_table[relative_index()].transpose(2, 0, 1)
    projected = jnp.einsum('wtc,cjd->wtjd', win_in.astype(jnp.float32), w_qkv.astype(jnp.float32))
    q_heads = split_heads(((projected[:, :, 0] + qv_bias[0]) * factor).astype(jnp.bfloat16))
    k_heads = split_heads(projected[:, :, 1].astype(jnp.bfloat16))
    v_heads = split_heads((projected[:, :, 2] + qv_bias[1]).astype(jnp.bfloat16))
    raw = jnp.einsum('wqhd,wkhd->whqk', q_heads.astype(jnp.float32), k_heads.astype(jnp.float32)) + rel_bias[None]
    scores = jnp.where(allowed, raw, -jnp.inf)
    top_score = lax.optimization_barrier(jnp.max(scores, axis=-1, keepdims=True))
    log_total = top_score + jnp.log(lax.optimization_barrier(jnp.sum(jnp.exp(scores - top_score), axis=-1, keepdims=True)))
    probs = jnp.exp(scores - log_total)
    probs_b = probs.astype(jnp.bfloat16)
    attended = jnp.einsum('whqk,wkhd->wqhd', probs_b.astype(jnp.float32), v_heads.astype(jnp.float32)).astype(jnp.bfloat16)
    merged = from_windows(attended.reshape(attended.shape[0], WIN * WIN, C), images).reshape(tok_rows, C)
    resid_one = inputs + jnp.dot(merged, w_proj.T, preferred_element_type=jnp.float32) + b_proj
    norm_two, normed_two, inv_two = layer_norm(resid_one, norm2_gain, norm2_bias)
    norm_two_b = norm_two.astype(jnp.bfloat16)
    pre_act = jnp.dot(norm_two_b, w_fc1, preferred_element_type=jnp.float32) + b_fc1
    activated = jax.nn.gelu(pre_act, approximate=False).astype(jnp.bfloat16)
    output = (resid_one + jnp.dot(activated, w_fc2.T, preferred_element_type=jnp.float32) + b_fc2).astype(jnp.bfloat16)
    grad_out = cot_blk.reshape(tok_rows, C)
    grad_out_f = grad_out.astype(jnp.float32)
    g_b_fc2 = lax.optimization_barrier(jnp.sum(grad_out_f, axis=0))
    g_w_fc2 = jnp.dot(grad_out.T, activated, preferred_element_type=jnp.float32)
    grad_pre = jnp.dot(grad_out, w_fc2, preferred_element_type=jnp.float32) * gelu_slope(pre_act)
    g_b_fc1 = lax.optimization_barrier(jnp.sum(grad_pre, axis=0))
    grad_pre_b = grad_pre.astype(jnp.bfloat16)
    g_w_fc1 = jnp.dot(norm_two_b.T, grad_pre_b, preferred_element_type=jnp.float32)
    grad_norm_two = jnp.dot(grad_pre_b, w_fc1.T, preferred_element_type=jnp.float32)
    g_gain_two = lax.optimization_barrier(jnp.sum(grad_norm_two * normed_two, axis=0))
    g_bias_two = lax.optimization_barrier(jnp.sum(grad_norm_two, axis=0))
    grad_resid = grad_out_f + norm_back(grad_norm_two, normed_two, inv_two, norm2_gain)
    g_b_proj = lax.optimization_barrier(jnp.sum(grad_resid, axis=0))
    grad_resid_b = grad_resid.astype(jnp.bfloat16)
    g_w_proj = jnp.dot(grad_resid_b.T, merged, preferred_element_type=jnp.float32)
    grad_merged = jnp.dot(grad_resid_b, w_proj, preferred_element_type=jnp.float32).astype(jnp.bfloat16)
    grad_att = split_heads(to_windows(grad_merged.reshape(images, SIDE * SIDE, C)))
    g_v = jnp.einsum('whqk,wqhd->wkhd', probs_b.astype(jnp.float32), grad_att.astype(jnp.float32))
    g_probs = jnp.einsum('wqhd,wkhd->whqk', grad_att.astype(jnp.float32), v_heads.astype(jnp.float32))
    g_scores = probs * (g_probs - lax.optimization_barrier(jnp.sum(probs * g_probs, axis=-1, keepdims=True)))
    head_count = rel_table.shape[1]
    g_table = jax.ops.segment_sum(lax.optimization_barrier(jnp.sum(g_scores, axis=0)).transpose(1, 2, 0).reshape(-1, head_count), relative_index().reshape(-1), num_segments=TABLE)
    g_scores_b = g_scores.astype(jnp.bfloat16)
    g_q = jnp.einsum('whqk,wkhd->wqhd', g_scores_b.astype(jnp.float32), k_heads.astype(jnp.float32)) * factor
    g_k = jnp.einsum('whqk,wqhd->wkhd', g_scores_b.astype(jnp.float32), q_heads.astype(jnp.float32))
    n_windows = g_q.shape[0]
    g_qv_bias = jnp.stack([lax.optimization_barrier(jnp.sum(g_q, axis=(0, 1))).reshape(C), lax.optimization_barrier(jnp.sum(g_v, axis=(0, 1))).reshape(C)])
    g_qkv_b = jnp.stack([g_q, g_k, g_v], axis=2).reshape(n_windows, WIN * WIN, 3, C).astype(jnp.bfloat16)
    g_w_qkv = jnp.einsum('wtc,wtjd->cjd', win_in.astype(jnp.float32), g_qkv_b.astype(jnp.float32))
    grad_norm_one = from_windows(jnp.einsum('wtjd,cjd->wtc', g_qkv_b.astype(jnp.float32), w_qkv.astype(jnp.float32)), images).reshape(tok_rows, C)
    g_gain_one = lax.optimization_barrier(jnp.sum(grad_norm_one * normed_one, axis=0))
    g_bias_one = lax.optimization_barrier(jnp.sum(grad_norm_one, axis=0))
    grad_in = grad_resid + norm_back(grad_norm_one, normed_one, inv_one, norm1_gain)
    grads = (g_gain_one, g_bias_one, g_w_qkv, g_qv_bias, g_table, g_w_proj, g_b_proj, g_gain_two, g_bias_two, g_w_fc1, g_b_fc1, g_w_fc2, g_b_fc2)
    return ((output.reshape(images, SIDE * SIDE, C), grad_in.reshape(images, SIDE * SIDE, C)), grads)

def reference(tokens, region_ids, norm1_gain, norm1_bias, w_qkv, qv_bias, rel_table, w_proj, b_proj, norm2_gain, norm2_bias, w_fc1, b_fc1, w_fc2, b_fc2, cotangent):
    params = (norm1_gain, norm1_bias, w_qkv, qv_bias, rel_table, w_proj, b_proj, norm2_gain, norm2_bias, w_fc1, b_fc1, w_fc2, b_fc2)
    block_count = IMAGES // IMG_DEV
    start = (jnp.zeros((C,), jnp.float32), jnp.zeros((C,), jnp.float32), jnp.zeros((C, 3, C), jnp.float32), jnp.zeros((2, C), jnp.float32), jnp.zeros((TABLE, HEADS), jnp.float32), jnp.zeros((C, C), jnp.float32), jnp.zeros((C,), jnp.float32), jnp.zeros((C,), jnp.float32), jnp.zeros((C,), jnp.float32), jnp.zeros((C, FF), jnp.float32), jnp.zeros((FF,), jnp.float32), jnp.zeros((C, FF), jnp.float32), jnp.zeros((C,), jnp.float32))

    def advance(carry, items):
        tokens_blk, cot_blk, ids_blk = items
        results, grads = block_pass(params, tokens_blk, cot_blk, ids_blk)
        return (jax.tree.map(lambda total, extra: total + extra, carry, grads), results)
    sums, stacked = lax.scan(advance, start, (tokens.reshape(block_count, IMG_DEV, SIDE * SIDE, C), cotangent.reshape(block_count, IMG_DEV, SIDE * SIDE, C), region_ids.reshape(block_count, IMG_DEV, SIDE * SIDE)))
    output = stacked[0].reshape(IMAGES, SIDE * SIDE, C)
    grad_in = stacked[1].reshape(IMAGES, SIDE * SIDE, C)
    return (output, grad_in, sums[0], sums[1], sums[2], sums[3], sums[4], sums[5], sums[6], sums[7], sums[8], sums[9], sums[10], sums[11], sums[12])
```

```python
import functools

import jax
import jax.numpy as jnp
from jax import lax
from jax.experimental import pallas as pl
from jax.experimental.pallas import tpu as pltpu
from jax.sharding import PartitionSpec as P

HEAD_DIM = 32
SIDE = 14
WIN = 7
SHIFT = 3
NORM_EPS = 1e-05

TOK = SIDE * SIDE
TPAD = 208
WTOK = WIN * WIN
WPAD = 64
BLOCKS = SIDE // WIN
WINS = BLOCKS * BLOCKS
F32 = jnp.float32
BF16 = jnp.bfloat16


def nn(a, b):
    return lax.dot_general(a, b, (((1,), (0,)), ((), ())), preferred_element_type=F32)


def nt(a, b):
    return lax.dot_general(a, b, (((1,), (1,)), ((), ())), preferred_element_type=F32)


def tn(a, b):
    return lax.dot_general(a, b, (((0,), (0,)), ((), ())), preferred_element_type=F32)


def iota(shape, axis):
    return lax.broadcasted_iota(jnp.int32, shape, axis)


def normalize(source):
    center = jnp.mean(source, axis=-1, keepdims=True)
    centred = source - center
    inverse = lax.rsqrt(jnp.mean(centred * centred, axis=-1, keepdims=True) + NORM_EPS)
    return centred * inverse, inverse


def norm_back(upstream, normed, inverse, gain_vec):
    scaled = upstream * gain_vec
    return inverse * (
        scaled
        - jnp.mean(scaled, axis=-1, keepdims=True)
        - normed * jnp.mean(scaled * normed, axis=-1, keepdims=True)
    )


def seventh(value):
    return (value * 37) >> 8


def window_source(slot):
    window, at = slot >> 6, slot & (WPAD - 1)
    row = (window >> 1) * WIN + seventh(at) + SHIFT
    col = (window & 1) * WIN + (at - seventh(at) * WIN) + SHIFT
    row = jnp.where(row >= SIDE, row - SIDE, row)
    col = jnp.where(col >= SIDE, col - SIDE, col)
    return jnp.where(at < WTOK, row * SIDE + col, -1)


def gather_matrix():
    shape = (WINS * WPAD, TPAD)
    hit = window_source(iota(shape, 0)) == iota(shape, 1)
    return jnp.where(hit, 1.0, 0.0).astype(BF16)


def scatter_matrix():
    shape = (TPAD, WINS * WPAD)
    hit = window_source(iota(shape, 1)) == iota(shape, 0)
    return jnp.where(hit, 1.0, 0.0).astype(BF16)


def head_mask(heads):
    shape = (heads * WPAD, 2 * heads * HEAD_DIM)
    hit = (iota(shape, 0) >> 6) == ((iota(shape, 1) & (heads * HEAD_DIM - 1)) >> 5)
    return jnp.where(hit, 1.0, 0.0).astype(BF16)


def load_images(block_ref, images, kind):
    pieces = []
    for image in range(images):
        pieces.append(block_ref[image].astype(kind))
        pieces.append(jnp.zeros((TPAD - TOK, block_ref.shape[2]), kind))
    return pieces


def fill_rows(rows_ref, block_ref, images):
    rows_ref[...] = jnp.zeros(rows_ref.shape, rows_ref.dtype)
    for image in range(images):
        rows_ref[image * TPAD : image * TPAD + TOK, :] = block_ref[image].astype(rows_ref.dtype)


def window_mask(ids_row, pick):
    ids_b = jnp.broadcast_to(ids_row.astype(F32), (2 * WPAD, TPAD)).astype(BF16)
    keys = nt(pick, ids_b)
    queries = nt(ids_b[:16], jnp.concatenate([pick, pick], axis=0))[0:1]
    shape = (WPAD, 2 * WPAD)
    key_at = iota(shape, 0)
    query_at = iota(shape, 1) & (WPAD - 1)
    same = jnp.logical_or(keys == queries, query_at >= WTOK)
    return jnp.where(jnp.logical_and(same, key_at < WTOK), 0.0, -jnp.inf)


def two_groups(rows):
    half = rows.shape[1] // 2
    zero = jnp.zeros((rows.shape[0], half), rows.dtype)
    return jnp.concatenate(
        [
            jnp.concatenate([rows[:, :half], zero], axis=1),
            jnp.concatenate([zero, rows[:, half:]], axis=1),
        ],
        axis=0,
    )


def own_groups(rows):
    half = rows.shape[1] // 2
    return jnp.concatenate([rows[:WPAD, :half], rows[WPAD:, half:]], axis=1)


def per_head(rows, mask, heads):
    return jnp.concatenate([rows] * heads, axis=0) * mask


def table_offsets(rows_half):
    shape = (2 * rows_half, 2 * WPAD)
    entry, query = iota(shape, 0), iota(shape, 1)
    group_e = jnp.where(entry >= rows_half, 1, 0)
    at = query & (WPAD - 1)
    place = seventh(at) * (2 * WIN - 1) + (at - seventh(at) * WIN)
    fits = jnp.logical_and(group_e == (query >> 6), at < WTOK)
    return jnp.where(fits, entry - group_e * rows_half - place, 4096)


def key_offset(key):
    row = key // WIN
    return 2 * WIN * (WIN - 1) - (row * (2 * WIN - 1) + key - row * WIN)


def bias_kernel(heads, rows_half, table_ref, bias_ref, off_ref):
    off_ref[...] = table_offsets(rows_half)
    bias_ref[...] = jnp.zeros(bias_ref.shape, F32)
    parts = table_ref[...]
    for key in range(WTOK):
        pick = jnp.where(off_ref[...] == key_offset(key), 1.0, 0.0).astype(BF16)
        rows = nn(parts, pick)
        bias_ref[pl.ds(key, heads, stride=WPAD), :] = (
            rows[:heads] + rows[heads : 2 * heads] + rows[2 * heads :]
        )


def attend_kernel(
    images,
    heads,
    me_ref,
    tok_ref,
    ids_ref,
    gain_ref,
    shift_ref,
    wm_ref,
    wo_ref,
    qvb_ref,
    bias_ref,
    pm_ref,
    po_ref,
    bproj_ref,
    q_ref,
    k_ref,
    v_ref,
    win_ref,
    lse_ref,
    merged_ref,
    resid_ref,
    x_ref,
    pick_ref,
    att_ref,
    mask_ref,
):
    chan = heads * HEAD_DIM
    factor = HEAD_DIM ** (-0.5)
    fill_rows(x_ref, tok_ref, images)
    normed, _ = normalize(x_ref[...])
    ln_one = (normed * gain_ref[...] + shift_ref[...]).astype(BF16)
    pick_ref[...] = gather_matrix()
    mask_ref[...] = head_mask(heads)
    slots = WINS * WPAD
    for image in range(images):
        win_ref[image * slots : (image + 1) * slots, :] = nn(
            pick_ref[...], ln_one[image * TPAD : (image + 1) * TPAD]
        ).astype(BF16)
    for group, w_ref in enumerate((wm_ref, wo_ref)):
        cols = slice(group * chan, (group + 1) * chan)
        win = win_ref[...]
        q_ref[:, cols] = (
            (nn(win, w_ref[:, :chan]) + qvb_ref[0:1, cols]) * factor
        ).astype(BF16)
        k_ref[:, cols] = nn(win, w_ref[:, chan : 2 * chan]).astype(BF16)
        v_ref[:, cols] = (nn(win, w_ref[:, 2 * chan :]) + qvb_ref[1:2, cols]).astype(BF16)

    def one_window(window, carry):
        rows = pl.ds(pl.multiple_of(window * WPAD, WPAD), WPAD)
        image = window // WINS
        local = pl.multiple_of((window - image * WINS) * WPAD, WPAD)
        ids_row = ids_ref[pl.ds(me_ref[0] * images + image, 1), :]
        allowed = window_mask(ids_row, pick_ref[pl.ds(local, WPAD), :])
        k_all = per_head(k_ref[rows, :], mask_ref[...], heads)
        v_all = per_head(v_ref[rows, :], mask_ref[...], heads)
        scores = nt(k_all, two_groups(q_ref[rows, :])) + bias_ref[...]
        scores = scores.reshape(heads, WPAD, 2 * WPAD) + allowed[None]
        top = jnp.max(scores, axis=1, keepdims=True)
        grown = jnp.exp(scores - top)
        total = jnp.sum(grown, axis=1, keepdims=True)
        lse_ref[window] = (top + jnp.log(total)).reshape(heads, 2 * WPAD)
        probs = (grown * (1.0 / total)).astype(BF16).reshape(heads * WPAD, 2 * WPAD)
        att_ref[rows, :] = own_groups(tn(probs, v_all)).astype(BF16)
        return carry

    lax.fori_loop(0, images * WINS, one_window, 0)
    back = scatter_matrix()
    for image in range(images):
        merged_ref[image * TPAD : (image + 1) * TPAD, :] = nn(
            back, att_ref[image * slots : (image + 1) * slots, :]
        ).astype(BF16)
    resid_ref[...] = (
        x_ref[...]
        + (nt(merged_ref[:, :chan], pm_ref[...]) + nt(merged_ref[:, chan:], po_ref[...]))
        + bproj_ref[...]
    )


def ffn_kernel(
    images,
    me_ref,
    resid_ref,
    cot_ref,
    gain_ref,
    shift_ref,
    b2_ref,
    w1m_ref,
    w1o_ref,
    w2m_ref,
    w2o_ref,
    b1m_ref,
    b1o_ref,
    g1m_ref,
    g1o_ref,
    g2m_ref,
    g2o_ref,
    gbm_ref,
    gbo_ref,
    out_ref,
    half_ref,
    gres_ref,
    sums_ref,
    ln_ref,
    lnt_ref,
    cot_b_ref,
    cot_t_ref,
    ffn_ref,
    gln_ref,
):
    step = pl.program_id(0)

    @pl.when(step == 0)
    def _():
        normed, _ = normalize(resid_ref[...])
        ln_two = normed * gain_ref[...] + shift_ref[...]
        ln_ref[...] = ln_two.astype(BF16)
        lnt_ref[...] = ln_two.T.astype(BF16)
        fill_rows(cot_b_ref, cot_ref, images)
        cot_t_ref[...] = cot_b_ref[...].astype(F32).T.astype(BF16)
        ffn_ref[...] = jnp.zeros(ffn_ref.shape, F32)
        gln_ref[...] = jnp.zeros(gln_ref.shape, F32)

    for w1_ref, w2_ref, b1_ref, g1_ref, g2_ref, gb_ref in (
        (w1m_ref, w2m_ref, b1m_ref, g1m_ref, g2m_ref, gbm_ref),
        (w1o_ref, w2o_ref, b1o_ref, g1o_ref, g2o_ref, gbo_ref),
    ):
        pre = nn(ln_ref[...], w1_ref[...]) + b1_ref[...]
        phi = 0.5 * (1.0 + lax.erf(pre * 0.7071067811865476))
        act = (pre * phi).astype(BF16)
        slope = phi + pre * jnp.exp(-0.5 * pre * pre) * 0.3989422804014327
        grad_pre = nn(cot_b_ref[...], w2_ref[...]) * slope
        gb_ref[...] = jnp.sum(grad_pre, axis=0, keepdims=True)
        grad_pre = grad_pre.astype(BF16)
        ffn_ref[...] += nt(act, w2_ref[...])
        gln_ref[...] += nt(grad_pre, w1_ref[...])
        g2_ref[...] = nn(cot_t_ref[...], act).astype(BF16)
        g1_ref[...] = nn(lnt_ref[...], grad_pre).astype(BF16)

    @pl.when(step == pl.num_programs(0) - 1)
    def _():
        resid = resid_ref[...]
        result = (resid + ffn_ref[...] + b2_ref[...]).astype(BF16)
        for image in range(images):
            piece = result[image * TPAD : image * TPAD + TOK]
            out_ref[image] = piece
            half_ref[image] = piece
        normed, inverse = normalize(resid)
        upstream = gln_ref[...]
        cot = cot_b_ref[...].astype(F32)
        grad_resid = cot + norm_back(upstream, normed, inverse, gain_ref[...])
        gres_ref[...] = grad_resid
        sums_ref[0:1, :] = jnp.sum(grad_resid, axis=0, keepdims=True)
        sums_ref[1:2, :] = jnp.sum(upstream * normed, axis=0, keepdims=True)
        sums_ref[2:3, :] = jnp.sum(upstream, axis=0, keepdims=True)
        sums_ref[3:4, :] = jnp.sum(cot, axis=0, keepdims=True)
        sums_ref[4:8, :] = jnp.zeros((4, sums_ref.shape[1]), F32)


def attend_back_kernel(
    images,
    heads,
    me_ref,
    gres_ref,
    ids_ref,
    merged_ref,
    pm_ref,
    po_ref,
    q_ref,
    k_ref,
    v_ref,
    win_ref,
    lse_ref,
    bias_ref,
    gwm_ref,
    gwo_ref,
    gpm_ref,
    gpo_ref,
    gqkv_ref,
    sums_ref,
    gbias_ref,
    pick_ref,
    gatt_ref,
    mask_ref,
    qsum_ref,
    vsum_ref,
):
    chan = heads * HEAD_DIM
    wide = 2 * chan
    factor = HEAD_DIM ** (-0.5)
    slots = WINS * WPAD
    pick_ref[...] = gather_matrix()
    mask_ref[...] = head_mask(heads)
    gres = gres_ref[...]
    gres_b = gres.astype(BF16)
    gres_t = gres.T.astype(BF16)
    gpm_ref[...] = nn(gres_t, merged_ref[:, :chan]).astype(BF16)
    gpo_ref[...] = nn(gres_t, merged_ref[:, chan:]).astype(BF16)
    grad_m = jnp.concatenate(
        [nn(gres_b, pm_ref[...]).astype(BF16), nn(gres_b, po_ref[...]).astype(BF16)], axis=1
    )
    for image in range(images):
        gatt_ref[image * slots : (image + 1) * slots, :] = nn(
            pick_ref[...], grad_m[image * TPAD : (image + 1) * TPAD]
        ).astype(BF16)
    gbias_ref[...] = jnp.zeros(gbias_ref.shape, F32)
    qsum_ref[...] = jnp.zeros(qsum_ref.shape, F32)
    vsum_ref[...] = jnp.zeros(vsum_ref.shape, F32)

    def one_window(window, carry):
        rows = pl.ds(pl.multiple_of(window * WPAD, WPAD), WPAD)
        image = window // WINS
        local = pl.multiple_of((window - image * WINS) * WPAD, WPAD)
        ids_row = ids_ref[pl.ds(me_ref[0] * images + image, 1), :]
        allowed = window_mask(ids_row, pick_ref[pl.ds(local, WPAD), :])
        mask = mask_ref[...]
        k_all = per_head(k_ref[rows, :], mask, heads)
        v_all = per_head(v_ref[rows, :], mask, heads)
        q_two = two_groups(q_ref[rows, :])
        g_two = two_groups(gatt_ref[rows, :])
        scores = nt(k_all, q_two) + bias_ref[...]
        scores = scores.reshape(heads, WPAD, 2 * WPAD) + allowed[None]
        probs = jnp.exp(scores - lse_ref[window].reshape(heads, 1, 2 * WPAD))
        g_probs = nt(v_all, g_two).reshape(heads, WPAD, 2 * WPAD)
        inner = jnp.sum(probs * g_probs, axis=1, keepdims=True)
        g_scores = (probs * (g_probs - inner)).reshape(heads * WPAD, 2 * WPAD)
        gbias_ref[...] += g_scores
        probs_b = probs.astype(BF16).reshape(heads * WPAD, 2 * WPAD)
        g_scores = g_scores.astype(BF16)

        def fold(product):
            return jnp.sum((product * mask.astype(F32)).reshape(heads, WPAD, wide), axis=0)

        g_v = fold(nn(probs_b, g_two))
        g_k = fold(nn(g_scores, q_two))
        g_q = own_groups(tn(g_scores, k_all)) * factor
        qsum_ref[...] += g_q
        vsum_ref[...] += g_v
        for group in range(2):
            cols = slice(group * chan, (group + 1) * chan)
            base = group * 3 * chan
            gqkv_ref[rows, base : base + chan] = g_q[:, cols].astype(BF16)
            gqkv_ref[rows, base + chan : base + 2 * chan] = g_k[:, cols].astype(BF16)
            gqkv_ref[rows, base + 2 * chan : base + 3 * chan] = g_v[:, cols].astype(BF16)
        return carry

    lax.fori_loop(0, images * WINS, one_window, 0)
    sums_ref[...] = jnp.zeros(sums_ref.shape, F32)
    sums_ref[0:1, :] = jnp.sum(qsum_ref[...], axis=0, keepdims=True)
    sums_ref[1:2, :] = jnp.sum(vsum_ref[...], axis=0, keepdims=True)
    win_t = win_ref[...].astype(F32).T.astype(BF16)
    gwm_ref[...] = nn(win_t, gqkv_ref[:, : 3 * chan]).astype(BF16)
    gwo_ref[...] = nn(win_t, gqkv_ref[:, 3 * chan :]).astype(BF16)


def last_kernel(
    images,
    heads,
    rows_half,
    me_ref,
    tok_ref,
    gres_ref,
    gqkv_ref,
    wm_ref,
    wo_ref,
    gain_ref,
    gbias_ref,
    full_ref,
    half_ref,
    sums_ref,
    table_ref,
    x_ref,
    off_ref,
    acc_ref,
):
    chan = heads * HEAD_DIM
    slots = WINS * WPAD
    grad_win = nt(gqkv_ref[:, : 3 * chan], wm_ref[...]) + nt(gqkv_ref[:, 3 * chan :], wo_ref[...])
    high = grad_win.astype(BF16)
    low = (grad_win - high.astype(F32)).astype(BF16)
    back = scatter_matrix()
    upstream = jnp.concatenate(
        [
            nn(back, high[image * slots : (image + 1) * slots])
            + nn(back, low[image * slots : (image + 1) * slots])
            for image in range(images)
        ],
        axis=0,
    )
    fill_rows(x_ref, tok_ref, images)
    normed, inverse = normalize(x_ref[...])
    grad_in = gres_ref[...] + norm_back(upstream, normed, inverse, gain_ref[...])
    for image in range(images):
        piece = grad_in[image * TPAD : image * TPAD + TOK]
        full_ref[image] = piece
        half_ref[image] = piece
    sums_ref[...] = jnp.zeros(sums_ref.shape, F32)
    sums_ref[0:1, :] = jnp.sum(upstream * normed, axis=0, keepdims=True)
    sums_ref[1:2, :] = jnp.sum(upstream, axis=0, keepdims=True)
    off_ref[...] = table_offsets(rows_half)
    acc_ref[...] = jnp.zeros(acc_ref.shape, F32)
    for key in range(WTOK):
        pick = jnp.where(off_ref[...] == key_offset(key), 1.0, 0.0).astype(BF16)
        rows = gbias_ref[pl.ds(key, heads, stride=WPAD), :]
        top = rows.astype(BF16).astype(F32)
        parts = jnp.concatenate([top, rows - top], axis=0).astype(BF16)
        acc_ref[...] += nt(parts, pick)
    table_ref[...] = acc_ref[:heads] + acc_ref[heads:]


def struct(shape, kind):
    return jax.ShapeDtypeStruct(shape, kind)


def whole(array):
    zeros = (0,) * array.ndim
    return pl.BlockSpec(array.shape, lambda *_: zeros)


def call(kernel, grid, in_specs, inputs, out_specs, out_shape, scratch, flops, name):
    moved = sum(a.size * a.dtype.itemsize for a in inputs)
    moved += sum(a.size * a.dtype.itemsize for a in jax.tree.leaves(out_shape))
    return pl.pallas_call(
        kernel,
        grid_spec=pltpu.PrefetchScalarGridSpec(
            num_scalar_prefetch=1,
            grid=grid,
            in_specs=in_specs,
            out_specs=out_specs,
            scratch_shapes=scratch,
        ),
        out_shape=out_shape,
        cost_estimate=pl.CostEstimate(flops=flops, bytes_accessed=moved, transcendentals=0),
        name=name,
    )


def digits_of(count):
    digits, stride = [], 1
    for size in (2, 2):
        if (count // stride) % size == 0 and count // stride > 1:
            digits.append((stride, size))
            stride *= size
    while count // stride > 1:
        size = 4 if (count // stride) % 4 == 0 else 2
        digits.append((stride, size))
        stride *= size
    return digits


def xor_exchange(value, axis, count, mask):
    return lax.ppermute(value, axis, [(i, i ^ mask) for i in range(count)])


def scatter_sum(value, axis, count, digits, order):
    index = lax.axis_index(axis)
    rows, cols = value.shape
    cur = value.reshape([size for _, size in reversed(digits)] + [rows // count, cols])
    left = list(reversed(range(len(digits))))
    for turn, digit in enumerate(order):
        stride, size = digits[digit]
        place = left.index(digit)
        mine = (index // stride) % size

        def part(which):
            return lax.dynamic_index_in_dim(cur, which, place, keepdims=False)

        received = [
            xor_exchange(part(mine ^ s), axis, count, s * stride) for s in range(1, size)
        ]
        total = part(mine).astype(F32)
        for piece in received:
            total = total + piece.astype(F32)
        left.remove(digit)
        cur = total if turn == len(order) - 1 else total.astype(BF16)
    return cur


def all_sum(value, axis, count):
    mask = 1
    while mask < count:
        if 4 * mask <= count:
            got = [xor_exchange(value, axis, count, s * mask) for s in (1, 2, 3)]
            value = (value + got[0]) + (got[1] + got[2])
            mask *= 4
        else:
            value = value + xor_exchange(value, axis, count, mask)
            mask *= 2
    return value


def per_device(
    n_dp,
    n_tensor,
    tokens,
    region_ids,
    norm1_gain,
    norm1_bias,
    w_qkv,
    qv_bias,
    rel_table,
    w_proj,
    b_proj,
    norm2_gain,
    norm2_bias,
    w_fc1,
    b_fc1,
    w_fc2,
    b_fc2,
    cotangent,
):
    all_images, _, width = tokens.shape
    images = all_images // n_tensor
    entries, heads = rel_table.shape
    chan = heads * HEAD_DIM
    hidden = w_fc1.shape[1]
    rows_t = images * TPAD
    rows_w = images * WINS * WPAD
    half_rows = -(-entries // 16) * 16
    me = lax.axis_index("tensor")
    me_arr = me.reshape(1).astype(jnp.int32)

    def swap(value):
        return lax.ppermute(value, "tensor", [(i, i ^ 1) for i in range(n_tensor)])

    table_o = swap(rel_table)
    qvb_o = swap(qv_bias)
    wm = w_qkv.reshape(width, 3 * chan)
    wo = swap(wm)
    po = swap(w_proj)
    b1_o = swap(b_fc1)
    w1o = swap(w_fc1)
    w2o = swap(w_fc2)

    row = lambda vec: vec.reshape(1, -1)
    ids = jnp.pad(region_ids, ((0, 0), (0, TPAD - TOK)))
    qvb = jnp.concatenate([qv_bias, qvb_o], axis=1)

    table_t = jnp.concatenate(
        [
            jnp.pad(rel_table.T, ((0, 0), (0, half_rows - entries))),
            jnp.pad(table_o.T, ((0, 0), (0, half_rows - entries))),
        ],
        axis=1,
    )
    part_a = lax.reduce_precision(table_t, 8, 7)
    part_b = lax.reduce_precision(table_t - part_a, 8, 7)
    part_c = table_t - part_a - part_b
    parts = jnp.concatenate([part_a, part_b, part_c], axis=0).astype(BF16)
    bias_shape = struct((heads * WPAD, 2 * WPAD), F32)
    bias = pl.pallas_call(
        functools.partial(bias_kernel, heads, half_rows),
        out_shape=bias_shape,
        scratch_shapes=[pltpu.VMEM((2 * half_rows, 2 * WPAD), jnp.int32)],
        name="bias",
    )(parts)

    image_spec = pl.BlockSpec((images, TOK, width), lambda i, me: (me[0], 0, 0))
    half_spec = pl.BlockSpec((images, TOK, width), lambda i, me: (0, 0, 0))

    ins = (
        tokens,
        ids,
        row(norm1_gain),
        row(norm1_bias),
        wm,
        wo,
        qvb,
        bias,
        w_proj,
        po,
        row(b_proj),
    )
    outs = (
        struct((rows_w, 2 * chan), BF16),
        struct((rows_w, 2 * chan), BF16),
        struct((rows_w, 2 * chan), BF16),
        struct((rows_w, width), BF16),
        struct((images * WINS, heads, 2 * WPAD), F32),
        struct((rows_t, 2 * chan), BF16),
        struct((rows_t, width), F32),
    )
    q, k, v, win_in, lse, merged, resid = call(
        functools.partial(attend_kernel, images, heads),
        (1,),
        [image_spec] + [whole(a) for a in ins[1:]],
        ins,
        [whole(a) for a in outs],
        outs,
        [
            pltpu.VMEM((rows_t, width), F32),
            pltpu.VMEM((WINS * WPAD, TPAD), BF16),
            pltpu.VMEM((rows_w, 2 * chan), BF16),
            pltpu.VMEM((heads * WPAD, 2 * chan), BF16),
        ],
        3 * 10**9,
        "attend",
    )(me_arr, *ins)

    steps = 4
    chunk = hidden // steps
    w_spec = pl.BlockSpec((width, chunk), lambda i, me: (0, i))
    b_spec = pl.BlockSpec((1, chunk), lambda i, me: (0, i))
    ins = (
        resid,
        cotangent,
        row(norm2_gain),
        row(norm2_bias),
        row(b_fc2),
        w_fc1,
        w1o,
        w_fc2,
        w2o,
        row(b_fc1),
        row(b1_o),
    )
    outs = (
        struct((width, hidden), BF16),
        struct((width, hidden), BF16),
        struct((width, hidden), BF16),
        struct((width, hidden), BF16),
        struct((1, hidden), F32),
        struct((1, hidden), F32),
        struct(tokens.shape, BF16),
        struct((images, TOK, width), BF16),
        struct((rows_t, width), F32),
        struct((8, width), F32),
    )
    g1m, g1o, g2m, g2o, gbm, gbo, out_full, out_half, gres, sums_two = call(
        functools.partial(ffn_kernel, images),
        (steps,),
        [whole(resid), image_spec]
        + [whole(a) for a in ins[2:5]]
        + [w_spec] * 4
        + [b_spec] * 2,
        ins,
        [w_spec] * 4 + [b_spec] * 2 + [image_spec, half_spec] + [whole(a) for a in outs[8:]],
        outs,
        [
            pltpu.VMEM((rows_t, width), BF16),
            pltpu.VMEM((width, rows_t), BF16),
            pltpu.VMEM((rows_t, width), BF16),
            pltpu.VMEM((width, rows_t), BF16),
            pltpu.VMEM((rows_t, width), F32),
            pltpu.VMEM((rows_t, width), F32),
        ],
        6 * 10**9,
        "ffn",
    )(me_arr, *ins)

    digits = digits_of(n_dp)
    order_a = list(range(len(digits)))
    order_b = order_a[1:2] + order_a[:1] + order_a[2:]

    def pair_sum(mine, other):
        return (mine.astype(F32) + swap(other).astype(F32)).astype(BF16)

    sent_fc1 = scatter_sum(pair_sum(g1m, g1o), "dp", n_dp, digits, order_a)
    sent_fc2 = scatter_sum(pair_sum(g2m, g2o), "dp", n_dp, digits, order_b)
    out_other = swap(out_half)
    output = lax.dynamic_update_slice_in_dim(out_full, out_other, (1 - me) * images, 0)

    ins = (gres, ids, merged, w_proj, po, q, k, v, win_in, lse, bias)
    outs = (
        struct((width, 3 * chan), BF16),
        struct((width, 3 * chan), BF16),
        struct((width, chan), BF16),
        struct((width, chan), BF16),
        struct((rows_w, 6 * chan), BF16),
        struct((8, 2 * chan), F32),
        bias_shape,
    )
    gwm, gwo, gpm, gpo, gqkv, sums_qv, gbias = call(
        functools.partial(attend_back_kernel, images, heads),
        (1,),
        [whole(a) for a in ins],
        ins,
        [whole(a) for a in outs],
        outs,
        [
            pltpu.VMEM((WINS * WPAD, TPAD), BF16),
            pltpu.VMEM((rows_w, 2 * chan), BF16),
            pltpu.VMEM((heads * WPAD, 2 * chan), BF16),
            pltpu.VMEM((WPAD, 2 * chan), F32),
            pltpu.VMEM((WPAD, 2 * chan), F32),
        ],
        5 * 10**9,
        "attend_back",
    )(me_arr, *ins)

    gw = pair_sum(gwm, gwo)
    gp = pair_sum(gpm, gpo)
    cut = 2 * chan
    sent_a = scatter_sum(gw[:, :cut], "dp", n_dp, digits, order_a)
    sent_b = scatter_sum(
        jnp.concatenate([gw[:, cut:], gp], axis=1), "dp", n_dp, digits, order_b
    )
    sent_qkv = jnp.concatenate([sent_a, sent_b[:, :chan]], axis=1).reshape(-1, 3, chan)
    sent_proj = sent_b[:, chan:]

    ins = (tokens, gres, gqkv, wm, wo, row(norm1_gain), gbias)
    outs = (
        struct(tokens.shape, F32),
        struct((images, TOK, width), F32),
        struct((8, width), F32),
        struct((heads, 2 * half_rows), F32),
    )
    grad_full, grad_half, sums_one, g_table = call(
        functools.partial(last_kernel, images, heads, half_rows),
        (1,),
        [image_spec] + [whole(a) for a in ins[1:]],
        ins,
        [image_spec, half_spec] + [whole(a) for a in outs[2:]],
        outs,
        [
            pltpu.VMEM((rows_t, width), F32),
            pltpu.VMEM((2 * half_rows, 2 * WPAD), jnp.int32),
            pltpu.VMEM((2 * heads, 2 * half_rows), F32),
        ],
        2 * 10**9,
        "last",
    )(me_arr, *ins)
    grad_in = lax.dynamic_update_slice_in_dim(
        grad_full, swap(grad_half), (1 - me) * images, 0
    )

    shared = jnp.concatenate([sums_two[:4], sums_one[:2]], axis=0).reshape(-1)
    own = jnp.concatenate(
        [sums_qv[:2, :chan].reshape(-1), g_table[:, :half_rows].reshape(-1), gbm.reshape(-1)]
    )
    theirs = jnp.concatenate(
        [sums_qv[:2, chan:].reshape(-1), g_table[:, half_rows:].reshape(-1), gbo.reshape(-1)]
    )
    lanes = 128
    small = jnp.concatenate([shared, own]).reshape(-1, lanes)
    small = small + swap(jnp.concatenate([shared, theirs]).reshape(-1, lanes))
    small = all_sum(small, "dp", n_dp).reshape(-1)
    vectors = small[: 6 * width].reshape(6, width)
    at = 6 * width
    sum_qv = small[at : at + 2 * chan].reshape(2, chan)
    at += 2 * chan
    sum_table = small[at : at + heads * half_rows].reshape(heads, half_rows)[:, :entries].T
    at += heads * half_rows
    sum_b1 = small[at : at + hidden]
    return (
        output,
        grad_in,
        vectors[4],
        vectors[5],
        sent_qkv,
        sum_qv,
        sum_table,
        sent_proj,
        vectors[0],
        vectors[1],
        vectors[2],
        sent_fc1,
        sum_b1,
        sent_fc2,
        vectors[3],
    )


def solution(mesh):
    return jax.shard_map(
        functools.partial(per_device, mesh.shape["dp"], mesh.shape["tensor"]),
        mesh=mesh,
        in_specs=(
            P("dp", None, None),
            P("dp", None),
            P(),
            P(),
            P(None, None, "tensor"),
            P(None, "tensor"),
            P(None, "tensor"),
            P(None, "tensor"),
            P(),
            P(),
            P(),
            P(None, "tensor"),
            P("tensor"),
            P(None, "tensor"),
            P(),
            P("dp", None, None),
        ),
        out_specs=(
            P("dp", None, None),
            P("dp", None, None),
            P(),
            P(),
            P("dp", None, "tensor"),
            P(None, "tensor"),
            P(None, "tensor"),
            P("dp", "tensor"),
            P(),
            P(),
            P(),
            P("dp", "tensor"),
            P("tensor"),
            P("dp", "tensor"),
            P(),
        ),
        check_vma=False,
    )
```

```python
import functools

import jax
import jax.numpy as jnp
from jax import lax
from jax.experimental import pallas as pl
from jax.experimental.pallas import tpu as pltpu
from jax.sharding import PartitionSpec as P


HEAD_DIM = 32
SIDE = 14
WIN = 7
SHIFT = 3
NORM_EPS = 1e-05

TOK = SIDE * SIDE
TPAD = 208
WTOK = WIN * WIN
WPAD = 64
BLOCKS = SIDE // WIN
WINS = BLOCKS * BLOCKS
F32 = jnp.float32
BF16 = jnp.bfloat16
LIMIT = 16


def nn(a, b):
    return lax.dot_general(a, b, (((1,), (0,)), ((), ())), preferred_element_type=F32)


def nt(a, b):
    return lax.dot_general(a, b, (((1,), (1,)), ((), ())), preferred_element_type=F32)


def tn(a, b):
    return lax.dot_general(a, b, (((0,), (0,)), ((), ())), preferred_element_type=F32)


def iota(shape, axis):
    return lax.broadcasted_iota(jnp.int32, shape, axis)


def normalize(source):
    center = jnp.mean(source, axis=-1, keepdims=True)
    centred = source - center
    inverse = lax.rsqrt(jnp.mean(centred * centred, axis=-1, keepdims=True) + NORM_EPS)
    return centred * inverse, inverse


def norm_back(upstream, normed, inverse, gain_vec):
    scaled = upstream * gain_vec
    return inverse * (
        scaled
        - jnp.mean(scaled, axis=-1, keepdims=True)
        - normed * jnp.mean(scaled * normed, axis=-1, keepdims=True)
    )


def seventh(value):
    return (value * 37) >> 8


def window_source(slot):
    window, at = slot >> 6, slot & (WPAD - 1)
    row = (window >> 1) * WIN + seventh(at) + SHIFT
    col = (window & 1) * WIN + (at - seventh(at) * WIN) + SHIFT
    row = jnp.where(row >= SIDE, row - SIDE, row)
    col = jnp.where(col >= SIDE, col - SIDE, col)
    return jnp.where(at < WTOK, row * SIDE + col, -1)


def gather_matrix():
    shape = (WINS * WPAD, TPAD)
    hit = window_source(iota(shape, 0)) == iota(shape, 1)
    return jnp.where(hit, 1.0, 0.0).astype(BF16)


def scatter_matrix():
    shape = (TPAD, WINS * WPAD)
    hit = window_source(iota(shape, 1)) == iota(shape, 0)
    return jnp.where(hit, 1.0, 0.0).astype(BF16)


def head_mask(heads):
    shape = (heads * WPAD, 2 * heads * HEAD_DIM)
    hit = (iota(shape, 0) >> 6) == ((iota(shape, 1) & (heads * HEAD_DIM - 1)) >> 5)
    return jnp.where(hit, 1.0, 0.0).astype(BF16)


def log2(value):
    return value.bit_length() - 1


def row_order(slot, rows, digits, order):
    rest, block = slot >> log2(rows), 0
    for digit in reversed(order):
        stride, size = digits[digit]
        block = block + (rest & (size - 1)) * stride
        rest = rest >> log2(size)
    return block * rows + (slot & (rows - 1))


def order_matrix(width, layout):
    shape = (width, width)
    hit = row_order(iota(shape, 0), *layout) == iota(shape, 1)
    return jnp.where(hit, 1.0, 0.0).astype(BF16)


def fill_rows(rows_ref, block_ref, first, images):
    rows_ref[...] = jnp.zeros(rows_ref.shape, rows_ref.dtype)
    for image in range(images):
        rows_ref[image * TPAD : image * TPAD + TOK, :] = block_ref[first + image].astype(
            rows_ref.dtype
        )


def window_mask(ids_row, pick):
    ids_b = jnp.broadcast_to(ids_row.astype(F32), (2 * WPAD, TOK)).astype(BF16)
    pick = pick[:, :TOK]
    keys = nt(pick, ids_b)
    queries = nt(ids_b[:16], jnp.concatenate([pick, pick], axis=0))[0:1]
    shape = (WPAD, 2 * WPAD)
    key_at = iota(shape, 0)
    query_at = iota(shape, 1) & (WPAD - 1)
    same = jnp.logical_or(keys == queries, query_at >= WTOK)
    return jnp.where(jnp.logical_and(same, key_at < WTOK), 0.0, -jnp.inf)


def two_groups(rows):
    half = rows.shape[1] // 2
    zero = jnp.zeros((rows.shape[0], half), rows.dtype)
    return jnp.concatenate(
        [
            jnp.concatenate([rows[:, :half], zero], axis=1),
            jnp.concatenate([zero, rows[:, half:]], axis=1),
        ],
        axis=0,
    )


def own_groups(rows):
    half = rows.shape[1] // 2
    return jnp.concatenate([rows[:WPAD, :half], rows[WPAD:, half:]], axis=1)


def per_head(rows, mask, heads):
    return jnp.concatenate([rows] * heads, axis=0) * mask


def table_offsets(rows_half):
    shape = (2 * rows_half, 2 * WPAD)
    entry, query = iota(shape, 0), iota(shape, 1)
    group_e = jnp.where(entry >= rows_half, 1, 0)
    at = query & (WPAD - 1)
    place = seventh(at) * (2 * WIN - 1) + (at - seventh(at) * WIN)
    fits = jnp.logical_and(group_e == (query >> 6), at < WTOK)
    return jnp.where(fits, entry - group_e * rows_half - place, 4096)


def key_offset(key):
    row = key // WIN
    return 2 * WIN * (WIN - 1) - (row * (2 * WIN - 1) + key - row * WIN)


def bias_kernel(heads, rows_half, sel_ref, mine_ref, other_ref, bias_ref, off_ref, table_ref):
    off_ref[...] = table_offsets(rows_half)
    bias_ref[...] = jnp.zeros(bias_ref.shape, F32)
    entries = mine_ref.shape[1]
    table_ref[...] = jnp.zeros(table_ref.shape, F32)
    table_ref[:, :entries] = mine_ref[...]
    table_ref[:, rows_half : rows_half + entries] = other_ref[...]
    table = table_ref[...]
    part_a = table.astype(BF16).astype(F32)
    part_b = (table - part_a).astype(BF16).astype(F32)
    part_c = table - part_a - part_b
    parts = jnp.concatenate([part_a, part_b, part_c], axis=0).astype(BF16)
    for key in range(WTOK):
        pick = jnp.where(off_ref[...] == key_offset(key), 1.0, 0.0).astype(BF16)
        rows = nn(parts, pick)
        bias_ref[pl.ds(key, heads, stride=WPAD), :] = (
            rows[:heads] + rows[heads : 2 * heads] + rows[2 * heads :]
        )


def attend_kernel(
    images,
    heads,
    me_ref,
    tok_ref,
    ids_ref,
    gain_ref,
    shift_ref,
    wm_ref,
    wo_ref,
    qvbm_ref,
    qvbo_ref,
    bias_ref,
    pm_ref,
    po_ref,
    bproj_ref,
    q_ref,
    k_ref,
    v_ref,
    win_ref,
    lse_ref,
    merged_ref,
    resid_ref,
    x_ref,
    pick_ref,
    att_ref,
    mask_ref,
):
    chan = heads * HEAD_DIM
    factor = HEAD_DIM ** (-0.5)
    fill_rows(x_ref, tok_ref, me_ref[0] * images, images)
    normed, _ = normalize(x_ref[...])
    ln_one = (normed * gain_ref[...] + shift_ref[...]).astype(BF16)
    pick_ref[...] = gather_matrix()
    mask_ref[...] = head_mask(heads)
    slots = WINS * WPAD
    for image in range(images):
        win_ref[image * slots : (image + 1) * slots, :] = nn(
            pick_ref[...], ln_one[image * TPAD : (image + 1) * TPAD]
        ).astype(BF16)
    for group, (w_ref, b_ref) in enumerate(((wm_ref, qvbm_ref), (wo_ref, qvbo_ref))):
        cols = slice(group * chan, (group + 1) * chan)
        win = win_ref[...]
        q_ref[:, cols] = ((nn(win, w_ref[0]) + b_ref[0:1, :]) * factor).astype(BF16)
        k_ref[:, cols] = nn(win, w_ref[1]).astype(BF16)
        v_ref[:, cols] = (nn(win, w_ref[2]) + b_ref[1:2, :]).astype(BF16)

    def one_window(window, carry):
        rows = pl.ds(pl.multiple_of(window * WPAD, WPAD), WPAD)
        image = window // WINS
        local = pl.multiple_of((window - image * WINS) * WPAD, WPAD)
        ids_row = ids_ref[pl.ds(me_ref[0] * images + image, 1), :]
        allowed = window_mask(ids_row, pick_ref[pl.ds(local, WPAD), :])
        k_all = per_head(k_ref[rows, :], mask_ref[...], heads)
        v_all = per_head(v_ref[rows, :], mask_ref[...], heads)
        scores = nt(k_all, two_groups(q_ref[rows, :])) + bias_ref[...]
        scores = scores.reshape(heads, WPAD, 2 * WPAD) + allowed[None]
        top = jnp.max(scores, axis=1, keepdims=True)
        grown = jnp.exp(scores - top)
        total = jnp.sum(grown, axis=1, keepdims=True)
        lse_ref[window] = (top + jnp.log(total)).reshape(heads, 2 * WPAD)
        probs = (grown * (1.0 / total)).astype(BF16).reshape(heads * WPAD, 2 * WPAD)
        att_ref[rows, :] = own_groups(tn(probs, v_all)).astype(BF16)
        return carry

    lax.fori_loop(0, images * WINS, one_window, 0)
    back = scatter_matrix()
    for image in range(images):
        merged_ref[image * TPAD : (image + 1) * TPAD, :] = nn(
            back, att_ref[image * slots : (image + 1) * slots, :]
        ).astype(BF16)
    resid_ref[...] = (
        x_ref[...]
        + (nt(merged_ref[:, :chan], pm_ref[...]) + nt(merged_ref[:, chan:], po_ref[...]))
        + bproj_ref[...]
    )


def ffn_kernel(
    images,
    layouts,
    last,
    me_ref,
    resid_ref,
    cot_ref,
    gain_ref,
    shift_ref,
    w1_ref,
    w2_ref,
    b1_ref,
    *refs,
):
    if last:
        b2_ref, ln_ref, lnt_ref, cot_b_ref, cot_t_ref, ffn_in, gln_in = refs[:7]
        g1_ref, g2_ref, gb_ref, out_ref, half_ref, gres_ref, sums_ref = refs[7:14]
        ffn_ref, gln_ref = refs[14:]
    else:
        g1_ref, g2_ref, gb_ref = refs[:3]
        ln_ref, lnt_ref, cot_b_ref, cot_t_ref, ffn_ref, gln_ref = refs[3:]
    if last:
        ffn_ref[...] = ffn_in[...]
        gln_ref[...] = gln_in[...]
    else:
        normed, _ = normalize(resid_ref[...])
        ln_ref[...] = (normed * gain_ref[...] + shift_ref[...]).astype(BF16)
        fill_rows(cot_b_ref, cot_ref, me_ref[0] * images, images)
        width = ln_ref.shape[1]
        lnt_ref[...] = nt(order_matrix(width, layouts[0]), ln_ref[...]).astype(BF16)
        cot_t_ref[...] = nt(order_matrix(width, layouts[1]), cot_b_ref[...]).astype(BF16)
        ffn_ref[...] = jnp.zeros(ffn_ref.shape, F32)
        gln_ref[...] = jnp.zeros(gln_ref.shape, F32)
    chunk = 256

    def one_chunk(at, carry):
        cols = pl.ds(pl.multiple_of(at * chunk, chunk), chunk)
        pre = nn(ln_ref[...], w1_ref[:, cols]) + b1_ref[:, cols]
        phi = 0.5 * (1.0 + lax.erf(pre * 0.7071067811865476))
        act = (pre * phi).astype(BF16)
        slope = phi + pre * jnp.exp(-0.5 * pre * pre) * 0.3989422804014327
        grad_pre = nn(cot_b_ref[...], w2_ref[:, cols]) * slope
        gb_ref[:, cols] = jnp.sum(grad_pre, axis=0, keepdims=True)
        grad_pre = grad_pre.astype(BF16)
        ffn_ref[...] += nt(act, w2_ref[:, cols])
        gln_ref[...] += nt(grad_pre, w1_ref[:, cols])
        g2_ref[:, cols] = nn(cot_t_ref[...], act).astype(BF16)
        g1_ref[:, cols] = nn(lnt_ref[...], grad_pre).astype(BF16)
        return carry

    lax.fori_loop(0, w1_ref.shape[1] // chunk, one_chunk, 0)
    if not last:
        return
    resid = resid_ref[...]
    result = (resid + ffn_ref[...] + b2_ref[...]).astype(BF16)
    for image in range(images):
        piece = result[image * TPAD : image * TPAD + TOK]
        out_ref[me_ref[0] * images + image] = piece
        half_ref[image] = piece
    normed, inverse = normalize(resid)
    upstream = gln_ref[...]
    cot = cot_b_ref[...].astype(F32)
    grad_resid = cot + norm_back(upstream, normed, inverse, gain_ref[...])
    gres_ref[...] = grad_resid
    sums_ref[0:1, :] = jnp.sum(grad_resid, axis=0, keepdims=True)
    sums_ref[1:2, :] = jnp.sum(upstream * normed, axis=0, keepdims=True)
    sums_ref[2:3, :] = jnp.sum(upstream, axis=0, keepdims=True)
    sums_ref[3:4, :] = jnp.sum(cot, axis=0, keepdims=True)
    sums_ref[4:8, :] = jnp.zeros((4, sums_ref.shape[1]), F32)


def attend_back_kernel(
    images,
    heads,
    layouts,
    me_ref,
    gres_ref,
    ids_ref,
    merged_ref,
    pm_ref,
    po_ref,
    q_ref,
    k_ref,
    v_ref,
    win_ref,
    lse_ref,
    bias_ref,
    gqkm_ref,
    gqko_ref,
    gvpm_ref,
    gvpo_ref,
    gqkv_ref,
    sums_ref,
    gbias_ref,
    pick_ref,
    gatt_ref,
    mask_ref,
    qsum_ref,
    vsum_ref,
):
    chan = heads * HEAD_DIM
    wide = 2 * chan
    factor = HEAD_DIM ** (-0.5)
    slots = WINS * WPAD
    pick_ref[...] = gather_matrix()
    mask_ref[...] = head_mask(heads)
    gres = gres_ref[...]
    gres_b = gres.astype(BF16)
    width = gres.shape[1]
    gres_t = nt(order_matrix(width, layouts[1]), gres_b).astype(BF16)
    gvpm_ref[:, chan:] = nn(gres_t, merged_ref[:, :chan]).astype(BF16)
    gvpo_ref[:, chan:] = nn(gres_t, merged_ref[:, chan:]).astype(BF16)
    grad_m = jnp.concatenate(
        [nn(gres_b, pm_ref[...]).astype(BF16), nn(gres_b, po_ref[...]).astype(BF16)], axis=1
    )
    for image in range(images):
        gatt_ref[image * slots : (image + 1) * slots, :] = nn(
            pick_ref[...], grad_m[image * TPAD : (image + 1) * TPAD]
        ).astype(BF16)
    gbias_ref[...] = jnp.zeros(gbias_ref.shape, F32)
    qsum_ref[...] = jnp.zeros(qsum_ref.shape, F32)
    vsum_ref[...] = jnp.zeros(vsum_ref.shape, F32)

    def one_window(window, carry):
        rows = pl.ds(pl.multiple_of(window * WPAD, WPAD), WPAD)
        image = window // WINS
        local = pl.multiple_of((window - image * WINS) * WPAD, WPAD)
        ids_row = ids_ref[pl.ds(me_ref[0] * images + image, 1), :]
        allowed = window_mask(ids_row, pick_ref[pl.ds(local, WPAD), :])
        mask = mask_ref[...]
        k_all = per_head(k_ref[rows, :], mask, heads)
        v_all = per_head(v_ref[rows, :], mask, heads)
        q_two = two_groups(q_ref[rows, :])
        g_two = two_groups(gatt_ref[rows, :])
        scores = nt(k_all, q_two) + bias_ref[...]
        scores = scores.reshape(heads, WPAD, 2 * WPAD) + allowed[None]
        probs = jnp.exp(scores - lse_ref[window].reshape(heads, 1, 2 * WPAD))
        g_probs = nt(v_all, g_two).reshape(heads, WPAD, 2 * WPAD)
        inner = jnp.sum(probs * g_probs, axis=1, keepdims=True)
        g_scores = (probs * (g_probs - inner)).reshape(heads * WPAD, 2 * WPAD)
        gbias_ref[...] += g_scores
        probs_b = probs.astype(BF16).reshape(heads * WPAD, 2 * WPAD)
        g_scores = g_scores.astype(BF16)

        def fold(product):
            return jnp.sum((product * mask.astype(F32)).reshape(heads, WPAD, wide), axis=0)

        g_v = fold(nn(probs_b, g_two))
        g_k = fold(nn(g_scores, q_two))
        g_q = own_groups(tn(g_scores, k_all)) * factor
        qsum_ref[...] += g_q
        vsum_ref[...] += g_v
        for group in range(2):
            cols = slice(group * chan, (group + 1) * chan)
            base = group * 3 * chan
            gqkv_ref[rows, base : base + chan] = g_q[:, cols].astype(BF16)
            gqkv_ref[rows, base + chan : base + 2 * chan] = g_k[:, cols].astype(BF16)
            gqkv_ref[rows, base + 2 * chan : base + 3 * chan] = g_v[:, cols].astype(BF16)
        return carry

    lax.fori_loop(0, images * WINS, one_window, 0)
    sums_ref[...] = jnp.zeros(sums_ref.shape, F32)
    sums_ref[0:1, :] = jnp.sum(qsum_ref[...], axis=0, keepdims=True)
    sums_ref[1:2, :] = jnp.sum(vsum_ref[...], axis=0, keepdims=True)
    win_a = nt(order_matrix(width, layouts[0]), win_ref[...]).astype(BF16)
    win_b = nt(order_matrix(width, layouts[1]), win_ref[...]).astype(BF16)
    gqko_ref[...] = nn(win_a, gqkv_ref[:, 3 * chan : 5 * chan]).astype(BF16)
    gvpo_ref[:, :chan] = nn(win_b, gqkv_ref[:, 5 * chan :]).astype(BF16)
    gqkm_ref[...] = nn(win_a, gqkv_ref[:, : 2 * chan]).astype(BF16)
    gvpm_ref[:, :chan] = nn(win_b, gqkv_ref[:, 2 * chan : 3 * chan]).astype(BF16)


def last_kernel(
    images,
    heads,
    rows_half,
    me_ref,
    tok_ref,
    gres_ref,
    gqkv_ref,
    wm_ref,
    wo_ref,
    gain_ref,
    gbias_ref,
    two_ref,
    qv_ref,
    gbm_ref,
    gbo_ref,
    full_ref,
    half_ref,
    mine_ref,
    theirs_ref,
    x_ref,
    off_ref,
    acc_ref,
):
    chan = heads * HEAD_DIM
    slots = WINS * WPAD
    grad_win = nt(gqkv_ref[:, :chan], wm_ref[0])
    for at in range(1, 6):
        w_ref = wm_ref if at < 3 else wo_ref
        grad_win += nt(gqkv_ref[:, at * chan : (at + 1) * chan], w_ref[at % 3])
    high = grad_win.astype(BF16)
    low = (grad_win - high.astype(F32)).astype(BF16)
    back = scatter_matrix()
    upstream = jnp.concatenate(
        [
            nn(back, high[image * slots : (image + 1) * slots])
            + nn(back, low[image * slots : (image + 1) * slots])
            for image in range(images)
        ],
        axis=0,
    )
    fill_rows(x_ref, tok_ref, me_ref[0] * images, images)
    normed, inverse = normalize(x_ref[...])
    grad_in = gres_ref[...] + norm_back(upstream, normed, inverse, gain_ref[...])
    for image in range(images):
        piece = grad_in[image * TPAD : image * TPAD + TOK]
        full_ref[me_ref[0] * images + image] = piece
        half_ref[image] = piece
    width = upstream.shape[1]
    gain_sum = jnp.sum(upstream * normed, axis=0, keepdims=True)
    shift_sum = jnp.sum(upstream, axis=0, keepdims=True)
    off_ref[...] = table_offsets(rows_half)
    acc_ref[...] = jnp.zeros(acc_ref.shape, F32)
    for key in range(WTOK):
        pick = jnp.where(off_ref[...] == key_offset(key), 1.0, 0.0).astype(BF16)
        rows = gbias_ref[pl.ds(key, heads, stride=WPAD), :]
        top = rows.astype(BF16).astype(F32)
        parts = jnp.concatenate([top, rows - top], axis=0).astype(BF16)
        acc_ref[...] += nt(parts, pick)
    table = acc_ref[:heads] + acc_ref[heads:]
    for group, (pack_ref, gb_ref) in enumerate(((mine_ref, gbm_ref), (theirs_ref, gbo_ref))):
        pack_ref[...] = jnp.zeros(pack_ref.shape, F32)
        pack_ref[0:4, :] = two_ref[0:4, :]
        pack_ref[4:5, :] = gain_sum
        pack_ref[5:6, :] = shift_sum
        pack_ref[6:8, :chan] = qv_ref[0:2, group * chan : (group + 1) * chan]
        for at in range(gb_ref.shape[1] // width):
            pack_ref[8 + at : 9 + at, :] = gb_ref[:, at * width : (at + 1) * width]
        pack_ref[16 : 16 + heads, :rows_half] = table[:, group * rows_half : (group + 1) * rows_half]


def unpack_kernel(parts, sel_ref, *refs):
    ins, outs = refs[:parts], refs[parts:]
    if parts == 2:
        total = ins[0][...] + ins[1][...]
    else:
        total = (ins[0][...] + ins[1][...]) + (ins[2][...] + ins[3][...])
    for at in range(6):
        outs[at][...] = total[at : at + 1]
    qv_ref, b1_ref, table_ref = outs[6:]
    qv_ref[...] = total[6:8, : qv_ref.shape[1]]
    width = total.shape[1]
    for at in range(b1_ref.shape[1] // width):
        b1_ref[:, at * width : (at + 1) * width] = total[8 + at : 9 + at]
    table_ref[...] = total[16 : 16 + table_ref.shape[0], : table_ref.shape[1]]


def row_block(ref, sel_ref, blocks, form):
    index = form[0]
    for at, factor in enumerate(form[1:]):
        if factor:
            index = index + factor * sel_ref[at]
    rows = ref.shape[0] // blocks
    if blocks == 1:
        return ref[...].astype(F32)
    return ref[pl.ds(pl.multiple_of(index * rows, rows), rows), :].astype(F32)


def sum_kernel(groups, sel_ref, *refs):
    at, outs = 0, refs[sum(len(g) for g in groups) :]
    for picks, out_ref in zip(groups, outs):
        total = row_block(refs[at], sel_ref, *picks[0])
        for more in range(1, len(picks)):
            total = total + row_block(refs[at + more], sel_ref, *picks[more])
        out_ref[...] = total.astype(out_ref.dtype)
        at += len(picks)


def fan_kernel(groups, rows, sends, sel_ref, *refs):
    flat = sum(len(g) for g in groups)
    outs, total_ref, at, col = refs[flat:-1], refs[-1], 0, 0
    for picks in groups:
        total = row_block(refs[at], sel_ref, *picks[0])
        for more in range(1, len(picks)):
            total = total + row_block(refs[at + more], sel_ref, *picks[more])
        total_ref[:, col : col + total.shape[1]] = total
        col += total.shape[1]
        at += len(picks)
    own = sel_ref[3]
    for s in range(1, sends + 1):
        piece = total_ref[pl.ds(pl.multiple_of((own ^ s) * rows, rows), rows), :]
        outs[s - 1][...] = piece.astype(BF16)
    outs[sends][...] = total_ref[pl.ds(pl.multiple_of(own * rows, rows), rows), :]


def total_kernel(sel_ref, own_ref, *refs):
    ins, (a_ref, b_ref) = refs[:-2], refs[-2:]
    total = own_ref[...]
    for in_ref in ins:
        total = total + in_ref[...].astype(F32)
    a_ref[...] = total[:, : a_ref.shape[1]]
    b_ref[...] = total[:, a_ref.shape[1] :]


def pair_kernel(sel_ref, a_ref, b_ref, out_ref):
    out_ref[...] = a_ref[...] + b_ref[...]


def four_kernel(sel_ref, a_ref, b_ref, c_ref, d_ref, out_ref):
    out_ref[...] = (a_ref[...] + b_ref[...]) + (c_ref[...] + d_ref[...])


def struct(shape, kind):
    return jax.ShapeDtypeStruct(shape, kind)


def call(kernel, scalars, inputs, outs, scratch, flops, limit_mib):
    moved = sum(a.size * a.dtype.itemsize for a in inputs)
    moved += sum(a.size * a.dtype.itemsize for a in outs)
    vmem = pl.BlockSpec(memory_space=pltpu.VMEM)
    return pl.pallas_call(
        kernel,
        in_specs=[pl.BlockSpec(memory_space=pltpu.SMEM)] + [vmem] * len(inputs),
        out_specs=[vmem] * len(outs),
        out_shape=outs,
        scratch_shapes=scratch,
        compiler_params=pltpu.CompilerParams(vmem_limit_bytes=limit_mib << 20),
        cost_estimate=pl.CostEstimate(flops=flops, bytes_accessed=moved, transcendentals=0),
    )(scalars, *inputs)


def digits_of(count):
    digits, stride = [], 1
    for size in (2, 2):
        if (count // stride) % size == 0 and count // stride > 1:
            digits.append((stride, size))
            stride *= size
    while count // stride > 1:
        size = 4 if (count // stride) % 4 == 0 else 2
        digits.append((stride, size))
        stride *= size
    return digits


def xor_exchange(value, axis, count, mask):
    return lax.ppermute(value, axis, [(i, i ^ mask) for i in range(count)])


def scatter_sum(addends, axis, count, digits, order):
    index = lax.axis_index(axis)
    rows, cols = addends[0].shape
    shape = [size for _, size in reversed(digits)] + [rows // count, cols]
    addends = [a.reshape(shape) for a in addends]
    left = list(reversed(range(len(digits))))
    for digit in order:
        stride, size = digits[digit]
        place = left.index(digit)
        mine = (index // stride) % size

        def part(which):
            return [lax.dynamic_index_in_dim(a, which, place, keepdims=False) for a in addends]

        def total(pieces):
            result = pieces[0].astype(F32)
            for piece in pieces[1:]:
                result = result + piece.astype(F32)
            return result

        received = [
            xor_exchange(total(part(mine ^ s)).astype(BF16), axis, count, s * stride)
            for s in range(1, size)
        ]
        addends = part(mine) + received
        left.remove(digit)
    return total(addends)


def all_sum(sel, value, axis, count):
    mask = 1
    while True:
        size = 4 if 4 * mask <= count else 2
        terms = [value] + [xor_exchange(value, axis, count, s * mask) for s in range(1, size)]
        mask *= size
        if mask >= count:
            return terms
        kernel = four_kernel if size == 4 else pair_kernel
        (value,) = call(kernel, sel, terms, [struct(value.shape, F32)], [], 10**5, 2)


def add_blocks(sel, groups, kind):
    flat = [item for group in groups for item in group]
    outs = [
        struct((group[0][0].shape[0] // group[0][1], group[0][0].shape[1]), kind)
        for group in groups
    ]
    picks = tuple(tuple((blocks, form) for _, blocks, form in group) for group in groups)
    return call(
        functools.partial(sum_kernel, picks), sel, [a for a, _, _ in flat], outs, [], 10**6, 4
    )


def scatter_pairs(sel, pair_a, pair_b, axis, count, digits):
    (stride_x, _), (stride_y, _), (stride_z, size_z) = digits
    (a0, a1), (b0, b1) = pair_a, pair_b
    not_x, not_y = (1, 0, -1, 0, 0), (1, 0, 0, -1, 0)
    send_a, send_b = add_blocks(
        sel, [[(a0, 2, not_x), (a1, 2, not_x)], [(b0, 2, not_y), (b1, 2, not_y)]], BF16
    )
    got_a = xor_exchange(send_a, axis, count, stride_x)
    got_b = xor_exchange(send_b, axis, count, stride_y)
    at_a, at_b = (1, 0, 2, -1, 0), (1, 0, -1, 2, 0)
    send_a, send_b = add_blocks(
        sel,
        [
            [(a0, 4, at_a), (a1, 4, at_a), (got_a, 2, not_y)],
            [(b0, 4, at_b), (b1, 4, at_b), (got_b, 2, not_x)],
        ],
        BF16,
    )
    more_a = xor_exchange(send_a, axis, count, stride_y)
    more_b = xor_exchange(send_b, axis, count, stride_x)
    groups = (
        (
            (4, (0, 0, 2, 1, 0)),
            (4, (0, 0, 2, 1, 0)),
            (2, (0, 0, 0, 1, 0)),
            (1, (0, 0, 0, 0, 0)),
        ),
        (
            (4, (0, 0, 1, 2, 0)),
            (4, (0, 0, 1, 2, 0)),
            (2, (0, 0, 1, 0, 0)),
            (1, (0, 0, 0, 0, 0)),
        ),
    )
    cols = a0.shape[1] + b0.shape[1]
    deep = a0.shape[0] // 4
    rows = deep // size_z
    outs = (struct((rows, cols), BF16),) * (size_z - 1) + (struct((rows, cols), F32),)
    *sends, own = call(
        functools.partial(fan_kernel, groups, rows, size_z - 1),
        sel,
        [a0, a1, got_a, more_a, b0, b1, got_b, more_b],
        outs,
        [pltpu.VMEM((deep, cols), F32)],
        10**6,
        6,
    )
    received = [xor_exchange(send, axis, count, s * stride_z) for s, send in enumerate(sends, 1)]
    half = a0.shape[1]
    outs = (struct((rows, half), F32), struct((rows, cols - half), F32))
    return call(total_kernel, sel, [own] + received, outs, [], 10**6, 4)


def per_device(n_dp, n_tensor, *args):
    return block(n_dp, n_tensor, *args)


def block(
    n_dp,
    n_tensor,
    tokens,
    region_ids,
    norm1_gain,
    norm1_bias,
    w_qkv,
    qv_bias,
    rel_table,
    w_proj,
    b_proj,
    norm2_gain,
    norm2_bias,
    w_fc1,
    b_fc1,
    w_fc2,
    b_fc2,
    cotangent,
):
    all_images, _, width = tokens.shape
    images = all_images // n_tensor
    entries, heads = rel_table.shape
    chan = heads * HEAD_DIM
    hidden = w_fc1.shape[1]
    rows_t = images * TPAD
    rows_w = images * WINS * WPAD
    half_rows = -(-entries // 16) * 16
    digits = digits_of(n_dp)
    by_pairs = [size for _, size in digits] == [2, 2, 4] and width // n_dp % 16 == 0
    order_a = list(range(len(digits)))
    order_b = order_a[1:2] + order_a[:1] + order_a[2:]
    plain = order_a[::-1]
    layouts = tuple(
        (width // n_dp, digits, order if by_pairs else plain) for order in (order_a, order_b)
    )
    me = lax.axis_index("tensor")
    spot = lax.axis_index("dp")
    places = [(spot // stride) % size for stride, size in digits[:3]]
    me_arr = sel = jnp.stack([me] + places).astype(jnp.int32)

    def swap(value):
        return lax.ppermute(value, "tensor", [(i, i ^ 1) for i in range(n_tensor)])

    wm = w_qkv.transpose(1, 0, 2)
    wo = swap(wm)
    table_m = rel_table.T
    table_o = swap(table_m)
    qvb_o = swap(qv_bias)
    po = swap(w_proj)
    b1_o = swap(b_fc1.reshape(1, hidden))
    w1o = swap(w_fc1)
    w2o = swap(w_fc2)

    row = lambda vec: vec.reshape(1, -1)

    bias_shape = struct((heads * WPAD, 2 * WPAD), F32)
    (bias,) = call(
        functools.partial(bias_kernel, heads, half_rows),
        sel,
        [table_m, table_o],
        [bias_shape],
        [
            pltpu.VMEM((2 * half_rows, 2 * WPAD), jnp.int32),
            pltpu.VMEM((heads, 2 * half_rows), F32),
        ],
        10**9,
        4,
    )

    ins = (
        tokens,
        region_ids,
        row(norm1_gain),
        row(norm1_bias),
        wm,
        wo,
        qv_bias,
        qvb_o,
        bias,
        w_proj,
        po,
        row(b_proj),
    )
    outs = (
        struct((rows_w, 2 * chan), BF16),
        struct((rows_w, 2 * chan), BF16),
        struct((rows_w, 2 * chan), BF16),
        struct((rows_w, width), BF16),
        struct((images * WINS, heads, 2 * WPAD), F32),
        struct((rows_t, 2 * chan), BF16),
        struct((rows_t, width), F32),
    )
    q, k, v, win_in, lse, merged, resid = call(
        functools.partial(attend_kernel, images, heads),
        me_arr,
        ins,
        outs,
        [
            pltpu.VMEM((rows_t, width), F32),
            pltpu.VMEM((WINS * WPAD, TPAD), BF16),
            pltpu.VMEM((rows_w, 2 * chan), BF16),
            pltpu.VMEM((heads * WPAD, 2 * chan), BF16),
        ],
        3 * 10**9,
        LIMIT,
    )

    weight_grad = struct((width, hidden), BF16)
    acc = struct((rows_t, width), F32)
    kept = (
        struct((rows_t, width), BF16),
        struct((width, rows_t), BF16),
        struct((rows_t, width), BF16),
        struct((width, rows_t), BF16),
        acc,
        acc,
    )
    common = (resid, cotangent, row(norm2_gain), row(norm2_bias))
    ins = common + (w1o, w2o, b1_o)
    outs = (weight_grad, weight_grad, struct((1, hidden), F32)) + kept
    g1o, g2o, gbo, *carried = call(
        functools.partial(ffn_kernel, images, layouts, False),
        me_arr,
        ins,
        outs,
        [],
        3 * 10**9,
        LIMIT,
    )
    got1 = swap(g1o)
    got2 = swap(g2o)
    ins = common + (w_fc1, w_fc2, row(b_fc1), row(b_fc2), *carried)
    outs = (
        weight_grad,
        weight_grad,
        struct((1, hidden), F32),
        struct(tokens.shape, BF16),
        struct((images, TOK, width), BF16),
        acc,
        struct((8, width), F32),
    )
    g1m, g2m, gbm, out_full, out_half, gres, sums_two = call(
        functools.partial(ffn_kernel, images, layouts, True),
        me_arr,
        ins,
        outs,
        [pltpu.VMEM((rows_t, width), F32), pltpu.VMEM((rows_t, width), F32)],
        3 * 10**9,
        LIMIT,
    )

    def scatter(pair_a, pair_b):
        if by_pairs:
            return scatter_pairs(sel, pair_a, pair_b, "dp", n_dp, digits)
        return (
            scatter_sum(pair_a, "dp", n_dp, digits, order_a),
            scatter_sum(pair_b, "dp", n_dp, digits, order_b),
        )

    sent_fc1, sent_fc2 = scatter((g1m, got1), (g2m, got2))
    out_other = swap(out_half)
    output = lax.dynamic_update_slice_in_dim(out_full, out_other, (1 - me) * images, 0)

    ins = (gres, region_ids, merged, w_proj, po, q, k, v, win_in, lse, bias)
    outs = (
        struct((width, 2 * chan), BF16),
        struct((width, 2 * chan), BF16),
        struct((width, 2 * chan), BF16),
        struct((width, 2 * chan), BF16),
        struct((rows_w, 6 * chan), BF16),
        struct((8, 2 * chan), F32),
        bias_shape,
    )
    gqkm, gqko, gvpm, gvpo, gqkv, sums_qv, gbias = call(
        functools.partial(attend_back_kernel, images, heads, layouts),
        me_arr,
        ins,
        outs,
        [
            pltpu.VMEM((WINS * WPAD, TPAD), BF16),
            pltpu.VMEM((rows_w, 2 * chan), BF16),
            pltpu.VMEM((heads * WPAD, 2 * chan), BF16),
            pltpu.VMEM((WPAD, 2 * chan), F32),
            pltpu.VMEM((WPAD, 2 * chan), F32),
        ],
        5 * 10**9,
        LIMIT,
    )

    got_qk = swap(gqko)
    got_vp = swap(gvpo)
    sent_qk, sent_vp = scatter((gqkm, got_qk), (gvpm, got_vp))
    sent_qkv = jnp.stack(
        [sent_qk[:, :chan], sent_qk[:, chan:], sent_vp[:, :chan]], axis=0
    ).transpose(1, 0, 2)
    sent_proj = sent_vp[:, chan:]

    ins = (tokens, gres, gqkv, wm, wo, row(norm1_gain), gbias, sums_two, sums_qv, gbm, gbo)
    pack = struct((16 + heads, width), F32)
    outs = (struct(tokens.shape, F32), struct((images, TOK, width), F32), pack, pack)
    grad_full, grad_half, small, theirs = call(
        functools.partial(last_kernel, images, heads, half_rows),
        me_arr,
        ins,
        outs,
        [
            pltpu.VMEM((rows_t, width), F32),
            pltpu.VMEM((2 * half_rows, 2 * WPAD), jnp.int32),
            pltpu.VMEM((2 * heads, 2 * half_rows), F32),
        ],
        2 * 10**9,
        LIMIT,
    )
    grad_in = lax.dynamic_update_slice_in_dim(grad_full, swap(grad_half), (1 - me) * images, 0)

    got = swap(theirs)
    (small,) = call(pair_kernel, sel, [small, got], [struct(small.shape, F32)], [], 10**5, 2)
    terms = all_sum(sel, small, "dp", n_dp)
    outs = (struct((1, width), F32),) * 6 + (
        struct((2, chan), F32),
        struct((1, hidden), F32),
        struct((heads, entries), F32),
    )
    *vectors, sum_qv, sum_b1, sum_table = call(
        functools.partial(unpack_kernel, len(terms)), sel, terms, outs, [], 10**5, 2
    )
    vectors = [vec.reshape(width) for vec in vectors]
    return (
        output,
        grad_in,
        vectors[4],
        vectors[5],
        sent_qkv,
        sum_qv,
        sum_table.T,
        sent_proj,
        vectors[0],
        vectors[1],
        vectors[2],
        sent_fc1,
        sum_b1.reshape(hidden),
        sent_fc2,
        vectors[3],
    )


def solution(mesh):
    return jax.shard_map(
        functools.partial(per_device, mesh.shape["dp"], mesh.shape["tensor"]),
        mesh=mesh,
        in_specs=(
            P("dp", None, None),
            P("dp", None),
            P(),
            P(),
            P(None, None, "tensor"),
            P(None, "tensor"),
            P(None, "tensor"),
            P(None, "tensor"),
            P(),
            P(),
            P(),
            P(None, "tensor"),
            P("tensor"),
            P(None, "tensor"),
            P(),
            P("dp", None, None),
        ),
        out_specs=(
            P("dp", None, None),
            P("dp", None, None),
            P(),
            P(),
            P("dp", None, "tensor"),
            P(None, "tensor"),
            P(None, "tensor"),
            P("dp", "tensor"),
            P(),
            P(),
            P(),
            P("dp", "tensor"),
            P("tensor"),
            P("dp", "tensor"),
            P(),
        ),
        check_vma=False,
    )
```

```python
import functools

import jax
import jax.numpy as jnp
from jax import lax
from jax.experimental import pallas as pl
from jax.experimental.pallas import tpu as pltpu
from jax.sharding import PartitionSpec as P


HEAD_DIM = 32
SIDE = 14
WIN = 7
SHIFT = 3
NORM_EPS = 1e-05

TOK = SIDE * SIDE
TPAD = 208
WTOK = WIN * WIN
WPAD = 64
BLOCKS = SIDE // WIN
WINS = BLOCKS * BLOCKS
F32 = jnp.float32
BF16 = jnp.bfloat16
LIMIT = 16


def nn(a, b):
    return lax.dot_general(a, b, (((1,), (0,)), ((), ())), preferred_element_type=F32)


def nt(a, b):
    return lax.dot_general(a, b, (((1,), (1,)), ((), ())), preferred_element_type=F32)


def tn(a, b):
    return lax.dot_general(a, b, (((0,), (0,)), ((), ())), preferred_element_type=F32)


def iota(shape, axis):
    return lax.broadcasted_iota(jnp.int32, shape, axis)


def normalize(source):
    center = jnp.mean(source, axis=-1, keepdims=True)
    centred = source - center
    inverse = lax.rsqrt(jnp.mean(centred * centred, axis=-1, keepdims=True) + NORM_EPS)
    return centred * inverse, inverse


def norm_back(upstream, normed, inverse, gain_vec):
    scaled = upstream * gain_vec
    return inverse * (
        scaled
        - jnp.mean(scaled, axis=-1, keepdims=True)
        - normed * jnp.mean(scaled * normed, axis=-1, keepdims=True)
    )


def seventh(value):
    return (value * 37) >> 8


def window_source(slot):
    window, at = slot >> 6, slot & (WPAD - 1)
    row = (window >> 1) * WIN + seventh(at) + SHIFT
    col = (window & 1) * WIN + (at - seventh(at) * WIN) + SHIFT
    row = jnp.where(row >= SIDE, row - SIDE, row)
    col = jnp.where(col >= SIDE, col - SIDE, col)
    return jnp.where(at < WTOK, row * SIDE + col, -1)


def gather_matrix():
    shape = (WINS * WPAD, TPAD)
    hit = window_source(iota(shape, 0)) == iota(shape, 1)
    return jnp.where(hit, 1.0, 0.0).astype(BF16)


def scatter_matrix():
    shape = (TPAD, WINS * WPAD)
    hit = window_source(iota(shape, 1)) == iota(shape, 0)
    return jnp.where(hit, 1.0, 0.0).astype(BF16)


def head_mask(heads):
    shape = (heads * WPAD, 2 * heads * HEAD_DIM)
    hit = (iota(shape, 0) >> 6) == ((iota(shape, 1) & (heads * HEAD_DIM - 1)) >> 5)
    return jnp.where(hit, 1.0, 0.0).astype(BF16)


def log2(value):
    return value.bit_length() - 1


def row_order(slot, rows, digits, order):
    rest, block = slot >> log2(rows), 0
    for digit in reversed(order):
        stride, size = digits[digit]
        block = block + (rest & (size - 1)) * stride
        rest = rest >> log2(size)
    return block * rows + (slot & (rows - 1))


def put_rows(out_ref, layout, col, value):
    rows = layout[0]
    cols = slice(col, col + value.shape[1])
    value = value.astype(out_ref.dtype)
    sources = [row_order(at, *layout) for at in range(0, value.shape[0], rows)]
    if sources == sorted(sources):
        out_ref[:, cols] = value
        return
    for place, source in enumerate(sources):
        out_ref[place * rows : (place + 1) * rows, cols] = value[source : source + rows]


def order_matrix(width, layout):
    shape = (width, width)
    hit = row_order(iota(shape, 0), *layout) == iota(shape, 1)
    return jnp.where(hit, 1.0, 0.0).astype(BF16)


def fill_rows(rows_ref, block_ref, first, images):
    rows_ref[...] = jnp.zeros(rows_ref.shape, rows_ref.dtype)
    for image in range(images):
        rows_ref[image * TPAD : image * TPAD + TOK, :] = block_ref[first + image].astype(
            rows_ref.dtype
        )


def window_mask(ids_row, pick):
    ids_b = jnp.broadcast_to(ids_row.astype(F32), (2 * WPAD, TOK)).astype(BF16)
    pick = pick[:, :TOK]
    keys = nt(pick, ids_b)
    queries = nt(ids_b[:16], jnp.concatenate([pick, pick], axis=0))[0:1]
    shape = (WPAD, 2 * WPAD)
    key_at = iota(shape, 0)
    query_at = iota(shape, 1) & (WPAD - 1)
    same = jnp.logical_or(keys == queries, query_at >= WTOK)
    return jnp.where(jnp.logical_and(same, key_at < WTOK), 0.0, -jnp.inf)


def two_groups(rows):
    half = rows.shape[1] // 2
    zero = jnp.zeros((rows.shape[0], half), rows.dtype)
    return jnp.concatenate(
        [
            jnp.concatenate([rows[:, :half], zero], axis=1),
            jnp.concatenate([zero, rows[:, half:]], axis=1),
        ],
        axis=0,
    )


def own_groups(rows):
    half = rows.shape[1] // 2
    return jnp.concatenate([rows[:WPAD, :half], rows[WPAD:, half:]], axis=1)


def per_head(rows, mask, heads):
    return jnp.concatenate([rows] * heads, axis=0) * mask


def table_offsets(rows_half):
    shape = (2 * rows_half, 2 * WPAD)
    entry, query = iota(shape, 0), iota(shape, 1)
    group_e = jnp.where(entry >= rows_half, 1, 0)
    at = query & (WPAD - 1)
    place = seventh(at) * (2 * WIN - 1) + (at - seventh(at) * WIN)
    fits = jnp.logical_and(group_e == (query >> 6), at < WTOK)
    return jnp.where(fits, entry - group_e * rows_half - place, 4096)


def key_offset(key):
    row = key // WIN
    return 2 * WIN * (WIN - 1) - (row * (2 * WIN - 1) + key - row * WIN)


def bias_kernel(heads, rows_half, sel_ref, mine_ref, other_ref, bias_ref, off_ref, table_ref):
    off_ref[...] = table_offsets(rows_half)
    bias_ref[...] = jnp.zeros(bias_ref.shape, F32)
    entries = mine_ref.shape[1]
    table_ref[...] = jnp.zeros(table_ref.shape, F32)
    table_ref[:, :entries] = mine_ref[...]
    table_ref[:, rows_half : rows_half + entries] = other_ref[...]
    table = table_ref[...]
    part_a = table.astype(BF16).astype(F32)
    part_b = (table - part_a).astype(BF16).astype(F32)
    part_c = table - part_a - part_b
    parts = jnp.concatenate([part_a, part_b, part_c], axis=0).astype(BF16)
    for key in range(WTOK):
        pick = jnp.where(off_ref[...] == key_offset(key), 1.0, 0.0).astype(BF16)
        rows = nn(parts, pick)
        bias_ref[pl.ds(key, heads, stride=WPAD), :] = (
            rows[:heads] + rows[heads : 2 * heads] + rows[2 * heads :]
        )


def attend_kernel(
    images,
    heads,
    me_ref,
    tok_ref,
    ids_ref,
    gain_ref,
    shift_ref,
    wm_ref,
    wo_ref,
    qvbm_ref,
    qvbo_ref,
    bias_ref,
    pm_ref,
    po_ref,
    bproj_ref,
    q_ref,
    k_ref,
    v_ref,
    win_ref,
    lse_ref,
    merged_ref,
    resid_ref,
    x_ref,
    pick_ref,
    att_ref,
    mask_ref,
):
    chan = heads * HEAD_DIM
    factor = HEAD_DIM ** (-0.5)
    fill_rows(x_ref, tok_ref, me_ref[0] * images, images)
    normed, _ = normalize(x_ref[...])
    ln_one = (normed * gain_ref[...] + shift_ref[...]).astype(BF16)
    pick_ref[...] = gather_matrix()
    mask_ref[...] = head_mask(heads)
    slots = WINS * WPAD
    for image in range(images):
        win_ref[image * slots : (image + 1) * slots, :] = nn(
            pick_ref[...], ln_one[image * TPAD : (image + 1) * TPAD]
        ).astype(BF16)
    for group, (w_ref, b_ref) in enumerate(((wm_ref, qvbm_ref), (wo_ref, qvbo_ref))):
        cols = slice(group * chan, (group + 1) * chan)
        win = win_ref[...]
        q_ref[:, cols] = ((nn(win, w_ref[0]) + b_ref[0:1, :]) * factor).astype(BF16)
        k_ref[:, cols] = nn(win, w_ref[1]).astype(BF16)
        v_ref[:, cols] = (nn(win, w_ref[2]) + b_ref[1:2, :]).astype(BF16)

    def one_window(window, carry):
        rows = pl.ds(pl.multiple_of(window * WPAD, WPAD), WPAD)
        image = window // WINS
        local = pl.multiple_of((window - image * WINS) * WPAD, WPAD)
        ids_row = ids_ref[pl.ds(me_ref[0] * images + image, 1), :]
        allowed = window_mask(ids_row, pick_ref[pl.ds(local, WPAD), :])
        k_all = per_head(k_ref[rows, :], mask_ref[...], heads)
        v_all = per_head(v_ref[rows, :], mask_ref[...], heads)
        scores = nt(k_all, two_groups(q_ref[rows, :])) + bias_ref[...]
        scores = scores.reshape(heads, WPAD, 2 * WPAD) + allowed[None]
        top = jnp.max(scores, axis=1, keepdims=True)
        grown = jnp.exp(scores - top)
        total = jnp.sum(grown, axis=1, keepdims=True)
        lse_ref[window] = (top + jnp.log(total)).reshape(heads, 2 * WPAD)
        probs = (grown * (1.0 / total)).astype(BF16).reshape(heads * WPAD, 2 * WPAD)
        att_ref[rows, :] = own_groups(tn(probs, v_all)).astype(BF16)
        return carry

    lax.fori_loop(0, images * WINS, one_window, 0, unroll=2)
    back = scatter_matrix()
    for image in range(images):
        merged_ref[image * TPAD : (image + 1) * TPAD, :] = nn(
            back, att_ref[image * slots : (image + 1) * slots, :]
        ).astype(BF16)
    resid_ref[...] = (
        x_ref[...]
        + (nt(merged_ref[:, :chan], pm_ref[...]) + nt(merged_ref[:, chan:], po_ref[...]))
        + bproj_ref[...]
    )


def ffn_kernel(
    images,
    layouts,
    last,
    me_ref,
    resid_ref,
    cot_ref,
    gain_ref,
    shift_ref,
    w1_ref,
    w2_ref,
    b1_ref,
    *refs,
):
    if last:
        b2_ref, ln_ref, lnt_ref, cot_b_ref, cot_t_ref, ffn_in, gln_in = refs[:7]
        g1_ref, g2_ref, gb_ref, out_ref, half_ref, gres_ref, sums_ref = refs[7:14]
        ffn_ref, gln_ref = refs[14:]
    else:
        g1_ref, g2_ref, gb_ref = refs[:3]
        ln_ref, lnt_ref, cot_b_ref, cot_t_ref, ffn_ref, gln_ref = refs[3:]
    if last:
        ffn_ref[...] = ffn_in[...]
        gln_ref[...] = gln_in[...]
    else:
        normed, _ = normalize(resid_ref[...])
        ln_ref[...] = (normed * gain_ref[...] + shift_ref[...]).astype(BF16)
        fill_rows(cot_b_ref, cot_ref, me_ref[0] * images, images)
        width = ln_ref.shape[1]
        lnt_ref[...] = nt(order_matrix(width, layouts[0]), ln_ref[...]).astype(BF16)
        cot_t_ref[...] = nt(order_matrix(width, layouts[1]), cot_b_ref[...]).astype(BF16)
        ffn_ref[...] = jnp.zeros(ffn_ref.shape, F32)
        gln_ref[...] = jnp.zeros(gln_ref.shape, F32)
    chunk = 256

    def one_chunk(at, carry):
        cols = pl.ds(pl.multiple_of(at * chunk, chunk), chunk)
        pre = nn(ln_ref[...], w1_ref[:, cols]) + b1_ref[:, cols]
        phi = 0.5 * (1.0 + lax.erf(pre * 0.7071067811865476))
        act = (pre * phi).astype(BF16)
        slope = phi + pre * jnp.exp(-0.5 * pre * pre) * 0.3989422804014327
        grad_pre = nn(cot_b_ref[...], w2_ref[:, cols]) * slope
        gb_ref[:, cols] = jnp.sum(grad_pre, axis=0, keepdims=True)
        grad_pre = grad_pre.astype(BF16)
        ffn_ref[...] += nt(act, w2_ref[:, cols])
        gln_ref[...] += nt(grad_pre, w1_ref[:, cols])
        g2_ref[:, cols] = nn(cot_t_ref[...], act).astype(BF16)
        g1_ref[:, cols] = nn(lnt_ref[...], grad_pre).astype(BF16)
        return carry

    lax.fori_loop(0, w1_ref.shape[1] // chunk, one_chunk, 0, unroll=True)
    if not last:
        return
    resid = resid_ref[...]
    result = (resid + ffn_ref[...] + b2_ref[...]).astype(BF16)
    for image in range(images):
        piece = result[image * TPAD : image * TPAD + TOK]
        out_ref[me_ref[0] * images + image] = piece
        half_ref[image] = piece
    normed, inverse = normalize(resid)
    upstream = gln_ref[...]
    cot = cot_b_ref[...].astype(F32)
    grad_resid = cot + norm_back(upstream, normed, inverse, gain_ref[...])
    gres_ref[...] = grad_resid
    sums_ref[0:1, :] = jnp.sum(grad_resid, axis=0, keepdims=True)
    sums_ref[1:2, :] = jnp.sum(upstream * normed, axis=0, keepdims=True)
    sums_ref[2:3, :] = jnp.sum(upstream, axis=0, keepdims=True)
    sums_ref[3:4, :] = jnp.sum(cot, axis=0, keepdims=True)
    sums_ref[4:8, :] = jnp.zeros((4, sums_ref.shape[1]), F32)


def attend_back_kernel(
    images,
    heads,
    layouts,
    me_ref,
    gres_ref,
    ids_ref,
    merged_ref,
    pm_ref,
    po_ref,
    q_ref,
    k_ref,
    v_ref,
    win_ref,
    lse_ref,
    bias_ref,
    gqkm_ref,
    gqko_ref,
    gvpm_ref,
    gvpo_ref,
    gqkv_ref,
    sums_ref,
    gbias_ref,
    pick_ref,
    gatt_ref,
    mask_ref,
    qsum_ref,
    vsum_ref,
):
    chan = heads * HEAD_DIM
    wide = 2 * chan
    factor = HEAD_DIM ** (-0.5)
    slots = WINS * WPAD
    pick_ref[...] = gather_matrix()
    mask_ref[...] = head_mask(heads)
    gres = gres_ref[...]
    gres_b = gres.astype(BF16)
    put_rows(gvpm_ref, layouts[1], chan, tn(gres_b, merged_ref[:, :chan]))
    put_rows(gvpo_ref, layouts[1], chan, tn(gres_b, merged_ref[:, chan:]))
    grad_m = jnp.concatenate(
        [nn(gres_b, pm_ref[...]).astype(BF16), nn(gres_b, po_ref[...]).astype(BF16)], axis=1
    )
    for image in range(images):
        gatt_ref[image * slots : (image + 1) * slots, :] = nn(
            pick_ref[...], grad_m[image * TPAD : (image + 1) * TPAD]
        ).astype(BF16)
    gbias_ref[...] = jnp.zeros(gbias_ref.shape, F32)
    qsum_ref[...] = jnp.zeros(qsum_ref.shape, F32)
    vsum_ref[...] = jnp.zeros(vsum_ref.shape, F32)

    def one_window(window, carry):
        rows = pl.ds(pl.multiple_of(window * WPAD, WPAD), WPAD)
        image = window // WINS
        local = pl.multiple_of((window - image * WINS) * WPAD, WPAD)
        ids_row = ids_ref[pl.ds(me_ref[0] * images + image, 1), :]
        allowed = window_mask(ids_row, pick_ref[pl.ds(local, WPAD), :])
        mask = mask_ref[...]
        k_all = per_head(k_ref[rows, :], mask, heads)
        v_all = per_head(v_ref[rows, :], mask, heads)
        q_two = two_groups(q_ref[rows, :])
        g_two = two_groups(gatt_ref[rows, :])
        scores = nt(k_all, q_two) + bias_ref[...]
        scores = scores.reshape(heads, WPAD, 2 * WPAD) + allowed[None]
        probs = jnp.exp(scores - lse_ref[window].reshape(heads, 1, 2 * WPAD))
        g_probs = nt(v_all, g_two).reshape(heads, WPAD, 2 * WPAD)
        inner = jnp.sum(probs * g_probs, axis=1, keepdims=True)
        g_scores = (probs * (g_probs - inner)).reshape(heads * WPAD, 2 * WPAD)
        gbias_ref[...] += g_scores
        probs_b = probs.astype(BF16).reshape(heads * WPAD, 2 * WPAD)
        g_scores = g_scores.astype(BF16)

        def fold(product):
            return jnp.sum((product * mask.astype(F32)).reshape(heads, WPAD, wide), axis=0)

        g_v = fold(nn(probs_b, g_two))
        g_k = fold(nn(g_scores, q_two))
        g_q = own_groups(tn(g_scores, k_all)) * factor
        qsum_ref[...] += g_q
        vsum_ref[...] += g_v
        for group in range(2):
            cols = slice(group * chan, (group + 1) * chan)
            base = group * 3 * chan
            gqkv_ref[rows, base : base + chan] = g_q[:, cols].astype(BF16)
            gqkv_ref[rows, base + chan : base + 2 * chan] = g_k[:, cols].astype(BF16)
            gqkv_ref[rows, base + 2 * chan : base + 3 * chan] = g_v[:, cols].astype(BF16)
        return carry

    lax.fori_loop(0, images * WINS, one_window, 0, unroll=2)
    sums_ref[...] = jnp.zeros(sums_ref.shape, F32)
    sums_ref[0:1, :] = jnp.sum(qsum_ref[...], axis=0, keepdims=True)
    sums_ref[1:2, :] = jnp.sum(vsum_ref[...], axis=0, keepdims=True)
    win = win_ref[...]
    put_rows(gqko_ref, layouts[0], 0, tn(win, gqkv_ref[:, 3 * chan : 5 * chan]))
    put_rows(gvpo_ref, layouts[1], 0, tn(win, gqkv_ref[:, 5 * chan :]))
    put_rows(gqkm_ref, layouts[0], 0, tn(win, gqkv_ref[:, : 2 * chan]))
    put_rows(gvpm_ref, layouts[1], 0, tn(win, gqkv_ref[:, 2 * chan : 3 * chan]))


def last_kernel(
    images,
    heads,
    rows_half,
    me_ref,
    tok_ref,
    gres_ref,
    gqkv_ref,
    wm_ref,
    wo_ref,
    gain_ref,
    gbias_ref,
    two_ref,
    qv_ref,
    gbm_ref,
    gbo_ref,
    full_ref,
    half_ref,
    mine_ref,
    theirs_ref,
    x_ref,
    off_ref,
    acc_ref,
):
    chan = heads * HEAD_DIM
    slots = WINS * WPAD
    grad_win = nt(gqkv_ref[:, :chan], wm_ref[0])
    for at in range(1, 6):
        w_ref = wm_ref if at < 3 else wo_ref
        grad_win += nt(gqkv_ref[:, at * chan : (at + 1) * chan], w_ref[at % 3])
    high = grad_win.astype(BF16)
    low = (grad_win - high.astype(F32)).astype(BF16)
    back = scatter_matrix()
    upstream = jnp.concatenate(
        [
            nn(back, high[image * slots : (image + 1) * slots])
            + nn(back, low[image * slots : (image + 1) * slots])
            for image in range(images)
        ],
        axis=0,
    )
    fill_rows(x_ref, tok_ref, me_ref[0] * images, images)
    normed, inverse = normalize(x_ref[...])
    grad_in = gres_ref[...] + norm_back(upstream, normed, inverse, gain_ref[...])
    for image in range(images):
        piece = grad_in[image * TPAD : image * TPAD + TOK]
        full_ref[me_ref[0] * images + image] = piece
        half_ref[image] = piece
    width = upstream.shape[1]
    gain_sum = jnp.sum(upstream * normed, axis=0, keepdims=True)
    shift_sum = jnp.sum(upstream, axis=0, keepdims=True)
    off_ref[...] = table_offsets(rows_half)
    acc_ref[...] = jnp.zeros(acc_ref.shape, F32)
    for key in range(WTOK):
        pick = jnp.where(off_ref[...] == key_offset(key), 1.0, 0.0).astype(BF16)
        rows = gbias_ref[pl.ds(key, heads, stride=WPAD), :]
        top = rows.astype(BF16).astype(F32)
        parts = jnp.concatenate([top, rows - top], axis=0).astype(BF16)
        acc_ref[...] += nt(parts, pick)
    table = acc_ref[:heads] + acc_ref[heads:]
    for group, (pack_ref, gb_ref) in enumerate(((mine_ref, gbm_ref), (theirs_ref, gbo_ref))):
        pack_ref[...] = jnp.zeros(pack_ref.shape, F32)
        pack_ref[0:4, :] = two_ref[0:4, :]
        pack_ref[4:5, :] = gain_sum
        pack_ref[5:6, :] = shift_sum
        pack_ref[6:7, :chan] = qv_ref[0:1, group * chan : (group + 1) * chan]
        pack_ref[6:7, chan:] = qv_ref[1:2, group * chan : (group + 1) * chan]
        for at in range(gb_ref.shape[1] // width):
            pack_ref[7 + at : 8 + at, :] = gb_ref[:, at * width : (at + 1) * width]
        half = table[:, group * rows_half : (group + 1) * rows_half]
        low = pack_ref.shape[0] - heads // 2
        pack_ref[low:, :rows_half] = half[: heads // 2]
        pack_ref[low:, chan : chan + rows_half] = half[heads // 2 :]


def unpack_kernel(parts, sel_ref, *refs):
    ins, outs = refs[:parts], refs[parts:]
    if parts == 2:
        total = ins[0][...] + ins[1][...]
    else:
        total = (ins[0][...] + ins[1][...]) + (ins[2][...] + ins[3][...])
    for at in range(6):
        outs[at][...] = total[at : at + 1]
    qv_ref, b1_ref, table_ref = outs[6:]
    chan, (heads, entries) = qv_ref.shape[1], table_ref.shape
    qv_ref[0:1, :] = total[6:7, :chan]
    qv_ref[1:2, :] = total[6:7, chan:]
    width = total.shape[1]
    for at in range(b1_ref.shape[1] // width):
        b1_ref[:, at * width : (at + 1) * width] = total[7 + at : 8 + at]
    low = total.shape[0] - heads // 2
    table_ref[: heads // 2, :] = total[low:, :entries]
    table_ref[heads // 2 :, :] = total[low:, chan : chan + entries]


def row_block(ref, sel_ref, blocks, form):
    index = form[0]
    for at, factor in enumerate(form[1:]):
        if factor:
            index = index + factor * sel_ref[at]
    rows = ref.shape[0] // blocks
    if blocks == 1:
        return ref[...].astype(F32)
    return ref[pl.ds(pl.multiple_of(index * rows, rows), rows), :].astype(F32)


def sum_kernel(groups, sel_ref, *refs):
    at, outs = 0, refs[sum(len(g) for g in groups) :]
    for picks, out_ref in zip(groups, outs):
        total = row_block(refs[at], sel_ref, *picks[0])
        for more in range(1, len(picks)):
            total = total + row_block(refs[at + more], sel_ref, *picks[more])
        out_ref[...] = total.astype(out_ref.dtype)
        at += len(picks)


def fan_kernel(groups, rows, sends, sel_ref, *refs):
    flat = sum(len(g) for g in groups)
    outs, total_ref, at, col = refs[flat:-1], refs[-1], 0, 0
    for picks in groups:
        total = row_block(refs[at], sel_ref, *picks[0])
        for more in range(1, len(picks)):
            total = total + row_block(refs[at + more], sel_ref, *picks[more])
        total_ref[:, col : col + total.shape[1]] = total
        col += total.shape[1]
        at += len(picks)
    own = sel_ref[3]
    for s in range(1, sends + 1):
        piece = total_ref[pl.ds(pl.multiple_of((own ^ s) * rows, rows), rows), :]
        outs[s - 1][...] = piece.astype(BF16)
    outs[sends][...] = total_ref[pl.ds(pl.multiple_of(own * rows, rows), rows), :]


def total_kernel(sel_ref, own_ref, *refs):
    ins, (a_ref, b_ref) = refs[:-2], refs[-2:]
    total = own_ref[...]
    for in_ref in ins:
        total = total + in_ref[...].astype(F32)
    a_ref[...] = total[:, : a_ref.shape[1]]
    b_ref[...] = total[:, a_ref.shape[1] :]


def pair_kernel(sel_ref, a_ref, b_ref, out_ref):
    out_ref[...] = a_ref[...] + b_ref[...]


def four_kernel(sel_ref, a_ref, b_ref, c_ref, d_ref, out_ref):
    out_ref[...] = (a_ref[...] + b_ref[...]) + (c_ref[...] + d_ref[...])


def struct(shape, kind):
    return jax.ShapeDtypeStruct(shape, kind)


def call(kernel, scalars, inputs, outs, scratch, flops, limit_mib):
    moved = sum(a.size * a.dtype.itemsize for a in inputs)
    moved += sum(a.size * a.dtype.itemsize for a in outs)
    vmem = pl.BlockSpec(memory_space=pltpu.VMEM)
    return pl.pallas_call(
        kernel,
        in_specs=[pl.BlockSpec(memory_space=pltpu.SMEM)] + [vmem] * len(inputs),
        out_specs=[vmem] * len(outs),
        out_shape=outs,
        scratch_shapes=scratch,
        compiler_params=pltpu.CompilerParams(vmem_limit_bytes=limit_mib << 20),
        cost_estimate=pl.CostEstimate(flops=flops, bytes_accessed=moved, transcendentals=0),
    )(scalars, *inputs)


def digits_of(count):
    digits, stride = [], 1
    for size in (2, 2):
        if (count // stride) % size == 0 and count // stride > 1:
            digits.append((stride, size))
            stride *= size
    while count // stride > 1:
        size = 4 if (count // stride) % 4 == 0 else 2
        digits.append((stride, size))
        stride *= size
    return digits


def xor_exchange(value, axis, count, mask):
    return lax.ppermute(value, axis, [(i, i ^ mask) for i in range(count)])


def scatter_sum(addends, axis, count, digits, order):
    index = lax.axis_index(axis)
    rows, cols = addends[0].shape
    shape = [size for _, size in reversed(digits)] + [rows // count, cols]
    addends = [a.reshape(shape) for a in addends]
    left = list(reversed(range(len(digits))))
    for digit in order:
        stride, size = digits[digit]
        place = left.index(digit)
        mine = (index // stride) % size

        def part(which):
            return [lax.dynamic_index_in_dim(a, which, place, keepdims=False) for a in addends]

        def total(pieces):
            result = pieces[0].astype(F32)
            for piece in pieces[1:]:
                result = result + piece.astype(F32)
            return result

        received = [
            xor_exchange(total(part(mine ^ s)).astype(BF16), axis, count, s * stride)
            for s in range(1, size)
        ]
        addends = part(mine) + received
        left.remove(digit)
    return total(addends)


def all_sum(sel, value, axis, count):
    mask = 1
    while True:
        size = 4 if 4 * mask <= count else 2
        terms = [value]
        for s in range(1, size):
            terms.append(xor_exchange(value, axis, count, s * mask))
        mask *= size
        if mask >= count:
            return terms
        kernel = four_kernel if size == 4 else pair_kernel
        (value,) = call(kernel, sel, terms, [struct(value.shape, F32)], [], 10**5, 2)


def add_blocks(sel, groups, kind):
    flat = [item for group in groups for item in group]
    outs = [
        struct((group[0][0].shape[0] // group[0][1], group[0][0].shape[1]), kind)
        for group in groups
    ]
    picks = tuple(tuple((blocks, form) for _, blocks, form in group) for group in groups)
    return call(
        functools.partial(sum_kernel, picks), sel, [a for a, _, _ in flat], outs, [], 10**6, 4
    )


def scatter_pairs(sel, pair_a, pair_b, axis, count, digits):
    (stride_x, _), (stride_y, _), (stride_z, size_z) = digits
    (a0, a1), (b0, b1) = pair_a, pair_b
    not_x, not_y = (1, 0, -1, 0, 0), (1, 0, 0, -1, 0)
    send_a, send_b = add_blocks(
        sel, [[(a0, 2, not_x), (a1, 2, not_x)], [(b0, 2, not_y), (b1, 2, not_y)]], BF16
    )
    got_a = xor_exchange(send_a, axis, count, stride_x)
    got_b = xor_exchange(send_b, axis, count, stride_y)
    at_a, at_b = (1, 0, 2, -1, 0), (1, 0, -1, 2, 0)
    send_a, send_b = add_blocks(
        sel,
        [
            [(a0, 4, at_a), (a1, 4, at_a), (got_a, 2, not_y)],
            [(b0, 4, at_b), (b1, 4, at_b), (got_b, 2, not_x)],
        ],
        BF16,
    )
    more_a = xor_exchange(send_a, axis, count, stride_y)
    more_b = xor_exchange(send_b, axis, count, stride_x)
    groups = (
        (
            (4, (0, 0, 2, 1, 0)),
            (4, (0, 0, 2, 1, 0)),
            (2, (0, 0, 0, 1, 0)),
            (1, (0, 0, 0, 0, 0)),
        ),
        (
            (4, (0, 0, 1, 2, 0)),
            (4, (0, 0, 1, 2, 0)),
            (2, (0, 0, 1, 0, 0)),
            (1, (0, 0, 0, 0, 0)),
        ),
    )
    cols = a0.shape[1] + b0.shape[1]
    deep = a0.shape[0] // 4
    rows = deep // size_z
    outs = (struct((rows, cols), BF16),) * (size_z - 1) + (struct((rows, cols), F32),)
    *sends, own = call(
        functools.partial(fan_kernel, groups, rows, size_z - 1),
        sel,
        [a0, a1, got_a, more_a, b0, b1, got_b, more_b],
        outs,
        [pltpu.VMEM((deep, cols), F32)],
        10**6,
        6,
    )
    received = []
    for s, send in enumerate(sends, 1):
        received.append(xor_exchange(send, axis, count, s * stride_z))
    half = a0.shape[1]
    outs = (struct((rows, half), F32), struct((rows, cols - half), F32))
    return call(total_kernel, sel, [own] + received, outs, [], 10**6, 4)


def per_device(n_dp, n_tensor, *args):
    return block(n_dp, n_tensor, *args)


def block(
    n_dp,
    n_tensor,
    tokens,
    region_ids,
    norm1_gain,
    norm1_bias,
    w_qkv,
    qv_bias,
    rel_table,
    w_proj,
    b_proj,
    norm2_gain,
    norm2_bias,
    w_fc1,
    b_fc1,
    w_fc2,
    b_fc2,
    cotangent,
):
    all_images, _, width = tokens.shape
    images = all_images // n_tensor
    entries, heads = rel_table.shape
    chan = heads * HEAD_DIM
    hidden = w_fc1.shape[1]
    rows_t = images * TPAD
    rows_w = images * WINS * WPAD
    half_rows = -(-entries // 16) * 16
    digits = digits_of(n_dp)
    by_pairs = [size for _, size in digits] == [2, 2, 4] and width // n_dp % 16 == 0
    order_a = list(range(len(digits)))
    order_b = order_a[1:2] + order_a[:1] + order_a[2:]
    plain = order_a[::-1]
    layouts = tuple(
        (width // n_dp, digits, order if by_pairs else plain) for order in (order_a, order_b)
    )
    me = lax.axis_index("tensor")
    spot = lax.axis_index("dp")
    places = [(spot // stride) % size for stride, size in digits[:3]]
    me_arr = sel = jnp.stack([me] + places).astype(jnp.int32)

    def swap(value):
        return lax.ppermute(value, "tensor", [(i, i ^ 1) for i in range(n_tensor)])

    wm = w_qkv.transpose(1, 0, 2)
    wo = swap(wm)
    table_m = rel_table.T
    table_o = swap(table_m)
    qvb_o = swap(qv_bias)
    po = swap(w_proj)
    b1_o = swap(b_fc1.reshape(1, hidden))
    w1o = swap(w_fc1)
    w2o = swap(w_fc2)

    row = lambda vec: vec.reshape(1, -1)

    bias_shape = struct((heads * WPAD, 2 * WPAD), F32)
    (bias,) = call(
        functools.partial(bias_kernel, heads, half_rows),
        sel,
        [table_m, table_o],
        [bias_shape],
        [
            pltpu.VMEM((2 * half_rows, 2 * WPAD), jnp.int32),
            pltpu.VMEM((heads, 2 * half_rows), F32),
        ],
        10**9,
        4,
    )

    ins = (
        tokens,
        region_ids,
        row(norm1_gain),
        row(norm1_bias),
        wm,
        wo,
        qv_bias,
        qvb_o,
        bias,
        w_proj,
        po,
        row(b_proj),
    )
    outs = (
        struct((rows_w, 2 * chan), BF16),
        struct((rows_w, 2 * chan), BF16),
        struct((rows_w, 2 * chan), BF16),
        struct((rows_w, width), BF16),
        struct((images * WINS, heads, 2 * WPAD), F32),
        struct((rows_t, 2 * chan), BF16),
        struct((rows_t, width), F32),
    )
    q, k, v, win_in, lse, merged, resid = call(
        functools.partial(attend_kernel, images, heads),
        me_arr,
        ins,
        outs,
        [
            pltpu.VMEM((rows_t, width), F32),
            pltpu.VMEM((WINS * WPAD, TPAD), BF16),
            pltpu.VMEM((rows_w, 2 * chan), BF16),
            pltpu.VMEM((heads * WPAD, 2 * chan), BF16),
        ],
        3 * 10**9,
        LIMIT,
    )

    weight_grad = struct((width, hidden), BF16)
    acc = struct((rows_t, width), F32)
    kept = (
        struct((rows_t, width), BF16),
        struct((width, rows_t), BF16),
        struct((rows_t, width), BF16),
        struct((width, rows_t), BF16),
        acc,
        acc,
    )
    common = (resid, cotangent, row(norm2_gain), row(norm2_bias))
    ins = common + (w1o, w2o, b1_o)
    outs = (weight_grad, weight_grad, struct((1, hidden), F32)) + kept
    g1o, g2o, gbo, *carried = call(
        functools.partial(ffn_kernel, images, layouts, False),
        me_arr,
        ins,
        outs,
        [],
        3 * 10**9,
        LIMIT,
    )
    got1 = swap(g1o)
    got2 = swap(g2o)
    ins = common + (w_fc1, w_fc2, row(b_fc1), row(b_fc2), *carried)
    outs = (
        weight_grad,
        weight_grad,
        struct((1, hidden), F32),
        struct(tokens.shape, BF16),
        struct((images, TOK, width), BF16),
        acc,
        struct((8, width), F32),
    )
    g1m, g2m, gbm, out_full, out_half, gres, sums_two = call(
        functools.partial(ffn_kernel, images, layouts, True),
        me_arr,
        ins,
        outs,
        [pltpu.VMEM((rows_t, width), F32), pltpu.VMEM((rows_t, width), F32)],
        3 * 10**9,
        LIMIT,
    )

    def scatter(pair_a, pair_b):
        if by_pairs:
            return scatter_pairs(sel, pair_a, pair_b, "dp", n_dp, digits)
        return (
            scatter_sum(pair_a, "dp", n_dp, digits, order_a),
            scatter_sum(pair_b, "dp", n_dp, digits, order_b),
        )

    sent_fc1, sent_fc2 = scatter((g1m, got1), (g2m, got2))
    out_other = swap(out_half)
    output = lax.dynamic_update_slice_in_dim(out_full, out_other, (1 - me) * images, 0)

    ins = (gres, region_ids, merged, w_proj, po, q, k, v, win_in, lse, bias)
    outs = (
        struct((width, 2 * chan), BF16),
        struct((width, 2 * chan), BF16),
        struct((width, 2 * chan), BF16),
        struct((width, 2 * chan), BF16),
        struct((rows_w, 6 * chan), BF16),
        struct((8, 2 * chan), F32),
        bias_shape,
    )
    gqkm, gqko, gvpm, gvpo, gqkv, sums_qv, gbias = call(
        functools.partial(attend_back_kernel, images, heads, layouts),
        me_arr,
        ins,
        outs,
        [
            pltpu.VMEM((WINS * WPAD, TPAD), BF16),
            pltpu.VMEM((rows_w, 2 * chan), BF16),
            pltpu.VMEM((heads * WPAD, 2 * chan), BF16),
            pltpu.VMEM((WPAD, 2 * chan), F32),
            pltpu.VMEM((WPAD, 2 * chan), F32),
        ],
        5 * 10**9,
        LIMIT,
    )

    got_qk = swap(gqko)
    got_vp = swap(gvpo)
    sent_qk, sent_vp = scatter((gqkm, got_qk), (gvpm, got_vp))
    sent_qkv = jnp.stack(
        [sent_qk[:, :chan], sent_qk[:, chan:], sent_vp[:, :chan]], axis=0
    ).transpose(1, 0, 2)
    sent_proj = sent_vp[:, chan:]

    ins = (tokens, gres, gqkv, wm, wo, row(norm1_gain), gbias, sums_two, sums_qv, gbm, gbo)
    pack = struct((-(-(7 + hidden // width + heads // 2) // 8) * 8, width), F32)
    outs = (struct(tokens.shape, F32), struct((images, TOK, width), F32), pack, pack)
    grad_full, grad_half, small, theirs = call(
        functools.partial(last_kernel, images, heads, half_rows),
        me_arr,
        ins,
        outs,
        [
            pltpu.VMEM((rows_t, width), F32),
            pltpu.VMEM((2 * half_rows, 2 * WPAD), jnp.int32),
            pltpu.VMEM((2 * heads, 2 * half_rows), F32),
        ],
        2 * 10**9,
        LIMIT,
    )
    grad_in = lax.dynamic_update_slice_in_dim(grad_full, swap(grad_half), (1 - me) * images, 0)

    got = swap(theirs)
    (small,) = call(pair_kernel, sel, [small, got], [struct(small.shape, F32)], [], 10**5, 2)
    terms = all_sum(sel, small, "dp", n_dp)
    outs = (struct((1, width), F32),) * 6 + (
        struct((2, chan), F32),
        struct((1, hidden), F32),
        struct((heads, entries), F32),
    )
    *vectors, sum_qv, sum_b1, sum_table = call(
        functools.partial(unpack_kernel, len(terms)), sel, terms, outs, [], 10**5, 2
    )
    vectors = [vec.reshape(width) for vec in vectors]
    return (
        output,
        grad_in,
        vectors[4],
        vectors[5],
        sent_qkv,
        sum_qv,
        sum_table.T,
        sent_proj,
        vectors[0],
        vectors[1],
        vectors[2],
        sent_fc1,
        sum_b1.reshape(hidden),
        sent_fc2,
        vectors[3],
    )


def solution(mesh):
    return jax.shard_map(
        functools.partial(per_device, mesh.shape["dp"], mesh.shape["tensor"]),
        mesh=mesh,
        in_specs=(
            P("dp", None, None),
            P("dp", None),
            P(),
            P(),
            P(None, None, "tensor"),
            P(None, "tensor"),
            P(None, "tensor"),
            P(None, "tensor"),
            P(),
            P(),
            P(),
            P(None, "tensor"),
            P("tensor"),
            P(None, "tensor"),
            P(),
            P("dp", None, None),
        ),
        out_specs=(
            P("dp", None, None),
            P("dp", None, None),
            P(),
            P(),
            P("dp", None, "tensor"),
            P(None, "tensor"),
            P(None, "tensor"),
            P("dp", "tensor"),
            P(),
            P(),
            P(),
            P("dp", "tensor"),
            P("tensor"),
            P("dp", "tensor"),
            P(),
        ),
        check_vma=False,
    )
```

```python
import functools

import jax
import jax.numpy as jnp
from jax import lax
from jax.experimental import pallas as pl
from jax.experimental.pallas import tpu as pltpu
from jax.sharding import PartitionSpec as P


HEAD_DIM = 32
SIDE = 14
WIN = 7
SHIFT = 3
NORM_EPS = 1e-05

TOK = SIDE * SIDE
TPAD = 208
WTOK = WIN * WIN
WPAD = 64
BLOCKS = SIDE // WIN
WINS = BLOCKS * BLOCKS
F32 = jnp.float32
BF16 = jnp.bfloat16
LIMIT = 16


def nn(a, b):
    return lax.dot_general(a, b, (((1,), (0,)), ((), ())), preferred_element_type=F32)


def nt(a, b):
    return lax.dot_general(a, b, (((1,), (1,)), ((), ())), preferred_element_type=F32)


def tn(a, b):
    return lax.dot_general(a, b, (((0,), (0,)), ((), ())), preferred_element_type=F32)


def iota(shape, axis):
    return lax.broadcasted_iota(jnp.int32, shape, axis)


def normalize(source):
    center = jnp.mean(source, axis=-1, keepdims=True)
    centred = source - center
    inverse = lax.rsqrt(jnp.mean(centred * centred, axis=-1, keepdims=True) + NORM_EPS)
    return centred * inverse, inverse


def norm_back(upstream, normed, inverse, gain_vec):
    scaled = upstream * gain_vec
    return inverse * (
        scaled
        - jnp.mean(scaled, axis=-1, keepdims=True)
        - normed * jnp.mean(scaled * normed, axis=-1, keepdims=True)
    )


def seventh(value):
    return (value * 37) >> 8


def window_source(slot):
    window, at = slot >> 6, slot & (WPAD - 1)
    row = (window >> 1) * WIN + seventh(at) + SHIFT
    col = (window & 1) * WIN + (at - seventh(at) * WIN) + SHIFT
    row = jnp.where(row >= SIDE, row - SIDE, row)
    col = jnp.where(col >= SIDE, col - SIDE, col)
    return jnp.where(at < WTOK, row * SIDE + col, -1)


def gather_matrix():
    shape = (WINS * WPAD, TPAD)
    hit = window_source(iota(shape, 0)) == iota(shape, 1)
    return jnp.where(hit, 1.0, 0.0).astype(BF16)


def scatter_matrix():
    shape = (TPAD, WINS * WPAD)
    hit = window_source(iota(shape, 1)) == iota(shape, 0)
    return jnp.where(hit, 1.0, 0.0).astype(BF16)


def head_mask(heads):
    shape = (heads * WPAD, 2 * heads * HEAD_DIM)
    hit = (iota(shape, 0) >> 6) == ((iota(shape, 1) & (heads * HEAD_DIM - 1)) >> 5)
    return jnp.where(hit, 1.0, 0.0).astype(BF16)


def log2(value):
    return value.bit_length() - 1


def row_order(slot, rows, digits, order):
    rest, block = slot >> log2(rows), 0
    for digit in reversed(order):
        stride, size = digits[digit]
        block = block + (rest & (size - 1)) * stride
        rest = rest >> log2(size)
    return block * rows + (slot & (rows - 1))


def put_rows(out_ref, layout, col, value):
    rows = layout[0]
    cols = slice(col, col + value.shape[1])
    value = value.astype(out_ref.dtype)
    sources = [row_order(at, *layout) for at in range(0, value.shape[0], rows)]
    if sources == sorted(sources):
        out_ref[:, cols] = value
        return
    for place, source in enumerate(sources):
        out_ref[place * rows : (place + 1) * rows, cols] = value[source : source + rows]


def order_matrix(width, layout):
    shape = (width, width)
    hit = row_order(iota(shape, 0), *layout) == iota(shape, 1)
    return jnp.where(hit, 1.0, 0.0).astype(BF16)


def fill_rows(rows_ref, block_ref, first, images):
    rows_ref[...] = jnp.zeros(rows_ref.shape, rows_ref.dtype)
    for image in range(images):
        rows_ref[image * TPAD : image * TPAD + TOK, :] = block_ref[first + image].astype(
            rows_ref.dtype
        )


def window_mask(ids_row, pick):
    ids_b = jnp.broadcast_to(ids_row.astype(F32), (2 * WPAD, TOK)).astype(BF16)
    pick = pick[:, :TOK]
    keys = nt(pick, ids_b)
    queries = nt(ids_b[:16], jnp.concatenate([pick, pick], axis=0))[0:1]
    shape = (WPAD, 2 * WPAD)
    key_at = iota(shape, 0)
    query_at = iota(shape, 1) & (WPAD - 1)
    same = jnp.logical_or(keys == queries, query_at >= WTOK)
    return jnp.where(jnp.logical_and(same, key_at < WTOK), 0.0, -jnp.inf)


def two_groups(rows):
    half = rows.shape[1] // 2
    zero = jnp.zeros((rows.shape[0], half), rows.dtype)
    return jnp.concatenate(
        [
            jnp.concatenate([rows[:, :half], zero], axis=1),
            jnp.concatenate([zero, rows[:, half:]], axis=1),
        ],
        axis=0,
    )


def own_groups(rows):
    half = rows.shape[1] // 2
    return jnp.concatenate([rows[:WPAD, :half], rows[WPAD:, half:]], axis=1)


def per_head(rows, mask, heads):
    return jnp.concatenate([rows] * heads, axis=0) * mask


def table_offsets(rows_half):
    shape = (2 * rows_half, 2 * WPAD)
    entry, query = iota(shape, 0), iota(shape, 1)
    group_e = jnp.where(entry >= rows_half, 1, 0)
    at = query & (WPAD - 1)
    place = seventh(at) * (2 * WIN - 1) + (at - seventh(at) * WIN)
    fits = jnp.logical_and(group_e == (query >> 6), at < WTOK)
    return jnp.where(fits, entry - group_e * rows_half - place, 4096)


def key_offset(key):
    row = key // WIN
    return 2 * WIN * (WIN - 1) - (row * (2 * WIN - 1) + key - row * WIN)


def bias_kernel(heads, rows_half, sel_ref, mine_ref, other_ref, bias_ref, off_ref, table_ref):
    off_ref[...] = table_offsets(rows_half)
    bias_ref[...] = jnp.zeros(bias_ref.shape, F32)
    entries = mine_ref.shape[1]
    table_ref[...] = jnp.zeros(table_ref.shape, F32)
    table_ref[:, :entries] = mine_ref[...]
    table_ref[:, rows_half : rows_half + entries] = other_ref[...]
    table = table_ref[...]
    part_a = table.astype(BF16).astype(F32)
    part_b = (table - part_a).astype(BF16).astype(F32)
    part_c = table - part_a - part_b
    parts = jnp.concatenate([part_a, part_b, part_c], axis=0).astype(BF16)
    for key in range(WTOK):
        pick = jnp.where(off_ref[...] == key_offset(key), 1.0, 0.0).astype(BF16)
        rows = nn(parts, pick)
        bias_ref[pl.ds(key, heads, stride=WPAD), :] = (
            rows[:heads] + rows[heads : 2 * heads] + rows[2 * heads :]
        )


def attend_kernel(
    images,
    heads,
    me_ref,
    tok_ref,
    ids_ref,
    gain_ref,
    shift_ref,
    wm_ref,
    wo_ref,
    qvbm_ref,
    qvbo_ref,
    bias_ref,
    pm_ref,
    po_ref,
    bproj_ref,
    q_ref,
    k_ref,
    v_ref,
    win_ref,
    lse_ref,
    merged_ref,
    resid_ref,
    x_ref,
    pick_ref,
    att_ref,
    mask_ref,
):
    chan = heads * HEAD_DIM
    factor = HEAD_DIM ** (-0.5)
    fill_rows(x_ref, tok_ref, me_ref[0] * images, images)
    normed, _ = normalize(x_ref[...])
    ln_one = (normed * gain_ref[...] + shift_ref[...]).astype(BF16)
    pick_ref[...] = gather_matrix()
    mask_ref[...] = head_mask(heads)
    slots = WINS * WPAD
    for image in range(images):
        win_ref[image * slots : (image + 1) * slots, :] = nn(
            pick_ref[...], ln_one[image * TPAD : (image + 1) * TPAD]
        ).astype(BF16)
    for group, (w_ref, b_ref) in enumerate(((wm_ref, qvbm_ref), (wo_ref, qvbo_ref))):
        cols = slice(group * chan, (group + 1) * chan)
        win = win_ref[...]
        q_ref[:, cols] = ((nn(win, w_ref[0]) + b_ref[0:1, :]) * factor).astype(BF16)
        k_ref[:, cols] = nn(win, w_ref[1]).astype(BF16)
        v_ref[:, cols] = (nn(win, w_ref[2]) + b_ref[1:2, :]).astype(BF16)

    def one_window(window, carry):
        rows = pl.ds(pl.multiple_of(window * WPAD, WPAD), WPAD)
        image = window // WINS
        local = pl.multiple_of((window - image * WINS) * WPAD, WPAD)
        ids_row = ids_ref[pl.ds(me_ref[0] * images + image, 1), :]
        allowed = window_mask(ids_row, pick_ref[pl.ds(local, WPAD), :])
        k_all = per_head(k_ref[rows, :], mask_ref[...], heads)
        v_all = per_head(v_ref[rows, :], mask_ref[...], heads)
        scores = nt(k_all, two_groups(q_ref[rows, :])) + bias_ref[...]
        scores = scores.reshape(heads, WPAD, 2 * WPAD) + allowed[None]
        top = jnp.max(scores, axis=1, keepdims=True)
        grown = jnp.exp(scores - top)
        total = jnp.sum(grown, axis=1, keepdims=True)
        lse_ref[window] = (top + jnp.log(total)).reshape(heads, 2 * WPAD)
        probs = (grown * (1.0 / total)).astype(BF16).reshape(heads * WPAD, 2 * WPAD)
        att_ref[rows, :] = own_groups(tn(probs, v_all)).astype(BF16)
        return carry

    lax.fori_loop(0, images * WINS, one_window, 0, unroll=2)
    back = scatter_matrix()
    for image in range(images):
        merged_ref[image * TPAD : (image + 1) * TPAD, :] = nn(
            back, att_ref[image * slots : (image + 1) * slots, :]
        ).astype(BF16)
    resid_ref[...] = (
        x_ref[...]
        + (nt(merged_ref[:, :chan], pm_ref[...]) + nt(merged_ref[:, chan:], po_ref[...]))
        + bproj_ref[...]
    )


def ffn_kernel(
    images,
    layout,
    last,
    me_ref,
    resid_ref,
    cot_ref,
    gain_ref,
    shift_ref,
    w1_ref,
    w2_ref,
    b1_ref,
    *refs,
):
    if last:
        b2_ref, ln_ref, lnt_ref, cot_b_ref, cot_t_ref, ffn_in, gln_in = refs[:7]
        g1_ref, g2_ref, gb_ref, half_ref, gres_ref, sums_ref = refs[7:13]
        ffn_ref, gln_ref = refs[13:]
    else:
        g1_ref, g2_ref, gb_ref = refs[:3]
        ln_ref, lnt_ref, cot_b_ref, cot_t_ref, ffn_ref, gln_ref = refs[3:]
    if last:
        ffn_ref[...] = ffn_in[...]
        gln_ref[...] = gln_in[...]
    else:
        normed, _ = normalize(resid_ref[...])
        ln_ref[...] = (normed * gain_ref[...] + shift_ref[...]).astype(BF16)
        fill_rows(cot_b_ref, cot_ref, me_ref[0] * images, images)
        width = ln_ref.shape[1]
        order = order_matrix(width, layout)
        lnt_ref[...] = nt(order, ln_ref[...]).astype(BF16)
        cot_t_ref[...] = nt(order, cot_b_ref[...]).astype(BF16)
        ffn_ref[...] = jnp.zeros(ffn_ref.shape, F32)
        gln_ref[...] = jnp.zeros(gln_ref.shape, F32)
    chunk = 256

    def one_chunk(at, carry):
        cols = pl.ds(pl.multiple_of(at * chunk, chunk), chunk)
        pre = nn(ln_ref[...], w1_ref[:, cols]) + b1_ref[:, cols]
        phi = 0.5 * (1.0 + lax.erf(pre * 0.7071067811865476))
        act = (pre * phi).astype(BF16)
        slope = phi + pre * jnp.exp(-0.5 * pre * pre) * 0.3989422804014327
        grad_pre = nn(cot_b_ref[...], w2_ref[:, cols]) * slope
        gb_ref[:, cols] = jnp.sum(grad_pre, axis=0, keepdims=True)
        grad_pre = grad_pre.astype(BF16)
        ffn_ref[...] += nt(act, w2_ref[:, cols])
        gln_ref[...] += nt(grad_pre, w1_ref[:, cols])
        g2_ref[:, cols] = nn(cot_t_ref[...], act).astype(BF16)
        g1_ref[:, cols] = nn(lnt_ref[...], grad_pre).astype(BF16)
        return carry

    lax.fori_loop(0, w1_ref.shape[1] // chunk, one_chunk, 0, unroll=True)
    if not last:
        return
    resid = resid_ref[...]
    result = (resid + ffn_ref[...] + b2_ref[...]).astype(BF16)
    for image in range(images):
        half_ref[image] = result[image * TPAD : image * TPAD + TOK]
    normed, inverse = normalize(resid)
    upstream = gln_ref[...]
    cot = cot_b_ref[...].astype(F32)
    grad_resid = cot + norm_back(upstream, normed, inverse, gain_ref[...])
    gres_ref[...] = grad_resid
    sums_ref[0:1, :] = jnp.sum(grad_resid, axis=0, keepdims=True)
    sums_ref[1:2, :] = jnp.sum(upstream * normed, axis=0, keepdims=True)
    sums_ref[2:3, :] = jnp.sum(upstream, axis=0, keepdims=True)
    sums_ref[3:4, :] = jnp.sum(cot, axis=0, keepdims=True)
    sums_ref[4:8, :] = jnp.zeros((4, sums_ref.shape[1]), F32)


def attend_back_kernel(
    images,
    heads,
    layout,
    me_ref,
    gres_ref,
    ids_ref,
    merged_ref,
    pm_ref,
    po_ref,
    q_ref,
    k_ref,
    v_ref,
    win_ref,
    lse_ref,
    bias_ref,
    gqkm_ref,
    gqko_ref,
    gvpm_ref,
    gvpo_ref,
    gqkv_ref,
    sums_ref,
    gbias_ref,
    pick_ref,
    gatt_ref,
    mask_ref,
    qsum_ref,
    vsum_ref,
):
    chan = heads * HEAD_DIM
    wide = 2 * chan
    factor = HEAD_DIM ** (-0.5)
    slots = WINS * WPAD
    pick_ref[...] = gather_matrix()
    mask_ref[...] = head_mask(heads)
    gres = gres_ref[...]
    gres_b = gres.astype(BF16)
    put_rows(gvpm_ref, layout, chan, tn(gres_b, merged_ref[:, :chan]))
    put_rows(gvpo_ref, layout, chan, tn(gres_b, merged_ref[:, chan:]))
    grad_m = jnp.concatenate(
        [nn(gres_b, pm_ref[...]).astype(BF16), nn(gres_b, po_ref[...]).astype(BF16)], axis=1
    )
    for image in range(images):
        gatt_ref[image * slots : (image + 1) * slots, :] = nn(
            pick_ref[...], grad_m[image * TPAD : (image + 1) * TPAD]
        ).astype(BF16)
    gbias_ref[...] = jnp.zeros(gbias_ref.shape, F32)
    qsum_ref[...] = jnp.zeros(qsum_ref.shape, F32)
    vsum_ref[...] = jnp.zeros(vsum_ref.shape, F32)

    def one_window(window, carry):
        rows = pl.ds(pl.multiple_of(window * WPAD, WPAD), WPAD)
        image = window // WINS
        local = pl.multiple_of((window - image * WINS) * WPAD, WPAD)
        ids_row = ids_ref[pl.ds(me_ref[0] * images + image, 1), :]
        allowed = window_mask(ids_row, pick_ref[pl.ds(local, WPAD), :])
        mask = mask_ref[...]
        k_all = per_head(k_ref[rows, :], mask, heads)
        v_all = per_head(v_ref[rows, :], mask, heads)
        q_two = two_groups(q_ref[rows, :])
        g_two = two_groups(gatt_ref[rows, :])
        scores = nt(k_all, q_two) + bias_ref[...]
        scores = scores.reshape(heads, WPAD, 2 * WPAD) + allowed[None]
        probs = jnp.exp(scores - lse_ref[window].reshape(heads, 1, 2 * WPAD))
        g_probs = nt(v_all, g_two).reshape(heads, WPAD, 2 * WPAD)
        inner = jnp.sum(probs * g_probs, axis=1, keepdims=True)
        g_scores = (probs * (g_probs - inner)).reshape(heads * WPAD, 2 * WPAD)
        gbias_ref[...] += g_scores
        probs_b = probs.astype(BF16).reshape(heads * WPAD, 2 * WPAD)
        g_scores = g_scores.astype(BF16)

        def fold(product):
            return jnp.sum((product * mask.astype(F32)).reshape(heads, WPAD, wide), axis=0)

        g_v = fold(nn(probs_b, g_two))
        g_k = fold(nn(g_scores, q_two))
        g_q = own_groups(tn(g_scores, k_all)) * factor
        qsum_ref[...] += g_q
        vsum_ref[...] += g_v
        for group in range(2):
            cols = slice(group * chan, (group + 1) * chan)
            base = group * 3 * chan
            gqkv_ref[rows, base : base + chan] = g_q[:, cols].astype(BF16)
            gqkv_ref[rows, base + chan : base + 2 * chan] = g_k[:, cols].astype(BF16)
            gqkv_ref[rows, base + 2 * chan : base + 3 * chan] = g_v[:, cols].astype(BF16)
        return carry

    lax.fori_loop(0, images * WINS, one_window, 0, unroll=2)
    sums_ref[...] = jnp.zeros(sums_ref.shape, F32)
    sums_ref[0:1, :] = jnp.sum(qsum_ref[...], axis=0, keepdims=True)
    sums_ref[1:2, :] = jnp.sum(vsum_ref[...], axis=0, keepdims=True)
    win = win_ref[...]
    put_rows(gqko_ref, layout, 0, tn(win, gqkv_ref[:, 3 * chan : 5 * chan]))
    put_rows(gvpo_ref, layout, 0, tn(win, gqkv_ref[:, 5 * chan :]))
    put_rows(gqkm_ref, layout, 0, tn(win, gqkv_ref[:, : 2 * chan]))
    put_rows(gvpm_ref, layout, 0, tn(win, gqkv_ref[:, 2 * chan : 3 * chan]))


def last_kernel(
    images,
    heads,
    rows_half,
    me_ref,
    tok_ref,
    gres_ref,
    gqkv_ref,
    wm_ref,
    wo_ref,
    gain_ref,
    gbias_ref,
    two_ref,
    qv_ref,
    gbm_ref,
    gbo_ref,
    half_ref,
    mine_ref,
    theirs_ref,
    x_ref,
    off_ref,
    acc_ref,
):
    chan = heads * HEAD_DIM
    slots = WINS * WPAD
    grad_win = nt(gqkv_ref[:, :chan], wm_ref[0])
    for at in range(1, 6):
        w_ref = wm_ref if at < 3 else wo_ref
        grad_win += nt(gqkv_ref[:, at * chan : (at + 1) * chan], w_ref[at % 3])
    high = grad_win.astype(BF16)
    low = (grad_win - high.astype(F32)).astype(BF16)
    back = scatter_matrix()
    upstream = jnp.concatenate(
        [
            nn(back, high[image * slots : (image + 1) * slots])
            + nn(back, low[image * slots : (image + 1) * slots])
            for image in range(images)
        ],
        axis=0,
    )
    fill_rows(x_ref, tok_ref, me_ref[0] * images, images)
    normed, inverse = normalize(x_ref[...])
    grad_in = gres_ref[...] + norm_back(upstream, normed, inverse, gain_ref[...])
    for image in range(images):
        half_ref[image] = grad_in[image * TPAD : image * TPAD + TOK]
    width = upstream.shape[1]
    gain_sum = jnp.sum(upstream * normed, axis=0, keepdims=True)
    shift_sum = jnp.sum(upstream, axis=0, keepdims=True)
    off_ref[...] = table_offsets(rows_half)
    acc_ref[...] = jnp.zeros(acc_ref.shape, F32)
    for key in range(WTOK):
        pick = jnp.where(off_ref[...] == key_offset(key), 1.0, 0.0).astype(BF16)
        rows = gbias_ref[pl.ds(key, heads, stride=WPAD), :]
        top = rows.astype(BF16).astype(F32)
        parts = jnp.concatenate([top, rows - top], axis=0).astype(BF16)
        acc_ref[...] += nt(parts, pick)
    table = acc_ref[:heads] + acc_ref[heads:]
    for group, (pack_ref, gb_ref) in enumerate(((mine_ref, gbm_ref), (theirs_ref, gbo_ref))):
        pack_ref[...] = jnp.zeros(pack_ref.shape, F32)
        pack_ref[0:4, :] = two_ref[0:4, :]
        pack_ref[4:5, :] = gain_sum
        pack_ref[5:6, :] = shift_sum
        pack_ref[6:7, :chan] = qv_ref[0:1, group * chan : (group + 1) * chan]
        pack_ref[6:7, chan:] = qv_ref[1:2, group * chan : (group + 1) * chan]
        for at in range(gb_ref.shape[1] // width):
            pack_ref[7 + at : 8 + at, :] = gb_ref[:, at * width : (at + 1) * width]
        half = table[:, group * rows_half : (group + 1) * rows_half]
        low = pack_ref.shape[0] - heads // 2
        pack_ref[low:, :rows_half] = half[: heads // 2]
        pack_ref[low:, chan : chan + rows_half] = half[heads // 2 :]


def unpack_kernel(parts, sel_ref, *refs):
    ins, outs = refs[:parts], refs[parts:]
    if parts == 2:
        total = ins[0][...] + ins[1][...]
    else:
        total = (ins[0][...] + ins[1][...]) + (ins[2][...] + ins[3][...])
    for at in range(6):
        outs[at][...] = total[at : at + 1]
    qv_ref, b1_ref, table_ref = outs[6:]
    chan, (heads, entries) = qv_ref.shape[1], table_ref.shape
    qv_ref[0:1, :] = total[6:7, :chan]
    qv_ref[1:2, :] = total[6:7, chan:]
    width = total.shape[1]
    for at in range(b1_ref.shape[1] // width):
        b1_ref[:, at * width : (at + 1) * width] = total[7 + at : 8 + at]
    low = total.shape[0] - heads // 2
    table_ref[: heads // 2, :] = total[low:, :entries]
    table_ref[heads // 2 :, :] = total[low:, chan : chan + entries]


def rows_at(ref, start, rows):
    return ref[pl.ds(pl.multiple_of(start, rows), rows), :].astype(F32)


def add_kernel(rows, sel_ref, a0_ref, a1_ref, b0_ref, b1_ref, *out_refs):
    half = a0_ref.shape[1]
    for s, out_ref in enumerate(out_refs, 1):
        at = (sel_ref[1] ^ s) * rows
        out_ref[:, :half] = (rows_at(a0_ref, at, rows) + rows_at(a1_ref, at, rows)).astype(BF16)
        out_ref[:, half:] = (rows_at(b0_ref, at, rows) + rows_at(b1_ref, at, rows)).astype(BF16)


def fan_kernel(rows, sends, sel_ref, *refs):
    pairs, wide, outs = refs[:4], refs[4 : -1 - sends], refs[-1 - sends :]
    half = pairs[0].shape[1]
    for s in range(sends + 1):
        near = (sel_ref[2] ^ s) * rows
        far = sel_ref[1] * (rows * (sends + 1)) + near
        got = rows_at(wide[0], near, rows)
        for ref in wide[1:]:
            got = got + rows_at(ref, near, rows)
        out_ref = outs[s - 1] if s else outs[sends]
        for cols, first, second in (
            (slice(0, half), pairs[0], pairs[1]),
            (slice(half, got.shape[1]), pairs[2], pairs[3]),
        ):
            total = rows_at(first, far, rows) + rows_at(second, far, rows) + got[:, cols]
            out_ref[:, cols] = total.astype(out_ref.dtype)


def total_kernel(parts, sel_ref, own_ref, *refs):
    total, at = own_ref[...], 0
    for in_ref in refs[: parts - 1]:
        total = total + in_ref[...].astype(F32)
    for out_ref in refs[parts - 1 :]:
        width = out_ref.shape[-1]
        if len(out_ref.shape) == 2:
            out_ref[...] = total[:, at : at + width]
            at += width
            continue
        for plane in range(out_ref.shape[0]):
            out_ref[plane] = total[:, at : at + width]
            at += width


def join_kernel(sel_ref, own_ref, other_ref, out_ref):
    images = own_ref.shape[0]
    for image in range(out_ref.shape[1]):
        mine = sel_ref[0] == image // images
        piece = jnp.where(
            mine, own_ref[image % images].astype(F32), other_ref[image % images].astype(F32)
        )
        out_ref[:, image, :] = piece.astype(out_ref.dtype)


def pair_kernel(sel_ref, a_ref, b_ref, out_ref):
    out_ref[...] = a_ref[...] + b_ref[...]


def four_kernel(sel_ref, a_ref, b_ref, c_ref, d_ref, out_ref):
    out_ref[...] = (a_ref[...] + b_ref[...]) + (c_ref[...] + d_ref[...])


def struct(shape, kind):
    return jax.ShapeDtypeStruct(shape, kind)


def call(kernel, scalars, inputs, outs, scratch, flops, limit_mib):
    moved = sum(a.size * a.dtype.itemsize for a in inputs)
    moved += sum(a.size * a.dtype.itemsize for a in outs)
    vmem = pl.BlockSpec(memory_space=pltpu.VMEM)
    return pl.pallas_call(
        kernel,
        in_specs=[pl.BlockSpec(memory_space=pltpu.SMEM)] + [vmem] * len(inputs),
        out_specs=[vmem] * len(outs),
        out_shape=outs,
        scratch_shapes=scratch,
        compiler_params=pltpu.CompilerParams(vmem_limit_bytes=limit_mib << 20),
        cost_estimate=pl.CostEstimate(flops=flops, bytes_accessed=moved, transcendentals=0),
    )(scalars, *inputs)


def digits_of(count):
    digits, stride = [], 1
    while stride < count:
        size = 4 if (count // stride) % 4 == 0 else 2
        digits.append((stride, size))
        stride *= size
    return digits


def xor_exchange(value, axis, count, mask):
    return lax.ppermute(value, axis, [(i, i ^ mask) for i in range(count)])


def scatter_sum(addends, axis, count, digits):
    index = lax.axis_index(axis)
    rows, cols = addends[0].shape
    shape = [size for _, size in reversed(digits)] + [rows // count, cols]
    addends = [a.reshape(shape) for a in addends]
    left = list(reversed(range(len(digits))))
    for digit in range(len(digits)):
        stride, size = digits[digit]
        place = left.index(digit)
        mine = (index // stride) % size

        def part(which):
            return [lax.dynamic_index_in_dim(a, which, place, keepdims=False) for a in addends]

        def total(pieces):
            result = pieces[0].astype(F32)
            for piece in pieces[1:]:
                result = result + piece.astype(F32)
            return result

        received = [
            xor_exchange(total(part(mine ^ s)).astype(BF16), axis, count, s * stride)
            for s in range(1, size)
        ]
        addends = part(mine) + received
        left.remove(digit)
    return total(addends)


def all_sum(sel, value, axis, count):
    mask = 1
    while True:
        size = 4 if 4 * mask <= count else 2
        terms = [value]
        for s in range(1, size):
            terms.append(xor_exchange(value, axis, count, s * mask))
        mask *= size
        if mask >= count:
            return terms
        kernel = four_kernel if size == 4 else pair_kernel
        (value,) = call(kernel, sel, terms, [struct(value.shape, F32)], [], 10**5, 2)


def scatter_pairs(sel, pairs, axis, count, digits, outs):
    (stride, size), (far_stride, far_size) = digits
    (a0, a1), (b0, b1) = pairs
    arrays = [a0, a1, b0, b1]
    cols = a0.shape[1] + b0.shape[1]
    deep = a0.shape[0] // size
    rows = deep // far_size

    def exchange(sends, step):
        received = []
        for s, send in enumerate(sends, 1):
            received.append(xor_exchange(send, axis, count, s * step))
        return received

    sends = call(
        functools.partial(add_kernel, deep),
        sel,
        arrays,
        [struct((deep, cols), BF16)] * (size - 1),
        [],
        10**6,
        4,
    )
    wide = exchange(sends, stride)
    *sends, own = call(
        functools.partial(fan_kernel, rows, far_size - 1),
        sel,
        arrays + wide,
        [struct((rows, cols), BF16)] * (far_size - 1) + [struct((rows, cols), F32)],
        [],
        10**6,
        4,
    )
    parts = [own] + exchange(sends, far_stride)
    return call(functools.partial(total_kernel, len(parts)), sel, parts, outs, [], 10**6, 4)


def per_device(n_dp, n_tensor, *args):
    return block(n_dp, n_tensor, *args)


def block(
    n_dp,
    n_tensor,
    tokens,
    region_ids,
    norm1_gain,
    norm1_bias,
    w_qkv,
    qv_bias,
    rel_table,
    w_proj,
    b_proj,
    norm2_gain,
    norm2_bias,
    w_fc1,
    b_fc1,
    w_fc2,
    b_fc2,
    cotangent,
):
    all_images, _, width = tokens.shape
    images = all_images // n_tensor
    entries, heads = rel_table.shape
    chan = heads * HEAD_DIM
    hidden = w_fc1.shape[1]
    rows_t = images * TPAD
    rows_w = images * WINS * WPAD
    half_rows = -(-entries // 16) * 16
    digits = digits_of(n_dp)
    by_pairs = len(digits) == 2 and width // n_dp % 16 == 0
    order = list(range(len(digits)))
    layout = (width // n_dp, digits, order if by_pairs else order[::-1])
    me = lax.axis_index("tensor")
    spot = lax.axis_index("dp")
    places = [(spot // stride) % size for stride, size in digits[:2]]
    me_arr = sel = jnp.stack([me] + places).astype(jnp.int32)

    def swap(value):
        return lax.ppermute(value, "tensor", [(i, i ^ 1) for i in range(n_tensor)])

    wm = w_qkv.transpose(1, 0, 2)
    wo = swap(wm)
    table_m = rel_table.T
    table_o = swap(table_m)
    qvb_o = swap(qv_bias)
    po = swap(w_proj)
    b1_o = swap(b_fc1.reshape(1, hidden))
    w1o = swap(w_fc1)
    w2o = swap(w_fc2)

    row = lambda vec: vec.reshape(1, -1)

    bias_shape = struct((heads * WPAD, 2 * WPAD), F32)
    (bias,) = call(
        functools.partial(bias_kernel, heads, half_rows),
        sel,
        [table_m, table_o],
        [bias_shape],
        [
            pltpu.VMEM((2 * half_rows, 2 * WPAD), jnp.int32),
            pltpu.VMEM((heads, 2 * half_rows), F32),
        ],
        10**9,
        4,
    )

    ins = (
        tokens,
        region_ids,
        row(norm1_gain),
        row(norm1_bias),
        wm,
        wo,
        qv_bias,
        qvb_o,
        bias,
        w_proj,
        po,
        row(b_proj),
    )
    outs = (
        struct((rows_w, 2 * chan), BF16),
        struct((rows_w, 2 * chan), BF16),
        struct((rows_w, 2 * chan), BF16),
        struct((rows_w, width), BF16),
        struct((images * WINS, heads, 2 * WPAD), F32),
        struct((rows_t, 2 * chan), BF16),
        struct((rows_t, width), F32),
    )
    q, k, v, win_in, lse, merged, resid = call(
        functools.partial(attend_kernel, images, heads),
        me_arr,
        ins,
        outs,
        [
            pltpu.VMEM((rows_t, width), F32),
            pltpu.VMEM((WINS * WPAD, TPAD), BF16),
            pltpu.VMEM((rows_w, 2 * chan), BF16),
            pltpu.VMEM((heads * WPAD, 2 * chan), BF16),
        ],
        3 * 10**9,
        LIMIT,
    )

    weight_grad = struct((width, hidden), BF16)
    acc = struct((rows_t, width), F32)
    kept = (
        struct((rows_t, width), BF16),
        struct((width, rows_t), BF16),
        struct((rows_t, width), BF16),
        struct((width, rows_t), BF16),
        acc,
        acc,
    )
    common = (resid, cotangent, row(norm2_gain), row(norm2_bias))
    ins = common + (w1o, w2o, b1_o)
    outs = (weight_grad, weight_grad, struct((1, hidden), F32)) + kept
    g1o, g2o, gbo, *carried = call(
        functools.partial(ffn_kernel, images, layout, False),
        me_arr,
        ins,
        outs,
        [],
        3 * 10**9,
        LIMIT,
    )
    got1 = swap(g1o)
    got2 = swap(g2o)
    ins = common + (w_fc1, w_fc2, row(b_fc1), row(b_fc2), *carried)
    outs = (
        weight_grad,
        weight_grad,
        struct((1, hidden), F32),
        struct((images, TOK, width), BF16),
        acc,
        struct((8, width), F32),
    )
    g1m, g2m, gbm, out_half, gres, sums_two = call(
        functools.partial(ffn_kernel, images, layout, True),
        me_arr,
        ins,
        outs,
        [pltpu.VMEM((rows_t, width), F32), pltpu.VMEM((rows_t, width), F32)],
        3 * 10**9,
        LIMIT,
    )

    share = width // n_dp

    def join(half):
        shape = struct((TOK, all_images, width), half.dtype)
        (joined,) = call(join_kernel, sel, [half, swap(half)], [shape], [], 10**6, LIMIT)
        return joined.transpose(1, 0, 2)

    if by_pairs:
        outs = [struct((share, hidden), F32)] * 2
        sent_fc1, sent_fc2 = scatter_pairs(
            sel, ((g1m, got1), (g2m, got2)), "dp", n_dp, digits, outs
        )
    else:
        sent_fc1 = scatter_sum((g1m, got1), "dp", n_dp, digits)
        sent_fc2 = scatter_sum((g2m, got2), "dp", n_dp, digits)
    output = join(out_half)

    ins = (gres, region_ids, merged, w_proj, po, q, k, v, win_in, lse, bias)
    outs = (
        struct((width, 2 * chan), BF16),
        struct((width, 2 * chan), BF16),
        struct((width, 2 * chan), BF16),
        struct((width, 2 * chan), BF16),
        struct((rows_w, 6 * chan), BF16),
        struct((8, 2 * chan), F32),
        bias_shape,
    )
    gqkm, gqko, gvpm, gvpo, gqkv, sums_qv, gbias = call(
        functools.partial(attend_back_kernel, images, heads, layout),
        me_arr,
        ins,
        outs,
        [
            pltpu.VMEM((WINS * WPAD, TPAD), BF16),
            pltpu.VMEM((rows_w, 2 * chan), BF16),
            pltpu.VMEM((heads * WPAD, 2 * chan), BF16),
            pltpu.VMEM((WPAD, 2 * chan), F32),
            pltpu.VMEM((WPAD, 2 * chan), F32),
        ],
        5 * 10**9,
        LIMIT,
    )

    got_qk = swap(gqko)
    got_vp = swap(gvpo)
    if by_pairs:
        outs = [struct((3, share, chan), F32), struct((share, chan), F32)]
        sent_qkv, sent_proj = scatter_pairs(
            sel, ((gqkm, got_qk), (gvpm, got_vp)), "dp", n_dp, digits, outs
        )
    else:
        sent_qk = scatter_sum((gqkm, got_qk), "dp", n_dp, digits)
        sent_vp = scatter_sum((gvpm, got_vp), "dp", n_dp, digits)
        sent_qkv = jnp.stack([sent_qk[:, :chan], sent_qk[:, chan:], sent_vp[:, :chan]], axis=0)
        sent_proj = sent_vp[:, chan:]
    sent_qkv = sent_qkv.transpose(1, 0, 2)

    ins = (tokens, gres, gqkv, wm, wo, row(norm1_gain), gbias, sums_two, sums_qv, gbm, gbo)
    pack = struct((-(-(7 + hidden // width + heads // 2) // 8) * 8, width), F32)
    outs = (struct((images, TOK, width), F32), pack, pack)
    grad_half, small, theirs = call(
        functools.partial(last_kernel, images, heads, half_rows),
        me_arr,
        ins,
        outs,
        [
            pltpu.VMEM((rows_t, width), F32),
            pltpu.VMEM((2 * half_rows, 2 * WPAD), jnp.int32),
            pltpu.VMEM((2 * heads, 2 * half_rows), F32),
        ],
        2 * 10**9,
        LIMIT,
    )
    grad_in = join(grad_half)

    got = swap(theirs)
    (small,) = call(pair_kernel, sel, [small, got], [struct(small.shape, F32)], [], 10**5, 2)
    terms = all_sum(sel, small, "dp", n_dp)
    outs = (struct((1, width), F32),) * 6 + (
        struct((2, chan), F32),
        struct((1, hidden), F32),
        struct((heads, entries), F32),
    )
    *vectors, sum_qv, sum_b1, sum_table = call(
        functools.partial(unpack_kernel, len(terms)), sel, terms, outs, [], 10**5, 2
    )
    vectors = [vec.reshape(width) for vec in vectors]
    return (
        output,
        grad_in,
        vectors[4],
        vectors[5],
        sent_qkv,
        sum_qv,
        sum_table.T,
        sent_proj,
        vectors[0],
        vectors[1],
        vectors[2],
        sent_fc1,
        sum_b1.reshape(hidden),
        sent_fc2,
        vectors[3],
    )


def solution(mesh):
    return jax.shard_map(
        functools.partial(per_device, mesh.shape["dp"], mesh.shape["tensor"]),
        mesh=mesh,
        in_specs=(
            P("dp", None, None),
            P("dp", None),
            P(),
            P(),
            P(None, None, "tensor"),
            P(None, "tensor"),
            P(None, "tensor"),
            P(None, "tensor"),
            P(),
            P(),
            P(),
            P(None, "tensor"),
            P("tensor"),
            P(None, "tensor"),
            P(),
            P("dp", None, None),
        ),
        out_specs=(
            P("dp", None, None),
            P("dp", None, None),
            P(),
            P(),
            P("dp", None, "tensor"),
            P(None, "tensor"),
            P(None, "tensor"),
            P("dp", "tensor"),
            P(),
            P(),
            P(),
            P("dp", "tensor"),
            P("tensor"),
            P("dp", "tensor"),
            P(),
        ),
        check_vma=False,
    )
```

```python
import functools

import jax
import jax.numpy as jnp
from jax import lax
from jax.experimental import pallas as pl
from jax.experimental.pallas import tpu as pltpu
from jax.sharding import PartitionSpec as P


HEAD_DIM = 32
SIDE = 14
WIN = 7
SHIFT = 3
NORM_EPS = 1e-05

TOK = SIDE * SIDE
TPAD = 208
WTOK = WIN * WIN
WPAD = 64
BLOCKS = SIDE // WIN
WINS = BLOCKS * BLOCKS
F32 = jnp.float32
BF16 = jnp.bfloat16
LIMIT = 16


def nn(a, b):
    return lax.dot_general(a, b, (((1,), (0,)), ((), ())), preferred_element_type=F32)


def nt(a, b):
    return lax.dot_general(a, b, (((1,), (1,)), ((), ())), preferred_element_type=F32)


def tn(a, b):
    return lax.dot_general(a, b, (((0,), (0,)), ((), ())), preferred_element_type=F32)


def iota(shape, axis):
    return lax.broadcasted_iota(jnp.int32, shape, axis)


def normalize(source):
    center = jnp.mean(source, axis=-1, keepdims=True)
    centred = source - center
    inverse = lax.rsqrt(jnp.mean(centred * centred, axis=-1, keepdims=True) + NORM_EPS)
    return centred * inverse, inverse


def norm_back(upstream, normed, inverse, gain_vec):
    scaled = upstream * gain_vec
    return inverse * (
        scaled
        - jnp.mean(scaled, axis=-1, keepdims=True)
        - normed * jnp.mean(scaled * normed, axis=-1, keepdims=True)
    )


def seventh(value):
    return (value * 37) >> 8


def window_source(slot):
    window, at = slot >> 6, slot & (WPAD - 1)
    row = (window >> 1) * WIN + seventh(at) + SHIFT
    col = (window & 1) * WIN + (at - seventh(at) * WIN) + SHIFT
    row = jnp.where(row >= SIDE, row - SIDE, row)
    col = jnp.where(col >= SIDE, col - SIDE, col)
    return jnp.where(at < WTOK, row * SIDE + col, -1)


def gather_matrix():
    shape = (WINS * WPAD, TPAD)
    hit = window_source(iota(shape, 0)) == iota(shape, 1)
    return jnp.where(hit, 1.0, 0.0).astype(BF16)


def scatter_matrix():
    shape = (TPAD, WINS * WPAD)
    hit = window_source(iota(shape, 1)) == iota(shape, 0)
    return jnp.where(hit, 1.0, 0.0).astype(BF16)


def head_mask(heads):
    shape = (heads * WPAD, 2 * heads * HEAD_DIM)
    hit = (iota(shape, 0) >> 6) == ((iota(shape, 1) & (heads * HEAD_DIM - 1)) >> 5)
    return jnp.where(hit, 1.0, 0.0).astype(BF16)


def log2(value):
    return value.bit_length() - 1


def row_order(slot, rows, digits, order):
    rest, block = slot >> log2(rows), 0
    for digit in reversed(order):
        stride, size = digits[digit]
        block = block + (rest & (size - 1)) * stride
        rest = rest >> log2(size)
    return block * rows + (slot & (rows - 1))


def put_rows(out_ref, layout, col, value):
    rows = layout[0]
    cols = slice(col, col + value.shape[1])
    value = value.astype(out_ref.dtype)
    sources = [row_order(at, *layout) for at in range(0, value.shape[0], rows)]
    if sources == sorted(sources):
        out_ref[:, cols] = value
        return
    for place, source in enumerate(sources):
        out_ref[place * rows : (place + 1) * rows, cols] = value[source : source + rows]


def order_matrix(width, layout):
    shape = (width, width)
    hit = row_order(iota(shape, 0), *layout) == iota(shape, 1)
    return jnp.where(hit, 1.0, 0.0).astype(BF16)


def fill_rows(rows_ref, block_ref, first, images):
    rows_ref[...] = jnp.zeros(rows_ref.shape, rows_ref.dtype)
    for image in range(images):
        rows_ref[image * TPAD : image * TPAD + TOK, :] = block_ref[first + image].astype(
            rows_ref.dtype
        )


def window_mask(ids_row, pick):
    ids_b = jnp.broadcast_to(ids_row.astype(F32), (2 * WPAD, TOK)).astype(BF16)
    pick = pick[:, :TOK]
    keys = nt(pick, ids_b)
    queries = nt(ids_b[:16], jnp.concatenate([pick, pick], axis=0))[0:1]
    shape = (WPAD, 2 * WPAD)
    key_at = iota(shape, 0)
    query_at = iota(shape, 1) & (WPAD - 1)
    same = jnp.logical_or(keys == queries, query_at >= WTOK)
    return jnp.where(jnp.logical_and(same, key_at < WTOK), 0.0, -jnp.inf)


def two_groups(rows):
    half = rows.shape[1] // 2
    zero = jnp.zeros((rows.shape[0], half), rows.dtype)
    return jnp.concatenate(
        [
            jnp.concatenate([rows[:, :half], zero], axis=1),
            jnp.concatenate([zero, rows[:, half:]], axis=1),
        ],
        axis=0,
    )


def own_groups(rows):
    half = rows.shape[1] // 2
    return jnp.concatenate([rows[:WPAD, :half], rows[WPAD:, half:]], axis=1)


def per_head(rows, mask, heads):
    return jnp.concatenate([rows] * heads, axis=0) * mask


def table_offsets(rows_half):
    shape = (2 * rows_half, 2 * WPAD)
    entry, query = iota(shape, 0), iota(shape, 1)
    group_e = jnp.where(entry >= rows_half, 1, 0)
    at = query & (WPAD - 1)
    place = seventh(at) * (2 * WIN - 1) + (at - seventh(at) * WIN)
    fits = jnp.logical_and(group_e == (query >> 6), at < WTOK)
    return jnp.where(fits, entry - group_e * rows_half - place, 4096)


def key_offset(key):
    row = key // WIN
    return 2 * WIN * (WIN - 1) - (row * (2 * WIN - 1) + key - row * WIN)


def bias_kernel(heads, rows_half, sel_ref, mine_ref, other_ref, bias_ref, off_ref, table_ref):
    off_ref[...] = table_offsets(rows_half)
    bias_ref[...] = jnp.zeros(bias_ref.shape, F32)
    entries = mine_ref.shape[1]
    table_ref[...] = jnp.zeros(table_ref.shape, F32)
    table_ref[:, :entries] = mine_ref[...]
    table_ref[:, rows_half : rows_half + entries] = other_ref[...]
    table = table_ref[...]
    part_a = table.astype(BF16).astype(F32)
    part_b = (table - part_a).astype(BF16).astype(F32)
    part_c = table - part_a - part_b
    parts = jnp.concatenate([part_a, part_b, part_c], axis=0).astype(BF16)
    for key in range(WTOK):
        pick = jnp.where(off_ref[...] == key_offset(key), 1.0, 0.0).astype(BF16)
        rows = nn(parts, pick)
        bias_ref[pl.ds(key, heads, stride=WPAD), :] = (
            rows[:heads] + rows[heads : 2 * heads] + rows[2 * heads :]
        )


def attend_kernel(
    images,
    heads,
    me_ref,
    tok_ref,
    ids_ref,
    gain_ref,
    shift_ref,
    wm_ref,
    wo_ref,
    qvbm_ref,
    qvbo_ref,
    bias_ref,
    pm_ref,
    po_ref,
    bproj_ref,
    q_ref,
    k_ref,
    v_ref,
    win_ref,
    lse_ref,
    merged_ref,
    resid_ref,
    x_ref,
    pick_ref,
    att_ref,
    mask_ref,
):
    chan = heads * HEAD_DIM
    factor = HEAD_DIM ** (-0.5)
    fill_rows(x_ref, tok_ref, me_ref[0] * images, images)
    normed, _ = normalize(x_ref[...])
    ln_one = (normed * gain_ref[...] + shift_ref[...]).astype(BF16)
    pick_ref[...] = gather_matrix()
    mask_ref[...] = head_mask(heads)
    slots = WINS * WPAD
    for image in range(images):
        win_ref[image * slots : (image + 1) * slots, :] = nn(
            pick_ref[...], ln_one[image * TPAD : (image + 1) * TPAD]
        ).astype(BF16)
    for group, (w_ref, b_ref) in enumerate(((wm_ref, qvbm_ref), (wo_ref, qvbo_ref))):
        cols = slice(group * chan, (group + 1) * chan)
        win = win_ref[...]
        q_ref[:, cols] = ((nn(win, w_ref[0]) + b_ref[0:1, :]) * factor).astype(BF16)
        k_ref[:, cols] = nn(win, w_ref[1]).astype(BF16)
        v_ref[:, cols] = (nn(win, w_ref[2]) + b_ref[1:2, :]).astype(BF16)

    def one_window(window, carry):
        rows = pl.ds(pl.multiple_of(window * WPAD, WPAD), WPAD)
        image = window // WINS
        local = pl.multiple_of((window - image * WINS) * WPAD, WPAD)
        ids_row = ids_ref[pl.ds(me_ref[0] * images + image, 1), :]
        allowed = window_mask(ids_row, pick_ref[pl.ds(local, WPAD), :])
        k_all = per_head(k_ref[rows, :], mask_ref[...], heads)
        v_all = per_head(v_ref[rows, :], mask_ref[...], heads)
        scores = nt(k_all, two_groups(q_ref[rows, :])) + bias_ref[...]
        scores = scores.reshape(heads, WPAD, 2 * WPAD) + allowed[None]
        top = jnp.max(scores, axis=1, keepdims=True)
        grown = jnp.exp(scores - top)
        total = jnp.sum(grown, axis=1, keepdims=True)
        lse_ref[window] = (top + jnp.log(total)).reshape(heads, 2 * WPAD)
        probs = (grown * (1.0 / total)).astype(BF16).reshape(heads * WPAD, 2 * WPAD)
        att_ref[rows, :] = own_groups(tn(probs, v_all)).astype(BF16)
        return carry

    lax.fori_loop(0, images * WINS, one_window, 0, unroll=True)
    back = scatter_matrix()
    for image in range(images):
        merged_ref[image * TPAD : (image + 1) * TPAD, :] = nn(
            back, att_ref[image * slots : (image + 1) * slots, :]
        ).astype(BF16)
    resid_ref[...] = (
        x_ref[...]
        + (nt(merged_ref[:, :chan], pm_ref[...]) + nt(merged_ref[:, chan:], po_ref[...]))
        + bproj_ref[...]
    )


def ffn_kernel(
    images,
    layout,
    last,
    me_ref,
    resid_ref,
    cot_ref,
    gain_ref,
    shift_ref,
    w1_ref,
    w2_ref,
    b1_ref,
    *refs,
):
    if last:
        b2_ref, ln_ref, lnt_ref, cot_b_ref, cot_t_ref, ffn_in, gln_in = refs[:7]
        g1_ref, g2_ref, gb_ref, half_ref, gres_ref, sums_ref = refs[7:13]
        ffn_ref, gln_ref = refs[13:]
    else:
        g1_ref, g2_ref, gb_ref = refs[:3]
        ln_ref, lnt_ref, cot_b_ref, cot_t_ref, ffn_ref, gln_ref = refs[3:]
    if last:
        ffn_ref[...] = ffn_in[...]
        gln_ref[...] = gln_in[...]
    else:
        normed, _ = normalize(resid_ref[...])
        ln_ref[...] = (normed * gain_ref[...] + shift_ref[...]).astype(BF16)
        fill_rows(cot_b_ref, cot_ref, me_ref[0] * images, images)
        width = ln_ref.shape[1]
        order = order_matrix(width, layout)
        lnt_ref[...] = nt(order, ln_ref[...]).astype(BF16)
        cot_t_ref[...] = nt(order, cot_b_ref[...]).astype(BF16)
        ffn_ref[...] = jnp.zeros(ffn_ref.shape, F32)
        gln_ref[...] = jnp.zeros(gln_ref.shape, F32)
    chunk = 256

    def one_chunk(at, carry):
        cols = pl.ds(pl.multiple_of(at * chunk, chunk), chunk)
        pre = nn(ln_ref[...], w1_ref[:, cols]) + b1_ref[:, cols]
        phi = 0.5 * (1.0 + lax.erf(pre * 0.7071067811865476))
        act = (pre * phi).astype(BF16)
        slope = phi + pre * jnp.exp(-0.5 * pre * pre) * 0.3989422804014327
        grad_pre = nn(cot_b_ref[...], w2_ref[:, cols]) * slope
        gb_ref[:, cols] = jnp.sum(grad_pre, axis=0, keepdims=True)
        grad_pre = grad_pre.astype(BF16)
        ffn_ref[...] += nt(act, w2_ref[:, cols])
        gln_ref[...] += nt(grad_pre, w1_ref[:, cols])
        g2_ref[:, cols] = nn(cot_t_ref[...], act).astype(BF16)
        g1_ref[:, cols] = nn(lnt_ref[...], grad_pre).astype(BF16)
        return carry

    lax.fori_loop(0, w1_ref.shape[1] // chunk, one_chunk, 0, unroll=True)
    if not last:
        return
    resid = resid_ref[...]
    result = (resid + ffn_ref[...] + b2_ref[...]).astype(BF16)
    for image in range(images):
        half_ref[image] = result[image * TPAD : image * TPAD + TOK]
    normed, inverse = normalize(resid)
    upstream = gln_ref[...]
    cot = cot_b_ref[...].astype(F32)
    grad_resid = cot + norm_back(upstream, normed, inverse, gain_ref[...])
    gres_ref[...] = grad_resid
    sums_ref[0:1, :] = jnp.sum(grad_resid, axis=0, keepdims=True)
    sums_ref[1:2, :] = jnp.sum(upstream * normed, axis=0, keepdims=True)
    sums_ref[2:3, :] = jnp.sum(upstream, axis=0, keepdims=True)
    sums_ref[3:4, :] = jnp.sum(cot, axis=0, keepdims=True)
    sums_ref[4:8, :] = jnp.zeros((4, sums_ref.shape[1]), F32)


def attend_back_kernel(
    images,
    heads,
    layout,
    me_ref,
    gres_ref,
    ids_ref,
    merged_ref,
    pm_ref,
    po_ref,
    q_ref,
    k_ref,
    v_ref,
    win_ref,
    lse_ref,
    bias_ref,
    gqkm_ref,
    gqko_ref,
    gvpm_ref,
    gvpo_ref,
    gqkv_ref,
    sums_ref,
    gbias_ref,
    pick_ref,
    gatt_ref,
    mask_ref,
    qsum_ref,
    vsum_ref,
):
    chan = heads * HEAD_DIM
    wide = 2 * chan
    factor = HEAD_DIM ** (-0.5)
    slots = WINS * WPAD
    pick_ref[...] = gather_matrix()
    mask_ref[...] = head_mask(heads)
    gres = gres_ref[...]
    gres_b = gres.astype(BF16)
    put_rows(gvpm_ref, layout, chan, tn(gres_b, merged_ref[:, :chan]))
    put_rows(gvpo_ref, layout, chan, tn(gres_b, merged_ref[:, chan:]))
    grad_m = jnp.concatenate(
        [nn(gres_b, pm_ref[...]).astype(BF16), nn(gres_b, po_ref[...]).astype(BF16)], axis=1
    )
    for image in range(images):
        gatt_ref[image * slots : (image + 1) * slots, :] = nn(
            pick_ref[...], grad_m[image * TPAD : (image + 1) * TPAD]
        ).astype(BF16)
    gbias_ref[...] = jnp.zeros(gbias_ref.shape, F32)
    qsum_ref[...] = jnp.zeros(qsum_ref.shape, F32)
    vsum_ref[...] = jnp.zeros(vsum_ref.shape, F32)

    def one_window(window, carry):
        rows = pl.ds(pl.multiple_of(window * WPAD, WPAD), WPAD)
        image = window // WINS
        local = pl.multiple_of((window - image * WINS) * WPAD, WPAD)
        ids_row = ids_ref[pl.ds(me_ref[0] * images + image, 1), :]
        allowed = window_mask(ids_row, pick_ref[pl.ds(local, WPAD), :])
        mask = mask_ref[...]
        k_all = per_head(k_ref[rows, :], mask, heads)
        v_all = per_head(v_ref[rows, :], mask, heads)
        q_two = two_groups(q_ref[rows, :])
        g_two = two_groups(gatt_ref[rows, :])
        scores = nt(k_all, q_two) + bias_ref[...]
        scores = scores.reshape(heads, WPAD, 2 * WPAD) + allowed[None]
        probs = jnp.exp(scores - lse_ref[window].reshape(heads, 1, 2 * WPAD))
        g_probs = nt(v_all, g_two).reshape(heads, WPAD, 2 * WPAD)
        inner = jnp.sum(probs * g_probs, axis=1, keepdims=True)
        g_scores = (probs * (g_probs - inner)).reshape(heads * WPAD, 2 * WPAD)
        gbias_ref[...] += g_scores
        probs_b = probs.astype(BF16).reshape(heads * WPAD, 2 * WPAD)
        g_scores = g_scores.astype(BF16)

        def fold(product):
            return jnp.sum((product * mask.astype(F32)).reshape(heads, WPAD, wide), axis=0)

        g_v = fold(nn(probs_b, g_two))
        g_k = fold(nn(g_scores, q_two))
        g_q = own_groups(tn(g_scores, k_all)) * factor
        qsum_ref[...] += g_q
        vsum_ref[...] += g_v
        for group in range(2):
            cols = slice(group * chan, (group + 1) * chan)
            base = group * 3 * chan
            gqkv_ref[rows, base : base + chan] = g_q[:, cols].astype(BF16)
            gqkv_ref[rows, base + chan : base + 2 * chan] = g_k[:, cols].astype(BF16)
            gqkv_ref[rows, base + 2 * chan : base + 3 * chan] = g_v[:, cols].astype(BF16)
        return carry

    lax.fori_loop(0, images * WINS, one_window, 0, unroll=True)
    sums_ref[...] = jnp.zeros(sums_ref.shape, F32)
    sums_ref[0:1, :] = jnp.sum(qsum_ref[...], axis=0, keepdims=True)
    sums_ref[1:2, :] = jnp.sum(vsum_ref[...], axis=0, keepdims=True)
    win = win_ref[...]
    put_rows(gqko_ref, layout, 0, tn(win, gqkv_ref[:, 3 * chan : 5 * chan]))
    put_rows(gvpo_ref, layout, 0, tn(win, gqkv_ref[:, 5 * chan :]))
    put_rows(gqkm_ref, layout, 0, tn(win, gqkv_ref[:, : 2 * chan]))
    put_rows(gvpm_ref, layout, 0, tn(win, gqkv_ref[:, 2 * chan : 3 * chan]))


def last_kernel(
    images,
    heads,
    rows_half,
    me_ref,
    tok_ref,
    gres_ref,
    gqkv_ref,
    wm_ref,
    wo_ref,
    gain_ref,
    gbias_ref,
    two_ref,
    qv_ref,
    gbm_ref,
    gbo_ref,
    half_ref,
    mine_ref,
    theirs_ref,
    x_ref,
    off_ref,
    acc_ref,
):
    chan = heads * HEAD_DIM
    slots = WINS * WPAD
    grad_win = nt(gqkv_ref[:, :chan], wm_ref[0])
    for at in range(1, 6):
        w_ref = wm_ref if at < 3 else wo_ref
        grad_win += nt(gqkv_ref[:, at * chan : (at + 1) * chan], w_ref[at % 3])
    high = grad_win.astype(BF16)
    low = (grad_win - high.astype(F32)).astype(BF16)
    back = scatter_matrix()
    upstream = jnp.concatenate(
        [
            nn(back, high[image * slots : (image + 1) * slots])
            + nn(back, low[image * slots : (image + 1) * slots])
            for image in range(images)
        ],
        axis=0,
    )
    fill_rows(x_ref, tok_ref, me_ref[0] * images, images)
    normed, inverse = normalize(x_ref[...])
    grad_in = gres_ref[...] + norm_back(upstream, normed, inverse, gain_ref[...])
    for image in range(images):
        half_ref[image] = grad_in[image * TPAD : image * TPAD + TOK]
    width = upstream.shape[1]
    gain_sum = jnp.sum(upstream * normed, axis=0, keepdims=True)
    shift_sum = jnp.sum(upstream, axis=0, keepdims=True)
    off_ref[...] = table_offsets(rows_half)
    acc_ref[...] = jnp.zeros(acc_ref.shape, F32)
    for key in range(WTOK):
        pick = jnp.where(off_ref[...] == key_offset(key), 1.0, 0.0).astype(BF16)
        rows = gbias_ref[pl.ds(key, heads, stride=WPAD), :]
        top = rows.astype(BF16).astype(F32)
        parts = jnp.concatenate([top, rows - top], axis=0).astype(BF16)
        acc_ref[...] += nt(parts, pick)
    table = acc_ref[:heads] + acc_ref[heads:]
    for group, (pack_ref, gb_ref) in enumerate(((mine_ref, gbm_ref), (theirs_ref, gbo_ref))):
        pack_ref[...] = jnp.zeros(pack_ref.shape, F32)
        pack_ref[0:4, :] = two_ref[0:4, :]
        pack_ref[4:5, :] = gain_sum
        pack_ref[5:6, :] = shift_sum
        pack_ref[6:7, :chan] = qv_ref[0:1, group * chan : (group + 1) * chan]
        pack_ref[6:7, chan:] = qv_ref[1:2, group * chan : (group + 1) * chan]
        for at in range(gb_ref.shape[1] // width):
            pack_ref[7 + at : 8 + at, :] = gb_ref[:, at * width : (at + 1) * width]
        half = table[:, group * rows_half : (group + 1) * rows_half]
        low = pack_ref.shape[0] - heads // 2
        pack_ref[low:, :rows_half] = half[: heads // 2]
        pack_ref[low:, chan : chan + rows_half] = half[heads // 2 :]


def spread_small(total, outs):
    for at in range(6):
        outs[at][...] = total[at : at + 1]
    qv_ref, b1_ref, table_ref = outs[6:]
    chan, (heads, entries) = qv_ref.shape[1], table_ref.shape
    qv_ref[0:1, :] = total[6:7, :chan]
    qv_ref[1:2, :] = total[6:7, chan:]
    width = total.shape[1]
    for at in range(b1_ref.shape[1] // width):
        b1_ref[:, at * width : (at + 1) * width] = total[7 + at : 8 + at]
    low = total.shape[0] - heads // 2
    table_ref[: heads // 2, :] = total[low:, :entries]
    table_ref[heads // 2 :, :] = total[low:, chan : chan + entries]


def in_pairs(terms):
    if len(terms) == 2:
        return terms[0] + terms[1]
    return (terms[0] + terms[1]) + (terms[2] + terms[3])


def unpack_kernel(parts, sel_ref, *refs):
    spread_small(in_pairs([ref[...] for ref in refs[:parts]]), refs[parts:])


def rows_at(ref, start, rows):
    return ref[pl.ds(pl.multiple_of(start, rows), rows), :].astype(F32)


def add_kernel(rows, sel_ref, a0_ref, a1_ref, b0_ref, b1_ref, *out_refs):
    half = a0_ref.shape[1]
    for s, out_ref in enumerate(out_refs, 1):
        at = (sel_ref[1] ^ s) * rows
        out_ref[:, :half] = (rows_at(a0_ref, at, rows) + rows_at(a1_ref, at, rows)).astype(BF16)
        out_ref[:, half:] = (rows_at(b0_ref, at, rows) + rows_at(b1_ref, at, rows)).astype(BF16)


def fan_kernel(rows, sends, sel_ref, *refs):
    pairs, wide, outs = refs[:4], refs[4 : -1 - sends], refs[-1 - sends :]
    half = pairs[0].shape[1]
    for s in range(sends + 1):
        near = (sel_ref[2] ^ s) * rows
        far = sel_ref[1] * (rows * (sends + 1)) + near
        got = rows_at(wide[0], near, rows)
        for ref in wide[1:]:
            got = got + rows_at(ref, near, rows)
        out_ref = outs[s - 1] if s else outs[sends]
        for cols, first, second in (
            (slice(0, half), pairs[0], pairs[1]),
            (slice(half, got.shape[1]), pairs[2], pairs[3]),
        ):
            total = rows_at(first, far, rows) + rows_at(second, far, rows) + got[:, cols]
            out_ref[:rows, cols] = total.astype(out_ref.dtype)


def total_kernel(parts, sel_ref, own_ref, *refs):
    total, at = own_ref[...], 0
    for in_ref in refs[: parts - 1]:
        total = total + in_ref[...].astype(F32)
    for out_ref in refs[parts - 1 :]:
        width = out_ref.shape[-1]
        if len(out_ref.shape) == 2:
            out_ref[...] = total[:, at : at + width]
            at += width
            continue
        for plane in range(out_ref.shape[0]):
            out_ref[plane] = total[:, at : at + width]
            at += width


def fan_small_kernel(rows, sends, terms, sel_ref, *refs):
    ins, small, outs = refs[: -terms - sends - 2], refs[-terms - sends - 2 : -sends - 2], refs[-sends - 2 :]
    fan_kernel(rows, sends, sel_ref, *ins, *outs[:-1])
    total = in_pairs([ref[...] for ref in small]).astype(BF16)
    half, width = total.shape[0] // 2, total.shape[1]
    for out_ref in outs[:sends]:
        out_ref[rows:, :width] = total[:half]
        out_ref[rows:, width:] = total[half:]
    outs[-1][...] = total.astype(F32)


def total_small_kernel(parts, main, sel_ref, own_ref, small_ref, *refs):
    rows, width = own_ref.shape[0], small_ref.shape[1]
    received = refs[: parts - 1]
    total_kernel(parts, sel_ref, own_ref, *[ref.at[:rows, :] for ref in received], *refs[parts - 1 :][:main])
    terms = [small_ref[...]]
    for ref in received:
        low = ref[rows:, :].astype(F32)
        terms.append(jnp.concatenate([low[:, :width], low[:, width:]], axis=0))
    spread_small(in_pairs(terms), refs[parts - 1 :][main:])


def join_kernel(sel_ref, own_ref, other_ref, out_ref):
    images = own_ref.shape[0]
    for image in range(out_ref.shape[1]):
        mine = sel_ref[0] == image // images
        piece = jnp.where(
            mine, own_ref[image % images].astype(F32), other_ref[image % images].astype(F32)
        )
        out_ref[:, image, :] = piece.astype(out_ref.dtype)


def pair_kernel(sel_ref, a_ref, b_ref, out_ref):
    out_ref[...] = a_ref[...] + b_ref[...]


def four_kernel(sel_ref, a_ref, b_ref, c_ref, d_ref, out_ref):
    out_ref[...] = (a_ref[...] + b_ref[...]) + (c_ref[...] + d_ref[...])


def struct(shape, kind):
    return jax.ShapeDtypeStruct(shape, kind)


def call(kernel, scalars, inputs, outs, scratch, flops, limit_mib):
    moved = sum(a.size * a.dtype.itemsize for a in inputs)
    moved += sum(a.size * a.dtype.itemsize for a in outs)
    vmem = pl.BlockSpec(memory_space=pltpu.VMEM)
    return pl.pallas_call(
        kernel,
        in_specs=[pl.BlockSpec(memory_space=pltpu.SMEM)] + [vmem] * len(inputs),
        out_specs=[vmem] * len(outs),
        out_shape=outs,
        scratch_shapes=scratch,
        compiler_params=pltpu.CompilerParams(vmem_limit_bytes=limit_mib << 20),
        cost_estimate=pl.CostEstimate(flops=flops, bytes_accessed=moved, transcendentals=0),
    )(scalars, *inputs)


def digits_of(count):
    digits, stride = [], 1
    while stride < count:
        size = 4 if (count // stride) % 4 == 0 else 2
        digits.append((stride, size))
        stride *= size
    return digits


def xor_exchange(value, axis, count, mask):
    return lax.ppermute(value, axis, [(i, i ^ mask) for i in range(count)])


def scatter_sum(addends, axis, count, digits):
    index = lax.axis_index(axis)
    rows, cols = addends[0].shape
    shape = [size for _, size in reversed(digits)] + [rows // count, cols]
    addends = [a.reshape(shape) for a in addends]
    left = list(reversed(range(len(digits))))
    for digit in range(len(digits)):
        stride, size = digits[digit]
        place = left.index(digit)
        mine = (index // stride) % size

        def part(which):
            return [lax.dynamic_index_in_dim(a, which, place, keepdims=False) for a in addends]

        def total(pieces):
            result = pieces[0].astype(F32)
            for piece in pieces[1:]:
                result = result + piece.astype(F32)
            return result

        received = [
            xor_exchange(total(part(mine ^ s)).astype(BF16), axis, count, s * stride)
            for s in range(1, size)
        ]
        addends = part(mine) + received
        left.remove(digit)
    return total(addends)


def all_sum(sel, value, axis, count, last):
    mask = 1
    while True:
        size = 4 if 4 * mask <= count else 2
        terms = [value]
        for s in range(1, size):
            terms.append(xor_exchange(value, axis, count, s * mask))
        mask *= size
        if mask >= last:
            return terms
        kernel = four_kernel if size == 4 else pair_kernel
        (value,) = call(kernel, sel, terms, [struct(value.shape, F32)], [], 10**5, 2)


def scatter_pairs(sel, pairs, axis, count, digits, outs, small=(), small_outs=()):
    (stride, size), (far_stride, far_size) = digits
    (a0, a1), (b0, b1) = pairs
    arrays = [a0, a1, b0, b1]
    cols = a0.shape[1] + b0.shape[1]
    deep = a0.shape[0] // size
    rows = deep // far_size

    def exchange(sends, step):
        received = []
        for s, send in enumerate(sends, 1):
            received.append(xor_exchange(send, axis, count, s * step))
        return received

    sends = call(
        functools.partial(add_kernel, deep),
        sel,
        arrays,
        [struct((deep, cols), BF16)] * (size - 1),
        [],
        10**6,
        4,
    )
    wide = exchange(sends, stride)
    own = [struct((rows, cols), F32)]
    if not small:
        *sends, own = call(
            functools.partial(fan_kernel, rows, far_size - 1),
            sel,
            arrays + wide,
            [struct((rows, cols), BF16)] * (far_size - 1) + own,
            [],
            10**6,
            4,
        )
        parts = [own] + exchange(sends, far_stride)
        kernel = functools.partial(total_kernel, len(parts))
        return call(kernel, sel, parts, outs, [], 10**6, 4)
    sent = struct((rows + small[0].shape[0] // 2, cols), BF16)
    *sends, own, own_small = call(
        functools.partial(fan_small_kernel, rows, far_size - 1, len(small)),
        sel,
        arrays + wide + list(small),
        [sent] * (far_size - 1) + own + [struct(small[0].shape, F32)],
        [],
        10**6,
        4,
    )
    parts = [own, own_small] + exchange(sends, far_stride)
    kernel = functools.partial(total_small_kernel, len(parts) - 1, len(outs))
    return call(kernel, sel, parts, list(outs) + list(small_outs), [], 10**6, 4)


def per_device(n_dp, n_tensor, *args):
    return block(n_dp, n_tensor, *args)


def block(
    n_dp,
    n_tensor,
    tokens,
    region_ids,
    norm1_gain,
    norm1_bias,
    w_qkv,
    qv_bias,
    rel_table,
    w_proj,
    b_proj,
    norm2_gain,
    norm2_bias,
    w_fc1,
    b_fc1,
    w_fc2,
    b_fc2,
    cotangent,
):
    all_images, _, width = tokens.shape
    images = all_images // n_tensor
    entries, heads = rel_table.shape
    chan = heads * HEAD_DIM
    hidden = w_fc1.shape[1]
    rows_t = images * TPAD
    rows_w = images * WINS * WPAD
    half_rows = -(-entries // 16) * 16
    digits = digits_of(n_dp)
    by_pairs = len(digits) == 2 and width // n_dp % 16 == 0
    order = list(range(len(digits)))
    layout = (width // n_dp, digits, order if by_pairs else order[::-1])
    me = lax.axis_index("tensor")
    spot = lax.axis_index("dp")
    places = [(spot // stride) % size for stride, size in digits[:2]]
    me_arr = sel = jnp.stack([me] + places).astype(jnp.int32)

    def swap(value):
        return lax.ppermute(value, "tensor", [(i, i ^ 1) for i in range(n_tensor)])

    wm = w_qkv.transpose(1, 0, 2)
    wo = swap(wm)
    table_m = rel_table.T
    table_o = swap(table_m)
    qvb_o = swap(qv_bias)
    po = swap(w_proj)
    b1_o = swap(b_fc1.reshape(1, hidden))
    w1o = swap(w_fc1)
    w2o = swap(w_fc2)

    row = lambda vec: vec.reshape(1, -1)

    bias_shape = struct((heads * WPAD, 2 * WPAD), F32)
    (bias,) = call(
        functools.partial(bias_kernel, heads, half_rows),
        sel,
        [table_m, table_o],
        [bias_shape],
        [
            pltpu.VMEM((2 * half_rows, 2 * WPAD), jnp.int32),
            pltpu.VMEM((heads, 2 * half_rows), F32),
        ],
        10**9,
        4,
    )

    ins = (
        tokens,
        region_ids,
        row(norm1_gain),
        row(norm1_bias),
        wm,
        wo,
        qv_bias,
        qvb_o,
        bias,
        w_proj,
        po,
        row(b_proj),
    )
    outs = (
        struct((rows_w, 2 * chan), BF16),
        struct((rows_w, 2 * chan), BF16),
        struct((rows_w, 2 * chan), BF16),
        struct((rows_w, width), BF16),
        struct((images * WINS, heads, 2 * WPAD), F32),
        struct((rows_t, 2 * chan), BF16),
        struct((rows_t, width), F32),
    )
    q, k, v, win_in, lse, merged, resid = call(
        functools.partial(attend_kernel, images, heads),
        me_arr,
        ins,
        outs,
        [
            pltpu.VMEM((rows_t, width), F32),
            pltpu.VMEM((WINS * WPAD, TPAD), BF16),
            pltpu.VMEM((rows_w, 2 * chan), BF16),
            pltpu.VMEM((heads * WPAD, 2 * chan), BF16),
        ],
        3 * 10**9,
        LIMIT,
    )

    weight_grad = struct((width, hidden), BF16)
    acc = struct((rows_t, width), F32)
    kept = (
        struct((rows_t, width), BF16),
        struct((width, rows_t), BF16),
        struct((rows_t, width), BF16),
        struct((width, rows_t), BF16),
        acc,
        acc,
    )
    common = (resid, cotangent, row(norm2_gain), row(norm2_bias))
    ins = common + (w1o, w2o, b1_o)
    outs = (weight_grad, weight_grad, struct((1, hidden), F32)) + kept
    g1o, g2o, gbo, *carried = call(
        functools.partial(ffn_kernel, images, layout, False),
        me_arr,
        ins,
        outs,
        [],
        3 * 10**9,
        LIMIT,
    )
    got1 = swap(g1o)
    got2 = swap(g2o)
    ins = common + (w_fc1, w_fc2, row(b_fc1), row(b_fc2), *carried)
    outs = (
        weight_grad,
        weight_grad,
        struct((1, hidden), F32),
        struct((images, TOK, width), BF16),
        acc,
        struct((8, width), F32),
    )
    g1m, g2m, gbm, out_half, gres, sums_two = call(
        functools.partial(ffn_kernel, images, layout, True),
        me_arr,
        ins,
        outs,
        [pltpu.VMEM((rows_t, width), F32), pltpu.VMEM((rows_t, width), F32)],
        3 * 10**9,
        LIMIT,
    )

    share = width // n_dp

    def join(half):
        shape = struct((TOK, all_images, width), half.dtype)
        (joined,) = call(join_kernel, sel, [half, swap(half)], [shape], [], 10**6, LIMIT)
        return joined.transpose(1, 0, 2)

    if by_pairs:
        outs = [struct((share, hidden), F32)] * 2
        sent_fc1, sent_fc2 = scatter_pairs(
            sel, ((g1m, got1), (g2m, got2)), "dp", n_dp, digits, outs
        )
    else:
        sent_fc1 = scatter_sum((g1m, got1), "dp", n_dp, digits)
        sent_fc2 = scatter_sum((g2m, got2), "dp", n_dp, digits)
    output = join(out_half)

    ins = (gres, region_ids, merged, w_proj, po, q, k, v, win_in, lse, bias)
    outs = (
        struct((width, 2 * chan), BF16),
        struct((width, 2 * chan), BF16),
        struct((width, 2 * chan), BF16),
        struct((width, 2 * chan), BF16),
        struct((rows_w, 6 * chan), BF16),
        struct((8, 2 * chan), F32),
        bias_shape,
    )
    gqkm, gqko, gvpm, gvpo, gqkv, sums_qv, gbias = call(
        functools.partial(attend_back_kernel, images, heads, layout),
        me_arr,
        ins,
        outs,
        [
            pltpu.VMEM((WINS * WPAD, TPAD), BF16),
            pltpu.VMEM((rows_w, 2 * chan), BF16),
            pltpu.VMEM((heads * WPAD, 2 * chan), BF16),
            pltpu.VMEM((WPAD, 2 * chan), F32),
            pltpu.VMEM((WPAD, 2 * chan), F32),
        ],
        5 * 10**9,
        LIMIT,
    )

    got_qk = swap(gqko)
    got_vp = swap(gvpo)
    ins = (tokens, gres, gqkv, wm, wo, row(norm1_gain), gbias, sums_two, sums_qv, gbm, gbo)
    pack = struct((-(-(7 + hidden // width + heads // 2) // 8) * 8, width), F32)
    outs = (struct((images, TOK, width), F32), pack, pack)
    grad_half, small, theirs = call(
        functools.partial(last_kernel, images, heads, half_rows),
        me_arr,
        ins,
        outs,
        [
            pltpu.VMEM((rows_t, width), F32),
            pltpu.VMEM((2 * half_rows, 2 * WPAD), jnp.int32),
            pltpu.VMEM((2 * heads, 2 * half_rows), F32),
        ],
        2 * 10**9,
        LIMIT,
    )
    grad_in = join(grad_half)

    got = swap(theirs)
    (small,) = call(pair_kernel, sel, [small, got], [struct(small.shape, F32)], [], 10**5, 2)
    small_outs = (struct((1, width), F32),) * 6 + (
        struct((2, chan), F32),
        struct((1, hidden), F32),
        struct((heads, entries), F32),
    )
    pairs = ((gqkm, got_qk), (gvpm, got_vp))
    if by_pairs and 4 * chan == 2 * width:
        terms = all_sum(sel, small, "dp", n_dp, digits[0][1])
        outs = [struct((3, share, chan), F32), struct((share, chan), F32)]
        sent_qkv, sent_proj, *small = scatter_pairs(
            sel, pairs, "dp", n_dp, digits, outs, terms, small_outs
        )
    else:
        terms = all_sum(sel, small, "dp", n_dp, n_dp)
        kernel = functools.partial(unpack_kernel, len(terms))
        small = call(kernel, sel, terms, small_outs, [], 10**5, 2)
        sent_qk = scatter_sum(pairs[0], "dp", n_dp, digits)
        sent_vp = scatter_sum(pairs[1], "dp", n_dp, digits)
        sent_qkv = jnp.stack([sent_qk[:, :chan], sent_qk[:, chan:], sent_vp[:, :chan]], axis=0)
        sent_proj = sent_vp[:, chan:]
    sent_qkv = sent_qkv.transpose(1, 0, 2)
    *vectors, sum_qv, sum_b1, sum_table = small
    vectors = [vec.reshape(width) for vec in vectors]
    return (
        output,
        grad_in,
        vectors[4],
        vectors[5],
        sent_qkv,
        sum_qv,
        sum_table.T,
        sent_proj,
        vectors[0],
        vectors[1],
        vectors[2],
        sent_fc1,
        sum_b1.reshape(hidden),
        sent_fc2,
        vectors[3],
    )


def solution(mesh):
    return jax.shard_map(
        functools.partial(per_device, mesh.shape["dp"], mesh.shape["tensor"]),
        mesh=mesh,
        in_specs=(
            P("dp", None, None),
            P("dp", None),
            P(),
            P(),
            P(None, None, "tensor"),
            P(None, "tensor"),
            P(None, "tensor"),
            P(None, "tensor"),
            P(),
            P(),
            P(),
            P(None, "tensor"),
            P("tensor"),
            P(None, "tensor"),
            P(),
            P("dp", None, None),
        ),
        out_specs=(
            P("dp", None, None),
            P("dp", None, None),
            P(),
            P(),
            P("dp", None, "tensor"),
            P(None, "tensor"),
            P(None, "tensor"),
            P("dp", "tensor"),
            P(),
            P(),
            P(),
            P("dp", "tensor"),
            P("tensor"),
            P("dp", "tensor"),
            P(),
        ),
        check_vma=False,
    )
```

```python
import functools

import jax
import jax.numpy as jnp
from jax import lax
from jax.experimental import pallas as pl
from jax.experimental.pallas import tpu as pltpu
from jax.sharding import PartitionSpec as P


HEAD_DIM = 32
SIDE = 14
WIN = 7
SHIFT = 3
NORM_EPS = 1e-05

TOK = SIDE * SIDE
TPAD = 208
WTOK = WIN * WIN
WPAD = 64
BLOCKS = SIDE // WIN
WINS = BLOCKS * BLOCKS
F32 = jnp.float32
BF16 = jnp.bfloat16
LIMIT = 16


def nn(a, b):
    return lax.dot_general(a, b, (((1,), (0,)), ((), ())), preferred_element_type=F32)


def nt(a, b):
    return lax.dot_general(a, b, (((1,), (1,)), ((), ())), preferred_element_type=F32)


def tn(a, b):
    return lax.dot_general(a, b, (((0,), (0,)), ((), ())), preferred_element_type=F32)


def iota(shape, axis):
    return lax.broadcasted_iota(jnp.int32, shape, axis)


def normalize(source):
    center = jnp.mean(source, axis=-1, keepdims=True)
    centred = source - center
    inverse = lax.rsqrt(jnp.mean(centred * centred, axis=-1, keepdims=True) + NORM_EPS)
    return centred * inverse, inverse


def norm_back(upstream, normed, inverse, gain_vec):
    scaled = upstream * gain_vec
    return inverse * (
        scaled
        - jnp.mean(scaled, axis=-1, keepdims=True)
        - normed * jnp.mean(scaled * normed, axis=-1, keepdims=True)
    )


def seventh(value):
    return (value * 37) >> 8


def window_source(slot):
    window, at = slot >> 6, slot & (WPAD - 1)
    row = (window >> 1) * WIN + seventh(at) + SHIFT
    col = (window & 1) * WIN + (at - seventh(at) * WIN) + SHIFT
    row = jnp.where(row >= SIDE, row - SIDE, row)
    col = jnp.where(col >= SIDE, col - SIDE, col)
    return jnp.where(at < WTOK, row * SIDE + col, -1)


def gather_matrix():
    shape = (WINS * WPAD, TPAD)
    hit = window_source(iota(shape, 0)) == iota(shape, 1)
    return jnp.where(hit, 1.0, 0.0).astype(BF16)


def scatter_matrix():
    shape = (TPAD, WINS * WPAD)
    hit = window_source(iota(shape, 1)) == iota(shape, 0)
    return jnp.where(hit, 1.0, 0.0).astype(BF16)


def head_mask(heads):
    shape = (heads * WPAD, 2 * heads * HEAD_DIM)
    hit = (iota(shape, 0) >> 6) == ((iota(shape, 1) & (heads * HEAD_DIM - 1)) >> 5)
    return jnp.where(hit, 1.0, 0.0).astype(BF16)


def log2(value):
    return value.bit_length() - 1


def row_order(slot, rows, digits, order):
    rest, block = slot >> log2(rows), 0
    for digit in reversed(order):
        stride, size = digits[digit]
        block = block + (rest & (size - 1)) * stride
        rest = rest >> log2(size)
    return block * rows + (slot & (rows - 1))


def put_rows(out_ref, layout, col, value):
    rows = layout[0]
    cols = slice(col, col + value.shape[1])
    value = value.astype(out_ref.dtype)
    sources = [row_order(at, *layout) for at in range(0, value.shape[0], rows)]
    if sources == sorted(sources):
        out_ref[:, cols] = value
        return
    for place, source in enumerate(sources):
        out_ref[place * rows : (place + 1) * rows, cols] = value[source : source + rows]


def order_matrix(width, layout):
    shape = (width, width)
    hit = row_order(iota(shape, 0), *layout) == iota(shape, 1)
    return jnp.where(hit, 1.0, 0.0).astype(BF16)


def fill_rows(rows_ref, block_ref, first, images):
    rows_ref[...] = jnp.zeros(rows_ref.shape, rows_ref.dtype)
    for image in range(images):
        rows_ref[image * TPAD : image * TPAD + TOK, :] = block_ref[first + image].astype(
            rows_ref.dtype
        )


def window_mask(ids_row, pick):
    ids_b = jnp.broadcast_to(ids_row.astype(F32), (2 * WPAD, TOK)).astype(BF16)
    pick = pick[:, :TOK]
    keys = nt(pick, ids_b)
    queries = nt(ids_b[:16], jnp.concatenate([pick, pick], axis=0))[0:1]
    shape = (WPAD, 2 * WPAD)
    key_at = iota(shape, 0)
    query_at = iota(shape, 1) & (WPAD - 1)
    same = jnp.logical_or(keys == queries, query_at >= WTOK)
    return jnp.where(jnp.logical_and(same, key_at < WTOK), 0.0, -jnp.inf)


def two_groups(rows):
    half = rows.shape[1] // 2
    zero = jnp.zeros((rows.shape[0], half), rows.dtype)
    return jnp.concatenate(
        [
            jnp.concatenate([rows[:, :half], zero], axis=1),
            jnp.concatenate([zero, rows[:, half:]], axis=1),
        ],
        axis=0,
    )


def own_groups(rows):
    half = rows.shape[1] // 2
    return jnp.concatenate([rows[:WPAD, :half], rows[WPAD:, half:]], axis=1)


def per_head(rows, mask, heads):
    return jnp.concatenate([rows] * heads, axis=0) * mask


def table_offsets(rows_half):
    shape = (2 * rows_half, 2 * WPAD)
    entry, query = iota(shape, 0), iota(shape, 1)
    group_e = jnp.where(entry >= rows_half, 1, 0)
    at = query & (WPAD - 1)
    place = seventh(at) * (2 * WIN - 1) + (at - seventh(at) * WIN)
    fits = jnp.logical_and(group_e == (query >> 6), at < WTOK)
    return jnp.where(fits, entry - group_e * rows_half - place, 4096)


def key_offset(key):
    row = key // WIN
    return 2 * WIN * (WIN - 1) - (row * (2 * WIN - 1) + key - row * WIN)


def bias_kernel(heads, rows_half, sel_ref, mine_ref, other_ref, bias_ref, off_ref, table_ref):
    off_ref[...] = table_offsets(rows_half)
    bias_ref[...] = jnp.zeros(bias_ref.shape, F32)
    entries = mine_ref.shape[1]
    table_ref[...] = jnp.zeros(table_ref.shape, F32)
    table_ref[:, :entries] = mine_ref[...]
    table_ref[:, rows_half : rows_half + entries] = other_ref[...]
    table = table_ref[...]
    part_a = table.astype(BF16).astype(F32)
    part_b = (table - part_a).astype(BF16).astype(F32)
    part_c = table - part_a - part_b
    parts = jnp.concatenate([part_a, part_b, part_c], axis=0).astype(BF16)
    for key in range(WTOK):
        pick = jnp.where(off_ref[...] == key_offset(key), 1.0, 0.0).astype(BF16)
        rows = nn(parts, pick)
        bias_ref[pl.ds(key, heads, stride=WPAD), :] = (
            rows[:heads] + rows[heads : 2 * heads] + rows[2 * heads :]
        )


def attend_kernel(
    images,
    heads,
    me_ref,
    tok_ref,
    ids_ref,
    gain_ref,
    shift_ref,
    wm_ref,
    wo_ref,
    qvbm_ref,
    qvbo_ref,
    bias_ref,
    pm_ref,
    po_ref,
    bproj_ref,
    q_ref,
    k_ref,
    v_ref,
    win_ref,
    lse_ref,
    merged_ref,
    resid_ref,
    x_ref,
    pick_ref,
    att_ref,
    mask_ref,
):
    chan = heads * HEAD_DIM
    factor = HEAD_DIM ** (-0.5)
    fill_rows(x_ref, tok_ref, me_ref[0] * images, images)
    normed, _ = normalize(x_ref[...])
    ln_one = (normed * gain_ref[...] + shift_ref[...]).astype(BF16)
    pick_ref[...] = gather_matrix()
    mask_ref[...] = head_mask(heads)
    slots = WINS * WPAD
    for image in range(images):
        win_ref[image * slots : (image + 1) * slots, :] = nn(
            pick_ref[...], ln_one[image * TPAD : (image + 1) * TPAD]
        ).astype(BF16)
    for group, (w_ref, b_ref) in enumerate(((wm_ref, qvbm_ref), (wo_ref, qvbo_ref))):
        cols = slice(group * chan, (group + 1) * chan)
        win = win_ref[...]
        q_ref[:, cols] = ((nn(win, w_ref[0]) + b_ref[0:1, :]) * factor).astype(BF16)
        k_ref[:, cols] = nn(win, w_ref[1]).astype(BF16)
        v_ref[:, cols] = (nn(win, w_ref[2]) + b_ref[1:2, :]).astype(BF16)

    def one_window(window, carry):
        rows = pl.ds(pl.multiple_of(window * WPAD, WPAD), WPAD)
        image = window // WINS
        local = pl.multiple_of((window - image * WINS) * WPAD, WPAD)
        ids_row = ids_ref[pl.ds(me_ref[0] * images + image, 1), :]
        allowed = window_mask(ids_row, pick_ref[pl.ds(local, WPAD), :])
        k_all = per_head(k_ref[rows, :], mask_ref[...], heads)
        v_all = per_head(v_ref[rows, :], mask_ref[...], heads)
        scores = nt(k_all, two_groups(q_ref[rows, :])) + bias_ref[...]
        scores = scores.reshape(heads, WPAD, 2 * WPAD) + allowed[None]
        top = jnp.max(scores, axis=1, keepdims=True)
        grown = jnp.exp(scores - top)
        total = jnp.sum(grown, axis=1, keepdims=True)
        lse_ref[window] = (top + jnp.log(total)).reshape(heads, 2 * WPAD)
        probs = (grown * (1.0 / total)).astype(BF16).reshape(heads * WPAD, 2 * WPAD)
        att_ref[rows, :] = own_groups(tn(probs, v_all)).astype(BF16)
        return carry

    lax.fori_loop(0, images * WINS, one_window, 0, unroll=True)
    back = scatter_matrix()
    for image in range(images):
        merged_ref[image * TPAD : (image + 1) * TPAD, :] = nn(
            back, att_ref[image * slots : (image + 1) * slots, :]
        ).astype(BF16)
    resid_ref[...] = (
        x_ref[...]
        + (nt(merged_ref[:, :chan], pm_ref[...]) + nt(merged_ref[:, chan:], po_ref[...]))
        + bproj_ref[...]
    )


def ffn_kernel(
    images,
    layout,
    last,
    me_ref,
    resid_ref,
    cot_ref,
    gain_ref,
    shift_ref,
    w1_ref,
    w2_ref,
    b1_ref,
    *refs,
):
    if last:
        ln_ref, lnt_ref, cot_b_ref, cot_t_ref, ffn_in, gln_in = refs[:6]
        g1_ref, g2_ref, gb_ref, ffn_ref, gln_ref = refs[6:]
    else:
        g1_ref, g2_ref, gb_ref = refs[:3]
        ln_ref, lnt_ref, cot_b_ref, cot_t_ref, ffn_ref, gln_ref = refs[3:]
    if last:
        ffn_ref[...] = ffn_in[...]
        gln_ref[...] = gln_in[...]
    else:
        normed, _ = normalize(resid_ref[...])
        ln_ref[...] = (normed * gain_ref[...] + shift_ref[...]).astype(BF16)
        fill_rows(cot_b_ref, cot_ref, me_ref[0] * images, images)
        width = ln_ref.shape[1]
        order = order_matrix(width, layout)
        lnt_ref[...] = nt(order, ln_ref[...]).astype(BF16)
        cot_t_ref[...] = nt(order, cot_b_ref[...]).astype(BF16)
        ffn_ref[...] = jnp.zeros(ffn_ref.shape, F32)
        gln_ref[...] = jnp.zeros(gln_ref.shape, F32)
    chunk = 512

    def one_chunk(at, carry):
        cols = pl.ds(pl.multiple_of(at * chunk, chunk), chunk)
        pre = nn(ln_ref[...], w1_ref[:, cols]) + b1_ref[:, cols]
        phi = 0.5 * (1.0 + lax.erf(pre * 0.7071067811865476))
        act = (pre * phi).astype(BF16)
        slope = phi + pre * jnp.exp(-0.5 * pre * pre) * 0.3989422804014327
        grad_pre = nn(cot_b_ref[...], w2_ref[:, cols]) * slope
        gb_ref[:, cols] = jnp.sum(grad_pre, axis=0, keepdims=True)
        grad_pre = grad_pre.astype(BF16)
        ffn_ref[...] += nt(act, w2_ref[:, cols])
        gln_ref[...] += nt(grad_pre, w1_ref[:, cols])
        g2_ref[:, cols] = nn(cot_t_ref[...], act).astype(BF16)
        g1_ref[:, cols] = nn(lnt_ref[...], grad_pre).astype(BF16)
        return carry

    lax.fori_loop(0, w1_ref.shape[1] // chunk, one_chunk, 0, unroll=True)


def second_norm_back(
    images, resid_ref, ffn_ref, gln_ref, cot_b_ref, gain_ref, b2_ref, half_ref, gres_ref, sums_ref
):
    resid = resid_ref[...]
    result = (resid + ffn_ref[...] + b2_ref[...]).astype(BF16)
    for image in range(images):
        half_ref[image] = result[image * TPAD : image * TPAD + TOK]
    normed, inverse = normalize(resid)
    upstream = gln_ref[...]
    cot = cot_b_ref[...].astype(F32)
    grad_resid = cot + norm_back(upstream, normed, inverse, gain_ref[...])
    gres_ref[...] = grad_resid
    sums_ref[0:1, :] = jnp.sum(grad_resid, axis=0, keepdims=True)
    sums_ref[1:2, :] = jnp.sum(upstream * normed, axis=0, keepdims=True)
    sums_ref[2:3, :] = jnp.sum(upstream, axis=0, keepdims=True)
    sums_ref[3:4, :] = jnp.sum(cot, axis=0, keepdims=True)
    sums_ref[4:8, :] = jnp.zeros((4, sums_ref.shape[1]), F32)


def attend_back_kernel(
    images,
    heads,
    layout,
    me_ref,
    resid_ref,
    ffn_ref,
    gln_ref,
    cot_b_ref,
    gain_two_ref,
    b2_ref,
    ids_ref,
    merged_ref,
    pm_ref,
    po_ref,
    q_ref,
    k_ref,
    v_ref,
    win_ref,
    lse_ref,
    bias_ref,
    gqkm_ref,
    gqko_ref,
    gvpm_ref,
    gvpo_ref,
    gqkv_ref,
    sums_ref,
    gbias_ref,
    half_ref,
    gres_ref,
    two_ref,
    pick_ref,
    gatt_ref,
    mask_ref,
    qsum_ref,
    vsum_ref,
):
    chan = heads * HEAD_DIM
    wide = 2 * chan
    factor = HEAD_DIM ** (-0.5)
    slots = WINS * WPAD
    pick_ref[...] = gather_matrix()
    mask_ref[...] = head_mask(heads)
    second_norm_back(
        images,
        resid_ref,
        ffn_ref,
        gln_ref,
        cot_b_ref,
        gain_two_ref,
        b2_ref,
        half_ref,
        gres_ref,
        two_ref,
    )
    gres_b = gres_ref[...].astype(BF16)
    put_rows(gvpm_ref, layout, chan, tn(gres_b, merged_ref[:, :chan]))
    put_rows(gvpo_ref, layout, chan, tn(gres_b, merged_ref[:, chan:]))
    grad_m = jnp.concatenate(
        [nn(gres_b, pm_ref[...]).astype(BF16), nn(gres_b, po_ref[...]).astype(BF16)], axis=1
    )
    for image in range(images):
        gatt_ref[image * slots : (image + 1) * slots, :] = nn(
            pick_ref[...], grad_m[image * TPAD : (image + 1) * TPAD]
        ).astype(BF16)
    gbias_ref[...] = jnp.zeros(gbias_ref.shape, F32)
    qsum_ref[...] = jnp.zeros(qsum_ref.shape, F32)
    vsum_ref[...] = jnp.zeros(vsum_ref.shape, F32)

    def one_window(window, carry):
        rows = pl.ds(pl.multiple_of(window * WPAD, WPAD), WPAD)
        image = window // WINS
        local = pl.multiple_of((window - image * WINS) * WPAD, WPAD)
        ids_row = ids_ref[pl.ds(me_ref[0] * images + image, 1), :]
        allowed = window_mask(ids_row, pick_ref[pl.ds(local, WPAD), :])
        mask = mask_ref[...]
        k_all = per_head(k_ref[rows, :], mask, heads)
        v_all = per_head(v_ref[rows, :], mask, heads)
        q_two = two_groups(q_ref[rows, :])
        g_two = two_groups(gatt_ref[rows, :])
        scores = nt(k_all, q_two) + bias_ref[...]
        scores = scores.reshape(heads, WPAD, 2 * WPAD) + allowed[None]
        probs = jnp.exp(scores - lse_ref[window].reshape(heads, 1, 2 * WPAD))
        g_probs = nt(v_all, g_two).reshape(heads, WPAD, 2 * WPAD)
        inner = jnp.sum(probs * g_probs, axis=1, keepdims=True)
        g_scores = (probs * (g_probs - inner)).reshape(heads * WPAD, 2 * WPAD)
        gbias_ref[...] += g_scores
        probs_b = probs.astype(BF16).reshape(heads * WPAD, 2 * WPAD)
        g_scores = g_scores.astype(BF16)

        def fold(product):
            return jnp.sum((product * mask.astype(F32)).reshape(heads, WPAD, wide), axis=0)

        g_v = fold(nn(probs_b, g_two))
        g_k = fold(nn(g_scores, q_two))
        g_q = own_groups(tn(g_scores, k_all)) * factor
        qsum_ref[...] += g_q
        vsum_ref[...] += g_v
        for group in range(2):
            cols = slice(group * chan, (group + 1) * chan)
            base = group * 3 * chan
            gqkv_ref[rows, base : base + chan] = g_q[:, cols].astype(BF16)
            gqkv_ref[rows, base + chan : base + 2 * chan] = g_k[:, cols].astype(BF16)
            gqkv_ref[rows, base + 2 * chan : base + 3 * chan] = g_v[:, cols].astype(BF16)
        return carry

    lax.fori_loop(0, images * WINS, one_window, 0, unroll=True)
    sums_ref[...] = jnp.zeros(sums_ref.shape, F32)
    sums_ref[0:1, :] = jnp.sum(qsum_ref[...], axis=0, keepdims=True)
    sums_ref[1:2, :] = jnp.sum(vsum_ref[...], axis=0, keepdims=True)
    win = win_ref[...]
    put_rows(gqko_ref, layout, 0, tn(win, gqkv_ref[:, 3 * chan : 5 * chan]))
    put_rows(gvpo_ref, layout, 0, tn(win, gqkv_ref[:, 5 * chan :]))
    put_rows(gqkm_ref, layout, 0, tn(win, gqkv_ref[:, : 2 * chan]))
    put_rows(gvpm_ref, layout, 0, tn(win, gqkv_ref[:, 2 * chan : 3 * chan]))


def last_kernel(
    images,
    heads,
    rows_half,
    me_ref,
    tok_ref,
    gres_ref,
    gqkv_ref,
    wm_ref,
    wo_ref,
    gain_ref,
    gbias_ref,
    two_ref,
    qv_ref,
    gbm_ref,
    gbo_ref,
    half_ref,
    mine_ref,
    theirs_ref,
    x_ref,
    off_ref,
    acc_ref,
):
    chan = heads * HEAD_DIM
    slots = WINS * WPAD
    grad_win = nt(gqkv_ref[:, :chan], wm_ref[0])
    for at in range(1, 6):
        w_ref = wm_ref if at < 3 else wo_ref
        grad_win += nt(gqkv_ref[:, at * chan : (at + 1) * chan], w_ref[at % 3])
    high = grad_win.astype(BF16)
    low = (grad_win - high.astype(F32)).astype(BF16)
    back = scatter_matrix()
    upstream = jnp.concatenate(
        [
            nn(back, high[image * slots : (image + 1) * slots])
            + nn(back, low[image * slots : (image + 1) * slots])
            for image in range(images)
        ],
        axis=0,
    )
    fill_rows(x_ref, tok_ref, me_ref[0] * images, images)
    normed, inverse = normalize(x_ref[...])
    grad_in = gres_ref[...] + norm_back(upstream, normed, inverse, gain_ref[...])
    for image in range(images):
        half_ref[image] = grad_in[image * TPAD : image * TPAD + TOK]
    width = upstream.shape[1]
    gain_sum = jnp.sum(upstream * normed, axis=0, keepdims=True)
    shift_sum = jnp.sum(upstream, axis=0, keepdims=True)
    off_ref[...] = table_offsets(rows_half)
    acc_ref[...] = jnp.zeros(acc_ref.shape, F32)
    for key in range(WTOK):
        pick = jnp.where(off_ref[...] == key_offset(key), 1.0, 0.0).astype(BF16)
        rows = gbias_ref[pl.ds(key, heads, stride=WPAD), :]
        top = rows.astype(BF16).astype(F32)
        parts = jnp.concatenate([top, rows - top], axis=0).astype(BF16)
        acc_ref[...] += nt(parts, pick)
    table = acc_ref[:heads] + acc_ref[heads:]
    for group, (pack_ref, gb_ref) in enumerate(((mine_ref, gbm_ref), (theirs_ref, gbo_ref))):
        pack_ref[...] = jnp.zeros(pack_ref.shape, F32)
        pack_ref[0:4, :] = two_ref[0:4, :]
        pack_ref[4:5, :] = gain_sum
        pack_ref[5:6, :] = shift_sum
        pack_ref[6:7, :chan] = qv_ref[0:1, group * chan : (group + 1) * chan]
        pack_ref[6:7, chan:] = qv_ref[1:2, group * chan : (group + 1) * chan]
        for at in range(gb_ref.shape[1] // width):
            pack_ref[7 + at : 8 + at, :] = gb_ref[:, at * width : (at + 1) * width]
        half = table[:, group * rows_half : (group + 1) * rows_half]
        low = pack_ref.shape[0] - heads // 2
        pack_ref[low:, :rows_half] = half[: heads // 2]
        pack_ref[low:, chan : chan + rows_half] = half[heads // 2 :]


def spread_small(total, outs):
    for at in range(6):
        outs[at][...] = total[at : at + 1]
    qv_ref, b1_ref, table_ref = outs[6:]
    chan, (heads, entries) = qv_ref.shape[1], table_ref.shape
    qv_ref[0:1, :] = total[6:7, :chan]
    qv_ref[1:2, :] = total[6:7, chan:]
    width = total.shape[1]
    for at in range(b1_ref.shape[1] // width):
        b1_ref[:, at * width : (at + 1) * width] = total[7 + at : 8 + at]
    low = total.shape[0] - heads // 2
    table_ref[: heads // 2, :] = total[low:, :entries]
    table_ref[heads // 2 :, :] = total[low:, chan : chan + entries]


def in_pairs(terms):
    if len(terms) == 2:
        return terms[0] + terms[1]
    return (terms[0] + terms[1]) + (terms[2] + terms[3])


def unpack_kernel(parts, sel_ref, *refs):
    spread_small(in_pairs([ref[...] for ref in refs[:parts]]), refs[parts:])


def rows_at(ref, start, rows):
    return ref[pl.ds(pl.multiple_of(start, rows), rows), :].astype(F32)


def add_kernel(rows, sel_ref, a0_ref, a1_ref, b0_ref, b1_ref, *out_refs):
    half = a0_ref.shape[1]
    for s, out_ref in enumerate(out_refs, 1):
        at = (sel_ref[1] ^ s) * rows
        out_ref[:, :half] = (rows_at(a0_ref, at, rows) + rows_at(a1_ref, at, rows)).astype(BF16)
        out_ref[:, half:] = (rows_at(b0_ref, at, rows) + rows_at(b1_ref, at, rows)).astype(BF16)


def fan_kernel(rows, sends, sel_ref, *refs):
    pairs, wide, outs = refs[:4], refs[4 : -1 - sends], refs[-1 - sends :]
    half = pairs[0].shape[1]
    for s in range(sends + 1):
        near = (sel_ref[2] ^ s) * rows
        far = sel_ref[1] * (rows * (sends + 1)) + near
        got = rows_at(wide[0], near, rows)
        for ref in wide[1:]:
            got = got + rows_at(ref, near, rows)
        out_ref = outs[s - 1] if s else outs[sends]
        for cols, first, second in (
            (slice(0, half), pairs[0], pairs[1]),
            (slice(half, got.shape[1]), pairs[2], pairs[3]),
        ):
            total = rows_at(first, far, rows) + rows_at(second, far, rows) + got[:, cols]
            out_ref[:rows, cols] = total.astype(out_ref.dtype)


def total_kernel(parts, sel_ref, own_ref, *refs):
    total, at = own_ref[...], 0
    for in_ref in refs[: parts - 1]:
        total = total + in_ref[...].astype(F32)
    for out_ref in refs[parts - 1 :]:
        width = out_ref.shape[-1]
        if len(out_ref.shape) == 2:
            out_ref[...] = total[:, at : at + width]
            at += width
            continue
        for plane in range(out_ref.shape[0]):
            out_ref[plane] = total[:, at : at + width]
            at += width


def fan_small_kernel(rows, sends, terms, sel_ref, *refs):
    ins, small, outs = refs[: -terms - sends - 2], refs[-terms - sends - 2 : -sends - 2], refs[-sends - 2 :]
    fan_kernel(rows, sends, sel_ref, *ins, *outs[:-1])
    total = in_pairs([ref[...] for ref in small]).astype(BF16)
    half, width = total.shape[0] // 2, total.shape[1]
    for out_ref in outs[:sends]:
        out_ref[rows:, :width] = total[:half]
        out_ref[rows:, width:] = total[half:]
    outs[-1][...] = total.astype(F32)


def total_small_kernel(parts, main, sel_ref, own_ref, small_ref, *refs):
    rows, width = own_ref.shape[0], small_ref.shape[1]
    received = refs[: parts - 1]
    total_kernel(parts, sel_ref, own_ref, *[ref.at[:rows, :] for ref in received], *refs[parts - 1 :][:main])
    terms = [small_ref[...]]
    for ref in received:
        low = ref[rows:, :].astype(F32)
        terms.append(jnp.concatenate([low[:, :width], low[:, width:]], axis=0))
    spread_small(in_pairs(terms), refs[parts - 1 :][main:])


def join_kernel(sel_ref, own_ref, other_ref, out_ref):
    images = own_ref.shape[0]
    for image in range(out_ref.shape[1]):
        mine = sel_ref[0] == image // images
        piece = jnp.where(
            mine, own_ref[image % images].astype(F32), other_ref[image % images].astype(F32)
        )
        out_ref[:, image, :] = piece.astype(out_ref.dtype)


def pair_kernel(sel_ref, a_ref, b_ref, out_ref):
    out_ref[...] = a_ref[...] + b_ref[...]


def four_kernel(sel_ref, a_ref, b_ref, c_ref, d_ref, out_ref):
    out_ref[...] = (a_ref[...] + b_ref[...]) + (c_ref[...] + d_ref[...])


def struct(shape, kind):
    return jax.ShapeDtypeStruct(shape, kind)


def call(kernel, scalars, inputs, outs, scratch, flops, limit_mib):
    moved = sum(a.size * a.dtype.itemsize for a in inputs)
    moved += sum(a.size * a.dtype.itemsize for a in outs)
    vmem = pl.BlockSpec(memory_space=pltpu.VMEM)
    return pl.pallas_call(
        kernel,
        in_specs=[pl.BlockSpec(memory_space=pltpu.SMEM)] + [vmem] * len(inputs),
        out_specs=[vmem] * len(outs),
        out_shape=outs,
        scratch_shapes=scratch,
        compiler_params=pltpu.CompilerParams(vmem_limit_bytes=limit_mib << 20),
        cost_estimate=pl.CostEstimate(flops=flops, bytes_accessed=moved, transcendentals=0),
    )(scalars, *inputs)


def digits_of(count):
    digits, stride = [], 1
    while stride < count:
        size = 4 if (count // stride) % 4 == 0 else 2
        digits.append((stride, size))
        stride *= size
    return digits


def xor_exchange(value, axis, count, mask):
    return lax.ppermute(value, axis, [(i, i ^ mask) for i in range(count)])


def scatter_sum(addends, axis, count, digits):
    index = lax.axis_index(axis)
    rows, cols = addends[0].shape
    shape = [size for _, size in reversed(digits)] + [rows // count, cols]
    addends = [a.reshape(shape) for a in addends]
    left = list(reversed(range(len(digits))))
    for digit in range(len(digits)):
        stride, size = digits[digit]
        place = left.index(digit)
        mine = (index // stride) % size

        def part(which):
            return [lax.dynamic_index_in_dim(a, which, place, keepdims=False) for a in addends]

        def total(pieces):
            result = pieces[0].astype(F32)
            for piece in pieces[1:]:
                result = result + piece.astype(F32)
            return result

        received = [
            xor_exchange(total(part(mine ^ s)).astype(BF16), axis, count, s * stride)
            for s in range(1, size)
        ]
        addends = part(mine) + received
        left.remove(digit)
    return total(addends)


def all_sum(sel, value, axis, count, last):
    mask = 1
    while True:
        size = 4 if 4 * mask <= count else 2
        terms = [value]
        for s in range(1, size):
            terms.append(xor_exchange(value, axis, count, s * mask))
        mask *= size
        if mask >= last:
            return terms
        kernel = four_kernel if size == 4 else pair_kernel
        (value,) = call(kernel, sel, terms, [struct(value.shape, F32)], [], 10**5, 2)


def scatter_pairs(sel, pairs, axis, count, digits, outs, small=(), small_outs=()):
    (stride, size), (far_stride, far_size) = digits
    (a0, a1), (b0, b1) = pairs
    arrays = [a0, a1, b0, b1]
    cols = a0.shape[1] + b0.shape[1]
    deep = a0.shape[0] // size
    rows = deep // far_size

    def exchange(sends, step):
        received = []
        for s, send in enumerate(sends, 1):
            received.append(xor_exchange(send, axis, count, s * step))
        return received

    sends = call(
        functools.partial(add_kernel, deep),
        sel,
        arrays,
        [struct((deep, cols), BF16)] * (size - 1),
        [],
        10**6,
        4,
    )
    wide = exchange(sends, stride)
    own = [struct((rows, cols), F32)]
    if not small:
        *sends, own = call(
            functools.partial(fan_kernel, rows, far_size - 1),
            sel,
            arrays + wide,
            [struct((rows, cols), BF16)] * (far_size - 1) + own,
            [],
            10**6,
            4,
        )
        parts = [own] + exchange(sends, far_stride)
        kernel = functools.partial(total_kernel, len(parts))
        return call(kernel, sel, parts, outs, [], 10**6, 4)
    sent = struct((rows + small[0].shape[0] // 2, cols), BF16)
    *sends, own, own_small = call(
        functools.partial(fan_small_kernel, rows, far_size - 1, len(small)),
        sel,
        arrays + wide + list(small),
        [sent] * (far_size - 1) + own + [struct(small[0].shape, F32)],
        [],
        10**6,
        4,
    )
    parts = [own, own_small] + exchange(sends, far_stride)
    kernel = functools.partial(total_small_kernel, len(parts) - 1, len(outs))
    return call(kernel, sel, parts, list(outs) + list(small_outs), [], 10**6, 4)


def per_device(n_dp, n_tensor, *args):
    return block(n_dp, n_tensor, *args)


def block(
    n_dp,
    n_tensor,
    tokens,
    region_ids,
    norm1_gain,
    norm1_bias,
    w_qkv,
    qv_bias,
    rel_table,
    w_proj,
    b_proj,
    norm2_gain,
    norm2_bias,
    w_fc1,
    b_fc1,
    w_fc2,
    b_fc2,
    cotangent,
):
    all_images, _, width = tokens.shape
    images = all_images // n_tensor
    entries, heads = rel_table.shape
    chan = heads * HEAD_DIM
    hidden = w_fc1.shape[1]
    rows_t = images * TPAD
    rows_w = images * WINS * WPAD
    half_rows = -(-entries // 16) * 16
    digits = digits_of(n_dp)
    by_pairs = len(digits) == 2 and width // n_dp % 16 == 0
    order = list(range(len(digits)))
    layout = (width // n_dp, digits, order if by_pairs else order[::-1])
    me = lax.axis_index("tensor")
    spot = lax.axis_index("dp")
    places = [(spot // stride) % size for stride, size in digits[:2]]
    me_arr = sel = jnp.stack([me] + places).astype(jnp.int32)

    def swap(value):
        return lax.ppermute(value, "tensor", [(i, i ^ 1) for i in range(n_tensor)])

    wm = w_qkv.transpose(1, 0, 2)
    wo = swap(wm)
    table_m = rel_table.T
    table_o = swap(table_m)
    qvb_o = swap(qv_bias)
    po = swap(w_proj)
    b1_o = swap(b_fc1.reshape(1, hidden))
    w1o = swap(w_fc1)
    w2o = swap(w_fc2)

    row = lambda vec: vec.reshape(1, -1)

    bias_shape = struct((heads * WPAD, 2 * WPAD), F32)
    (bias,) = call(
        functools.partial(bias_kernel, heads, half_rows),
        sel,
        [table_m, table_o],
        [bias_shape],
        [
            pltpu.VMEM((2 * half_rows, 2 * WPAD), jnp.int32),
            pltpu.VMEM((heads, 2 * half_rows), F32),
        ],
        10**9,
        4,
    )

    ins = (
        tokens,
        region_ids,
        row(norm1_gain),
        row(norm1_bias),
        wm,
        wo,
        qv_bias,
        qvb_o,
        bias,
        w_proj,
        po,
        row(b_proj),
    )
    outs = (
        struct((rows_w, 2 * chan), BF16),
        struct((rows_w, 2 * chan), BF16),
        struct((rows_w, 2 * chan), BF16),
        struct((rows_w, width), BF16),
        struct((images * WINS, heads, 2 * WPAD), F32),
        struct((rows_t, 2 * chan), BF16),
        struct((rows_t, width), F32),
    )
    q, k, v, win_in, lse, merged, resid = call(
        functools.partial(attend_kernel, images, heads),
        me_arr,
        ins,
        outs,
        [
            pltpu.VMEM((rows_t, width), F32),
            pltpu.VMEM((WINS * WPAD, TPAD), BF16),
            pltpu.VMEM((rows_w, 2 * chan), BF16),
            pltpu.VMEM((heads * WPAD, 2 * chan), BF16),
        ],
        3 * 10**9,
        LIMIT,
    )

    weight_grad = struct((width, hidden), BF16)
    acc = struct((rows_t, width), F32)
    kept = (
        struct((rows_t, width), BF16),
        struct((width, rows_t), BF16),
        struct((rows_t, width), BF16),
        struct((width, rows_t), BF16),
        acc,
        acc,
    )
    common = (resid, cotangent, row(norm2_gain), row(norm2_bias))
    ins = common + (w1o, w2o, b1_o)
    outs = (weight_grad, weight_grad, struct((1, hidden), F32)) + kept
    g1o, g2o, gbo, *carried = call(
        functools.partial(ffn_kernel, images, layout, False),
        me_arr,
        ins,
        outs,
        [],
        3 * 10**9,
        LIMIT,
    )
    got1 = swap(g1o)
    got2 = swap(g2o)
    ins = common + (w_fc1, w_fc2, row(b_fc1), *carried)
    outs = (
        weight_grad,
        weight_grad,
        struct((1, hidden), F32),
        acc,
        acc,
    )
    g1m, g2m, gbm, ffn_acc, gln_acc = call(
        functools.partial(ffn_kernel, images, layout, True), me_arr, ins, outs, [], 3 * 10**9, LIMIT
    )

    share = width // n_dp

    def join(half):
        shape = struct((TOK, all_images, width), half.dtype)
        (joined,) = call(join_kernel, sel, [half, swap(half)], [shape], [], 10**6, LIMIT)
        return joined.transpose(1, 0, 2)

    if by_pairs:
        outs = [struct((share, hidden), F32)] * 2
        sent_fc1, sent_fc2 = scatter_pairs(
            sel, ((g1m, got1), (g2m, got2)), "dp", n_dp, digits, outs
        )
    else:
        sent_fc1 = scatter_sum((g1m, got1), "dp", n_dp, digits)
        sent_fc2 = scatter_sum((g2m, got2), "dp", n_dp, digits)
    before = (resid, ffn_acc, gln_acc, carried[2], row(norm2_gain), row(b_fc2))
    ins = before + (region_ids, merged, w_proj, po, q, k, v, win_in, lse, bias)
    outs = (
        struct((width, 2 * chan), BF16),
        struct((width, 2 * chan), BF16),
        struct((width, 2 * chan), BF16),
        struct((width, 2 * chan), BF16),
        struct((rows_w, 6 * chan), BF16),
        struct((8, 2 * chan), F32),
        bias_shape,
        struct((images, TOK, width), BF16),
        acc,
        struct((8, width), F32),
    )
    gqkm, gqko, gvpm, gvpo, gqkv, sums_qv, gbias, out_half, gres, sums_two = call(
        functools.partial(attend_back_kernel, images, heads, layout),
        me_arr,
        ins,
        outs,
        [
            pltpu.VMEM((WINS * WPAD, TPAD), BF16),
            pltpu.VMEM((rows_w, 2 * chan), BF16),
            pltpu.VMEM((heads * WPAD, 2 * chan), BF16),
            pltpu.VMEM((WPAD, 2 * chan), F32),
            pltpu.VMEM((WPAD, 2 * chan), F32),
        ],
        5 * 10**9,
        LIMIT,
    )

    got_qk = swap(gqko)
    got_vp = swap(gvpo)
    ins = (tokens, gres, gqkv, wm, wo, row(norm1_gain), gbias, sums_two, sums_qv, gbm, gbo)
    pack = struct((-(-(7 + hidden // width + heads // 2) // 8) * 8, width), F32)
    outs = (struct((images, TOK, width), F32), pack, pack)
    grad_half, small, theirs = call(
        functools.partial(last_kernel, images, heads, half_rows),
        me_arr,
        ins,
        outs,
        [
            pltpu.VMEM((rows_t, width), F32),
            pltpu.VMEM((2 * half_rows, 2 * WPAD), jnp.int32),
            pltpu.VMEM((2 * heads, 2 * half_rows), F32),
        ],
        2 * 10**9,
        LIMIT,
    )
    output = join(out_half)
    grad_in = join(grad_half)

    got = swap(theirs)
    (small,) = call(pair_kernel, sel, [small, got], [struct(small.shape, F32)], [], 10**5, 2)
    small_outs = (struct((1, width), F32),) * 6 + (
        struct((2, chan), F32),
        struct((1, hidden), F32),
        struct((heads, entries), F32),
    )
    pairs = ((gqkm, got_qk), (gvpm, got_vp))
    if by_pairs and 4 * chan == 2 * width:
        terms = all_sum(sel, small, "dp", n_dp, digits[0][1])
        outs = [struct((3, share, chan), F32), struct((share, chan), F32)]
        sent_qkv, sent_proj, *small = scatter_pairs(
            sel, pairs, "dp", n_dp, digits, outs, terms, small_outs
        )
    else:
        terms = all_sum(sel, small, "dp", n_dp, n_dp)
        kernel = functools.partial(unpack_kernel, len(terms))
        small = call(kernel, sel, terms, small_outs, [], 10**5, 2)
        sent_qk = scatter_sum(pairs[0], "dp", n_dp, digits)
        sent_vp = scatter_sum(pairs[1], "dp", n_dp, digits)
        sent_qkv = jnp.stack([sent_qk[:, :chan], sent_qk[:, chan:], sent_vp[:, :chan]], axis=0)
        sent_proj = sent_vp[:, chan:]
    sent_qkv = sent_qkv.transpose(1, 0, 2)
    *vectors, sum_qv, sum_b1, sum_table = small
    vectors = [vec.reshape(width) for vec in vectors]
    return (
        output,
        grad_in,
        vectors[4],
        vectors[5],
        sent_qkv,
        sum_qv,
        sum_table.T,
        sent_proj,
        vectors[0],
        vectors[1],
        vectors[2],
        sent_fc1,
        sum_b1.reshape(hidden),
        sent_fc2,
        vectors[3],
    )


def solution(mesh):
    return jax.shard_map(
        functools.partial(per_device, mesh.shape["dp"], mesh.shape["tensor"]),
        mesh=mesh,
        in_specs=(
            P("dp", None, None),
            P("dp", None),
            P(),
            P(),
            P(None, None, "tensor"),
            P(None, "tensor"),
            P(None, "tensor"),
            P(None, "tensor"),
            P(),
            P(),
            P(),
            P(None, "tensor"),
            P("tensor"),
            P(None, "tensor"),
            P(),
            P("dp", None, None),
        ),
        out_specs=(
            P("dp", None, None),
            P("dp", None, None),
            P(),
            P(),
            P("dp", None, "tensor"),
            P(None, "tensor"),
            P(None, "tensor"),
            P("dp", "tensor"),
            P(),
            P(),
            P(),
            P("dp", "tensor"),
            P("tensor"),
            P("dp", "tensor"),
            P(),
        ),
        check_vma=False,
    )
```
